32 devices in a mesh: ctx: 8 (over y, x, core), wt: 4 (over z).
Axes of the slice: x: 2, y: 2, z: 4, core: 2. Of those that a mesh axis runs over, the one named last changes fastest.
Arguments:
- tokens: bfloat16 [4, 1024, 2048], P('wt', 'ctx'), may hold values from -6 to 6
- cotangent: bfloat16 [4, 1024, 2048], P('wt', 'ctx'), may hold values from -6 to 6
- segments: int32 [4, 1024], P('wt'), may hold values from 0 to 7, never falling along the last dimension, each value on 1 to 512 neighbouring positions
- routes: int32 [4, 1024, 8], P('wt', 'ctx'), may hold values from 0 to 31, all different within a row; in each aligned block of 64 rows (0 to 63, 64 to 127, ..., all dimensions but the last counted through in order) at most 20 rows name the same one
- pair_order: int32 [8], replicated, may hold values from 0 to 7, each once
- attn_gain: float32 [2048], replicated, may hold values from 0.25 to 1.75
- ffn_gain: float32 [2048], replicated, may hold values from 0.25 to 1.75
- query_gain: float32 [128], replicated, may hold values from 0.25 to 1.75
- key_gain: float32 [128], replicated, may hold values from 0.25 to 1.75
- w_query: bfloat16 [2048, 4096], P('wt'), may hold values from -0.125 to 0.125
- key_weight: bfloat16 [2048, 512], P('wt'), may hold values from -0.125 to 0.125
- value_weight: bfloat16 [2048, 512], P('wt'), may hold values from -0.125 to 0.125
- w_output: bfloat16 [4096, 2048], P('wt'), may hold values from -0.75 to 0.75
- w_router: bfloat16 [2048, 32], P('wt'), may hold values from -0.0625 to 0.0625
- w_gate: bfloat16 [32, 2048, 768], P(('ctx', 'wt')), may hold values from -0.125 to 0.125
- w_up: bfloat16 [32, 2048, 768], P(('ctx', 'wt')), may hold values from -0.125 to 0.125
- w_down: bfloat16 [32, 768, 2048], P(('ctx', 'wt')), may hold values from -1 to 1
Outputs:
- mixed: bfloat16 [4, 1024, 2048], P('wt', 'ctx')
- loss: float32 [], replicated
- balance: float32 [32], replicated
- tokens_grad: float32 [4, 1024, 2048], P('wt', 'ctx')
- attn_gain_grad: float32 [2048], P('wt')
- ffn_gain_grad: float32 [2048], P('wt')
- query_gain_grad: float32 [128], P('wt')
- key_gain_grad: float32 [128], P('wt')
- w_query_grad: float32 [2048, 4096], P('wt')
- w_key_grad: float32 [2048, 512], P('wt')
- w_value_grad: float32 [2048, 512], P('wt')
- w_output_grad: float32 [4096, 2048], P('wt')
- w_router_grad: float32 [2048, 32], P('wt')
- w_gate_grad: float32 [32, 2048, 768], P(('ctx', 'wt'))
- w_up_grad: float32 [32, 2048, 768], P(('ctx', 'wt'))
- w_down_grad: float32 [32, 768, 2048], P(('ctx', 'wt'))
The draws below stay inside these ranges and needn't reach their ends.
Inputs may be any that keep to these rules, and one draw needn't show every extreme that they name: `segments`: positions of a sequence run through documents in order; every document has 1 to 512 positions, and one has exactly that many. `routes`: A token's 8 experts differ. In each aligned block of 64 rows (one device holds two) no expert is named by more than 20 rows, a bound that some block reaches. A permutation; index j of ctx holds blocks pair_order[j] and 15 - pair_order[j] of every sequence of its wt index.
All inputs are finite; a program needn't handle non-finite values.
Results may differ from the reference program's by a relative error of at most 0.024.
Values may be sent and summed in bfloat16 or wider, within the bound.
No kernel may reach another device: no remote copies, remote signals or barrier semaphores. Data moves between devices by JAX's collectives and lax.ppermute only.
A program may use at most 320 MiB of HBM per device.

```python
import math
import jax
import jax.numpy as jnp
import numpy as np
from jax import lax

MODEL_DIMENSION = 2048
QUERY_HEADS = 32
KEY_VALUE_HEADS = 4
HEAD_SIZE = 128
FF = 768
TOP = 8
DOCS = 8
PAIRS = 8
HALF = 64
SEQUENCE_LENGTH = 1024
SEQS = 4
TOKENS = 4096
EXPERTS = 32
HALF_CAP = 20


def levels(stream_key, extent, split, smallest, high):
    loudness, own = 1.0, jax.random.fold_in(stream_key, 6)
    for position, blocks in split:
        steps = jnp.exp(jax.random.uniform(jax.random.fold_in(own, position), (blocks,), jnp.float32, smallest / len(split), high / len(split)))
        loudness = loudness * jnp.repeat(steps, extent[position] // blocks).reshape([-1 if axis == position else 1 for axis in range(len(extent))])
    return loudness


def profile(amount, total, most, lean):
    loads = [(1 << 20) // math.isqrt(grade ** lean) + 1 for grade in range(2, amount + 1)]
    rest, given = total - most - (amount - 1), [1] * (amount - 1)
    while rest > 0:
        movable = [i for i in range(amount - 1) if given[i] < most]
        pool, left = sum([loads[i] for i in movable]), rest
        for i in movable:
            more = min(most - given[i], max(1, left * loads[i] // pool), rest)
            given[i] = given[i] + more
            rest = rest - more
    return np.array([most] + given)


def uneven_parts(key, number_of, total, most, lean):
    if number_of == 2:
        one = jax.random.randint(key, (), max(1, total - most), min(most, total - 1) + 1)
        return jnp.stack([one, total - one])
    tallies = jnp.asarray(profile(number_of, total, most, lean), jnp.int32)
    pairs = (number_of - 1) // 2
    giver, receiver = tallies[1:1 + 2 * pairs:2], tallies[2:2 + 2 * pairs:2]
    slack = jnp.minimum(giver - 1, most - receiver)
    shifted = jax.random.randint(jax.random.fold_in(key, 1), (pairs,), 0, 1 << 20) % (slack + 1)
    tallies = tallies.at[1:1 + 2 * pairs:2].set(giver - shifted).at[2:2 + 2 * pairs:2].set(receiver + shifted)
    return tallies[jax.random.permutation(jax.random.fold_in(key, 2), number_of)]


def shared_out(key, own, number, rows, number_of, top, limit, skew):
    ranking = jax.random.permutation(key, number_of)
    crowded, ordinary = portions_of(number_of, rows * top, limit, skew, True), portions_of(number_of, rows * top, limit, skew, False)
    places = jnp.arange(number_of)

    def named(sizes, turn):
        used = int((sizes > 0).sum())
        fixed = max(1, used // 4)
        moved = fixed + (places - fixed + turn * (used - fixed)) % max(1, number_of - fixed)
        return jnp.zeros((number_of,), jnp.int32).at[ranking[jnp.where(places < fixed, places, moved)]].set(jnp.asarray(sizes, jnp.int32))

    sizes = jnp.where(number % 4 == 0, named(crowded, number // 4), named(ordinary, number - number // 4 - 1))
    mixed = jax.random.permutation(jax.random.fold_in(own, 3), number_of)
    giver, sink = mixed[0:number_of // 2 * 2:2], mixed[1:number_of // 2 * 2:2]
    room = jnp.minimum(sizes[giver] - 1, limit - sizes[sink]) // 2
    room = jnp.where((giver == ranking[0]) | (sink == ranking[0]) | (sizes[sink] == 0), 0, jnp.maximum(room, 0))
    moved = jax.random.randint(jax.random.fold_in(own, 4), (number_of // 2,), 0, 1 << 20) % (room + 1)
    sizes = sizes.at[giver].add(-moved).at[sink].add(moved)
    members = jnp.searchsorted(jnp.cumsum(sizes), jnp.arange(rows * top), side="right").astype(jnp.int32)
    listing = members.reshape(top, rows).T
    listing = listing[jax.random.permutation(jax.random.fold_in(own, 1), rows)]
    turn = jax.random.randint(jax.random.fold_in(own, 2), (rows, 1), 0, top)
    return jnp.take_along_axis(listing, (jnp.arange(top)[None, :] + turn) % top, axis=1)


def portions_of(number_of, total, limit, slope, full):
    loads = [(1 << 20) // math.isqrt(standing ** slope) + 1 for standing in range(1, number_of + 1)]
    largest = limit if full else min(limit, max(-(-total // number_of), total * loads[0] // sum(loads)))
    least = 1 if total - largest >= number_of - 1 else 0
    given, rest = [largest] + [least] * (number_of - 1), total - largest - least * (number_of - 1)
    while rest > 0:
        candidates = [i for i in range(1, number_of) if given[i] < largest] or [i for i in range(1, number_of) if given[i] < limit]
        mass, remaining = sum([loads[i] for i in candidates]), rest
        for i in candidates:
            extra = min(limit - given[i], max(1, remaining * loads[i] // mass), rest)
            given[i] = given[i] + extra
            rest = rest - extra
    return np.array(given)


def bell_draw(key, extent, spread, reach, cuts=(), kind=jnp.bfloat16):
    values = jax.random.normal(key, extent, jnp.float32) * spread
    if len(cuts) > 0:
        values = levels(key, extent, cuts, -0.22, 0.18) * values
    return jnp.clip(values, min=-reach, max=reach).astype(kind)


def setup_inputs(seed: int = 0) -> dict:
    streams_of = jax.random.split(jax.random.key(seed), 18)
    tokens = bell_draw(streams_of[0], (SEQS, SEQUENCE_LENGTH, MODEL_DIMENSION), 1.0, 6.0, ((0, 4), (1, 8)))
    cotangent = bell_draw(streams_of[1], (SEQS, SEQUENCE_LENGTH, MODEL_DIMENSION), 1.0, 6.0, ((0, 4), (1, 8)))
    segments = jax.vmap(lambda own: jnp.searchsorted(jnp.cumsum(uneven_parts(own, DOCS, SEQUENCE_LENGTH, SEQUENCE_LENGTH // 2, 2)), jnp.arange(SEQUENCE_LENGTH), side="right"))(jax.random.split(streams_of[2], SEQS)).reshape((SEQS, SEQUENCE_LENGTH)).astype(jnp.int32)
    routes_keys = jax.random.split(jax.random.fold_in(streams_of[3], 1), SEQS * SEQUENCE_LENGTH // HALF)
    routes_turns = jax.random.permutation(jax.random.fold_in(streams_of[3], 3), SEQS * SEQUENCE_LENGTH // HALF)
    routes = jax.vmap(lambda own, number: shared_out(jax.random.fold_in(streams_of[3], 2), own, number, HALF, EXPERTS, TOP, HALF_CAP, 1))(routes_keys, routes_turns).reshape((SEQS, SEQUENCE_LENGTH, TOP))
    pair_order = jax.random.permutation(streams_of[4], PAIRS).astype(jnp.int32)
    attn_gain = jnp.clip(1.0 + 0.15 * jax.random.normal(streams_of[5], (MODEL_DIMENSION,), jnp.float32), 0.25, 1.75)
    ffn_gain = jnp.clip(1.0 + 0.15 * jax.random.normal(streams_of[6], (MODEL_DIMENSION,), jnp.float32), 0.25, 1.75)
    query_gain = jnp.clip(1.0 + 0.15 * jax.random.normal(streams_of[7], (HEAD_SIZE,), jnp.float32), 0.25, 1.75)
    key_gain = jnp.clip(1.0 + 0.15 * jax.random.normal(streams_of[8], (HEAD_SIZE,), jnp.float32), 0.25, 1.75)
    w_query = bell_draw(streams_of[9], (MODEL_DIMENSION, QUERY_HEADS * HEAD_SIZE), MODEL_DIMENSION ** -0.5, 0.125, ((0, 4),))
    key_weight = bell_draw(streams_of[10], (MODEL_DIMENSION, KEY_VALUE_HEADS * HEAD_SIZE), MODEL_DIMENSION ** -0.5, 0.125, ((0, 4),))
    value_weight = bell_draw(streams_of[11], (MODEL_DIMENSION, KEY_VALUE_HEADS * HEAD_SIZE), MODEL_DIMENSION ** -0.5, 0.125, ((0, 4),))
    w_output = bell_draw(streams_of[12], (QUERY_HEADS * HEAD_SIZE, MODEL_DIMENSION), (max(QUERY_HEADS * HEAD_SIZE // 64, 1)) ** -0.5, 0.75, ((0, 4),))
    w_router = bell_draw(streams_of[13], (MODEL_DIMENSION, EXPERTS), (4 * MODEL_DIMENSION) ** -0.5, 0.0625, ((0, 4),))
    w_gate = bell_draw(streams_of[14], (EXPERTS, MODEL_DIMENSION, FF), MODEL_DIMENSION ** -0.5, 0.125, ((0, 32),))
    w_up = bell_draw(streams_of[15], (EXPERTS, MODEL_DIMENSION, FF), MODEL_DIMENSION ** -0.5, 0.125, ((0, 32),))
    w_down = bell_draw(streams_of[16], (EXPERTS, FF, MODEL_DIMENSION), (max(FF // 24, 1)) ** -0.5, 1.0, ((0, 32),))
    return dict(tokens=tokens, cotangent=cotangent, segments=segments, routes=routes, pair_order=pair_order, attn_gain=attn_gain, ffn_gain=ffn_gain, query_gain=query_gain, key_gain=key_gain, w_query=w_query, key_weight=key_weight, value_weight=value_weight, w_output=w_output, w_router=w_router, w_gate=w_gate, w_up=w_up, w_down=w_down)


EPSILON = 1e-06
ROPE_BASE = 1000000.0
MASKED = -1e+30

@jax.custom_vjp
def reduced_precision(v):
    return lax.optimization_barrier(v.astype(jnp.bfloat16)).astype(jnp.float32)

@jax.custom_vjp
def reduced_backward(v):
    return v

def low_keep(v):
    return (reduced_precision(v), None)

def low_pass(kept, grad):
    return (grad,)

def back_keep(v):
    return (v, None)

def back_low(kept, grad):
    return (reduced_precision(grad),)
reduced_precision.defvjp(low_keep, low_pass)
reduced_backward.defvjp(back_keep, back_low)

def product_highest(left, right):
    return jnp.dot(left, right, precision=lax.Precision.HIGHEST)

def rms_norm(value_vectors, gain_vector):
    return value_vectors * lax.rsqrt(lax.optimization_barrier(jnp.mean(value_vectors * value_vectors, axis=-1, keepdims=True)) + EPSILON) * gain_vector

def rope_tables(positions, head_width):
    inv_freq = ROPE_BASE ** (-jnp.arange(0, head_width // 2, dtype=jnp.float32) * 2.0 / head_width)
    angle_table = positions.astype(jnp.float32)[:, None] * inv_freq[None, :]
    angle_table = jnp.concatenate([angle_table, angle_table], axis=-1)
    return (jnp.cos(angle_table), jnp.sin(angle_table))

def rotate(value_vectors, cosine_table, sine_lookup):
    half_width = value_vectors.shape[-1] // 2
    turned = jnp.concatenate([-value_vectors[..., half_width:], value_vectors[..., :half_width]], axis=-1)
    return value_vectors * cosine_table[:, None, :] + turned * sine_lookup[:, None, :]

def prepare_heads(raw_values, gain_vector, cosine_table, sine_lookup, head_count):
    shaped = raw_values.reshape(raw_values.shape[0], head_count, -1)
    return rotate(rms_norm(shaped, gain_vector), cosine_table, sine_lookup)

def layout_positions(pair_order, half_rows):
    pair_count = pair_order.shape[0]
    offsets = jnp.arange(half_rows, dtype=jnp.int32)
    first_half = pair_order[:, None] * half_rows + offsets[None, :]
    second = (2 * pair_count - 1 - pair_order[:, None]) * half_rows + offsets[None, :]
    return jnp.concatenate([first_half, second], axis=1).reshape(-1).astype(jnp.int32)

def reference(tokens, cotangent, segments, routes, pair_order, attn_gain, ffn_gain, query_gain, key_gain, w_query, key_weight, value_weight, w_output, w_router, w_gate, w_up, w_down):
    positions = layout_positions(pair_order, HALF)
    layout_segments = segments[:, positions]
    cosine_table, sine_lookup = rope_tables(positions, HEAD_SIZE)
    causal = positions[None, :] <= positions[:, None]
    flat_routes = routes.reshape(TOKENS, TOP)
    counts = lax.optimization_barrier(jnp.sum((flat_routes.reshape(-1)[:, None] == jnp.arange(EXPERTS, dtype=jnp.int32)[None, :]).astype(jnp.float32), axis=0))
    shares = counts / (TOKENS * TOP)
    capacity_all = SEQS * PAIRS * 2 * HALF_CAP
    score_scale = HEAD_SIZE ** (-0.5)
    rows_per_block = min(512, SEQUENCE_LENGTH)

    def expert_rows(expert_index):
        route_hits = jnp.any(flat_routes == expert_index, axis=1)
        return jnp.nonzero(route_hits, size=capacity_all, fill_value=TOKENS)[0].astype(jnp.int32)
    row_table = lax.map(expert_rows, jnp.arange(EXPERTS, dtype=jnp.int32))
    padded_routes = jnp.concatenate([flat_routes, jnp.full((1, TOP), -1, jnp.int32)], axis=0)

    def forward(inputs, attn_g, ffn_g, query_g, key_gain_vector, wq, key_matrix, value_matrix, wo, wr, wg, wu, wd):

        def sequence(pieces):
            seq_in, seq_seg = pieces
            normalized_input = reduced_precision(rms_norm(seq_in, attn_g))
            query_reduced = reduced_precision(prepare_heads(reduced_backward(product_highest(normalized_input, wq)), query_g, cosine_table, sine_lookup, QUERY_HEADS))
            key_reduced = reduced_precision(prepare_heads(reduced_backward(product_highest(normalized_input, key_matrix)), key_gain_vector, cosine_table, sine_lookup, KEY_VALUE_HEADS))
            value_vectors = reduced_precision(reduced_backward(product_highest(normalized_input, value_matrix))).reshape(SEQUENCE_LENGTH, KEY_VALUE_HEADS, HEAD_SIZE)
            grouped_heads = query_reduced.reshape(SEQUENCE_LENGTH // rows_per_block, rows_per_block, KEY_VALUE_HEADS, QUERY_HEADS // KEY_VALUE_HEADS, HEAD_SIZE)
            allowed = causal & (seq_seg[:, None] == seq_seg[None, :])
            mask_blocks = allowed.reshape(SEQUENCE_LENGTH // rows_per_block, rows_per_block, SEQUENCE_LENGTH)

            def score_block(parts):
                query_part, mask_part = parts
                raw_scores = reduced_backward(jnp.einsum('tngd,knd->ngtk', query_part, key_reduced, precision=lax.Precision.HIGHEST))
                scores = jnp.where(mask_part[None, None], raw_scores * score_scale, MASKED)
                attn_probs = reduced_precision(jax.nn.softmax(scores, axis=-1))
                return jnp.einsum('ngtk,knd->tngd', attn_probs, value_vectors, precision=lax.Precision.HIGHEST)
            head_out = lax.map(jax.checkpoint(score_block), (grouped_heads, mask_blocks))
            head_out = reduced_precision(reduced_backward(head_out.reshape(SEQUENCE_LENGTH, QUERY_HEADS * HEAD_SIZE)))
            attn_out = reduced_backward(product_highest(head_out, wo))
            return seq_in + attn_out
        residual = lax.map(jax.checkpoint(sequence), (inputs, layout_segments))
        flat_tokens = residual.reshape(TOKENS, MODEL_DIMENSION)
        normed_two = reduced_precision(rms_norm(flat_tokens, ffn_g))
        logits = reduced_backward(product_highest(normed_two, wr))
        router_probs = jax.nn.softmax(logits, axis=-1)
        chosen = jnp.take_along_axis(router_probs, flat_routes, axis=1)
        gate_values = chosen / lax.optimization_barrier(jnp.sum(chosen, axis=1, keepdims=True))
        padded = jnp.concatenate([normed_two, jnp.zeros((1, MODEL_DIMENSION), jnp.float32)], axis=0)
        padded_gates = jnp.concatenate([gate_values, jnp.zeros((1, TOP), jnp.float32)], axis=0)

        def expert(parts):
            row_index, gate_w, up_w, down_w, expert_index = parts
            taken_rows = reduced_backward(padded[row_index])
            gate_pre = reduced_backward(product_highest(taken_rows, gate_w))
            up_pre = reduced_backward(product_highest(taken_rows, up_w))
            hidden = reduced_precision(jax.nn.silu(gate_pre) * up_pre)
            result = reduced_precision(reduced_backward(product_highest(hidden, down_w)))
            weight = lax.optimization_barrier(jnp.sum(jnp.where(padded_routes[row_index] == expert_index, padded_gates[row_index], 0.0), axis=1))
            return result * weight[:, None]
        contributions = lax.map(jax.checkpoint(expert), (row_table, wg, wu, wd, jnp.arange(EXPERTS, dtype=jnp.int32)))
        mixture = jnp.zeros((TOKENS + 1, MODEL_DIMENSION), jnp.float32).at[row_table.reshape(-1)].add(contributions.reshape(-1, MODEL_DIMENSION))[:TOKENS]
        output = (flat_tokens + mixture).reshape(SEQS, SEQUENCE_LENGTH, MODEL_DIMENSION)
        balance = EXPERTS * EXPERTS * shares * lax.optimization_barrier(jnp.mean(router_probs, axis=0))
        return (output, balance)
    params = (tokens.astype(jnp.float32), attn_gain, ffn_gain, query_gain, key_gain, w_query.astype(jnp.float32), key_weight.astype(jnp.float32), value_weight.astype(jnp.float32), w_output.astype(jnp.float32), w_router.astype(jnp.float32), w_gate.astype(jnp.float32), w_up.astype(jnp.float32), w_down.astype(jnp.float32))
    primal, pullback = jax.vjp(forward, *params)
    output, balance = primal
    gradients = pullback((cotangent.astype(jnp.float32), jnp.full((EXPERTS,), 1.0 / EXPERTS, jnp.float32)))
    loss = jnp.mean(balance)
    return (output.astype(jnp.bfloat16), loss, balance, gradients[0], gradients[1], gradients[2], gradients[3], gradients[4], gradients[5], gradients[6], gradients[7], gradients[8], gradients[9], gradients[10], gradients[11], gradients[12])
```

```python
import functools

import jax
import jax.numpy as jnp
from jax import lax
from jax.experimental import pallas as pl
from jax.experimental.pallas import tpu as pltpu
from jax.sharding import PartitionSpec as P

EPSILON = 1e-06
ROPE_BASE = 1000000.0
MASKED = -1e30
BF = jnp.bfloat16
F32 = jnp.float32
VMEM_SPEC = pl.BlockSpec(memory_space=pltpu.VMEM)
SMEM_SPEC = pl.BlockSpec(memory_space=pltpu.SMEM)
QUERY_ROWS = 128
KEY_ROWS = 256


def rms_norm(value_vectors, gain_vector):
    return (
        value_vectors
        * lax.rsqrt(jnp.mean(value_vectors * value_vectors, axis=-1, keepdims=True) + EPSILON)
        * gain_vector
    )


def low_matmul(left, right):
    return jnp.dot(left, right, preferred_element_type=F32)


def swiglu(gate_pre, up_pre):
    return jax.nn.silu(gate_pre) * up_pre


def rope_tables(length, head_width):
    inv_freq = ROPE_BASE ** (-jnp.arange(0, head_width // 2, dtype=F32) * 2.0 / head_width)
    angle_table = jnp.arange(length, dtype=F32)[:, None] * inv_freq[None, :]
    cosine, sine = jnp.cos(angle_table), jnp.sin(angle_table)
    return jnp.concatenate([cosine, cosine], 1), jnp.concatenate([-sine, sine], 1)


RELATIVE = (0, 2, 4, 6, 1, 3, 5, 7)


def swap(value, bit):
    count = lax.axis_size("ctx")
    return lax.ppermute(value, "ctx", [(i, i ^ bit) for i in range(count)])


def block_owner(count, me):
    if count == 8:
        return jnp.asarray(RELATIVE, jnp.int32) ^ me
    return jnp.arange(count, dtype=jnp.int32)


def plane_gather(block):
    count = lax.axis_size("ctx")
    if count != 8:
        return lax.all_gather(block, "ctx", axis=0, tiled=False)
    half = block.shape[0] // 2
    via_x = swap(block, 2)
    via_y = swap(block, 4)
    diag_a = swap(via_x[:half], 4)
    diag_b = swap(via_y[half:], 2)
    mine = jnp.concatenate([block, via_x, via_y, diag_a, diag_b], axis=0)
    return jnp.concatenate([mine, swap(mine, 1)], axis=0).reshape((count,) + block.shape)


def plane_scatter(parts):
    count = parts.shape[0]
    if count != 8:
        return lax.psum_scatter(parts, "ctx", scatter_dimension=0, tiled=False).astype(F32)
    half = parts.shape[1] // 2
    kept = parts[:4].astype(F32) + swap(parts[4:], 1).astype(F32)
    diag = kept[3].astype(BF)
    from_y = swap(diag[:half], 4)
    from_x = swap(diag[half:], 2)
    part_x = kept[1].at[:half].add(from_y.astype(F32)).astype(BF)
    part_y = kept[2].at[half:].add(from_x.astype(F32)).astype(BF)
    return kept[0] + swap(part_x, 2).astype(F32) + swap(part_y, 4).astype(F32)


def head_norm(raw, gain):
    scale = lax.rsqrt(jnp.mean(raw * raw, axis=-1, keepdims=True) + EPSILON)
    return raw * scale * gain


def turn(value):
    return pltpu.roll(value, value.shape[-1] // 2, 1)


def tile_mask(seg_col, seg_row, row_start, col_start):
    shape = (seg_col.shape[0], seg_row.shape[1])
    rows = lax.broadcasted_iota(jnp.int32, shape, 0) + row_start
    cols = lax.broadcasted_iota(jnp.int32, shape, 1) + col_start
    return (seg_col == seg_row) & (cols <= rows)


def attend_kernel(
    heads,
    block_ref,
    place_ref,
    first_ref,
    hidden_ref,
    weight_ref,
    query_gain_ref,
    key_gain_ref,
    cosine_ref,
    sine_ref,
    seg_row_ref,
    seg_col_ref,
    query_ref,
    key_ref,
    value_ref,
    raw_ref,
    out_ref,
    score_ref,
):
    count, rows, width = hidden_ref.shape
    half = rows // 2
    dim = query_gain_ref.shape[1]
    scale = dim ** (-0.5)

    def project(pair, carry):
        lhs = hidden_ref[pl.ds(pair * 2, 2)].reshape(2 * rows, width)
        raw = jnp.dot(lhs, weight_ref[...], preferred_element_type=F32)
        for piece in range(4):
            start = pl.multiple_of(block_ref[pair * 4 + piece] * half, half)
            spot = pl.ds(start, half)
            cosine, sine = cosine_ref[spot, :], sine_ref[spot, :]
            part = raw[piece * half : (piece + 1) * half]
            for head in range(heads + 1):
                cols = slice(head * dim, (head + 1) * dim)
                gain = query_gain_ref[...] if head < heads else key_gain_ref[...]
                normed = head_norm(part[:, cols], gain)
                roped = (normed * cosine + turn(normed) * sine).astype(BF)
                if head < heads:
                    query_ref[spot, cols] = roped
                else:
                    key_ref[spot, :] = roped
            raw_ref[spot, :] = part[:, : (heads + 1) * dim]
            value_ref[spot, :] = part[:, (heads + 1) * dim :].astype(BF)
        return carry

    lax.fori_loop(0, count // 2, project, 0)
    seq = key_ref.shape[0]
    stacked = heads * QUERY_ROWS

    def attend(index, carry):
        row_start = pl.multiple_of(index * QUERY_ROWS, QUERY_ROWS)
        row_spot = pl.ds(row_start, QUERY_ROWS)
        query = jnp.concatenate(
            [query_ref[row_spot, h * dim : (h + 1) * dim] for h in range(heads)], axis=0
        )
        seg_col = seg_col_ref[row_spot, :]
        low = first_ref[index] // KEY_ROWS
        high = (row_start + QUERY_ROWS + KEY_ROWS - 1) // KEY_ROWS

        def scores(tile, top):
            start = pl.multiple_of(tile * KEY_ROWS, KEY_ROWS)
            spot = pl.ds(start, KEY_ROWS)
            raw = lax.dot_general(
                query, key_ref[spot, :], (((1,), (1,)), ((), ())), preferred_element_type=F32
            )
            allowed = tile_mask(seg_col, seg_row_ref[:, spot], row_start, start)
            raw = raw.reshape(heads, QUERY_ROWS, KEY_ROWS) * scale
            masked = jnp.where(allowed[None], raw, MASKED).reshape(stacked, KEY_ROWS)
            score_ref[:, spot] = masked
            return jnp.maximum(top, jnp.max(masked, axis=1, keepdims=True))

        top = lax.fori_loop(low, high, scores, jnp.full((stacked, 1), MASKED, F32))

        def gather(tile, state):
            total, acc = state
            start = pl.multiple_of(tile * KEY_ROWS, KEY_ROWS)
            spot = pl.ds(start, KEY_ROWS)
            probs = jnp.exp(score_ref[:, spot] - top)
            total = total + jnp.sum(probs, axis=1, keepdims=True)
            acc = acc + jnp.dot(
                probs.astype(BF), value_ref[spot, :], preferred_element_type=F32
            )
            return total, acc

        total, acc = lax.fori_loop(
            low, high, gather, (jnp.zeros((stacked, 1), F32), jnp.zeros((stacked, dim), F32))
        )
        result = (acc / total).astype(BF)
        for head in range(heads):
            for piece in range(QUERY_ROWS // half):
                spot = place_ref[index * (QUERY_ROWS // half) + piece]
                begin = head * QUERY_ROWS + piece * half
                out_ref[spot, :, head * dim : (head + 1) * dim] = result[begin : begin + half]
        return carry

    lax.fori_loop(0, seq // QUERY_ROWS, attend, 0)


def attend_back_kernel(
    heads,
    place_ref,
    first_ref,
    grad_ref,
    query_ref,
    key_ref,
    value_ref,
    raw_ref,
    query_gain_ref,
    key_gain_ref,
    cosine_ref,
    sine_ref,
    seg_row_ref,
    seg_col_ref,
    out_ref,
    query_gain_grad_ref,
    key_gain_grad_ref,
    score_ref,
    prob_grad_ref,
    key_grad_ref,
    value_grad_ref,
):
    half = grad_ref.shape[1]
    dim = query_gain_ref.shape[1]
    scale = dim ** (-0.5)
    seq = key_ref.shape[0]
    stacked = heads * QUERY_ROWS
    pieces = QUERY_ROWS // half
    key_grad_ref[...] = jnp.zeros_like(key_grad_ref)
    value_grad_ref[...] = jnp.zeros_like(value_grad_ref)
    query_gain_grad_ref[...] = jnp.zeros_like(query_gain_grad_ref)
    key_gain_grad_ref[...] = jnp.zeros_like(key_gain_grad_ref)

    def unrope(grad, raw, gain, cosine, sine):
        norm_scale = lax.rsqrt(jnp.mean(raw * raw, axis=-1, keepdims=True) + EPSILON)
        unit = raw * norm_scale
        grad = grad * cosine + turn(grad * sine)
        gain_grad = jnp.sum(grad * unit, axis=0, keepdims=True)
        grad = grad * gain
        grad = norm_scale * (grad - unit * jnp.mean(grad * unit, axis=-1, keepdims=True))
        return grad, gain_grad

    def back(index, carry):
        row_start = pl.multiple_of(index * QUERY_ROWS, QUERY_ROWS)
        row_spot = pl.ds(row_start, QUERY_ROWS)
        places = [place_ref[index * pieces + piece] for piece in range(pieces)]
        query = jnp.concatenate(
            [query_ref[row_spot, h * dim : (h + 1) * dim] for h in range(heads)], axis=0
        )
        grad = jnp.concatenate(
            [
                grad_ref[place, :, h * dim : (h + 1) * dim]
                for h in range(heads)
                for place in places
            ],
            axis=0,
        )
        seg_col = seg_col_ref[row_spot, :]
        low = first_ref[index] // KEY_ROWS
        high = (row_start + QUERY_ROWS + KEY_ROWS - 1) // KEY_ROWS

        def scores(tile, top):
            start = pl.multiple_of(tile * KEY_ROWS, KEY_ROWS)
            spot = pl.ds(start, KEY_ROWS)
            raw = lax.dot_general(
                query, key_ref[spot, :], (((1,), (1,)), ((), ())), preferred_element_type=F32
            )
            allowed = tile_mask(seg_col, seg_row_ref[:, spot], row_start, start)
            raw = raw.reshape(heads, QUERY_ROWS, KEY_ROWS) * scale
            masked = jnp.where(allowed[None], raw, MASKED).reshape(stacked, KEY_ROWS)
            score_ref[:, spot] = masked
            return jnp.maximum(top, jnp.max(masked, axis=1, keepdims=True))

        top = lax.fori_loop(low, high, scores, jnp.full((stacked, 1), MASKED, F32))

        def probabilities(tile, state):
            total, inner = state
            start = pl.multiple_of(tile * KEY_ROWS, KEY_ROWS)
            spot = pl.ds(start, KEY_ROWS)
            probs = jnp.exp(score_ref[:, spot] - top)
            prob_grad = lax.dot_general(
                grad, value_ref[spot, :], (((1,), (1,)), ((), ())), preferred_element_type=F32
            )
            score_ref[:, spot] = probs
            prob_grad_ref[:, spot] = prob_grad
            total = total + jnp.sum(probs, axis=1, keepdims=True)
            inner = inner + jnp.sum(probs * prob_grad, axis=1, keepdims=True)
            return total, inner

        zero = jnp.zeros((stacked, 1), F32)
        total, inner = lax.fori_loop(low, high, probabilities, (zero, zero))
        share = 1.0 / total
        inner = inner * share

        def gradients(tile, acc):
            start = pl.multiple_of(tile * KEY_ROWS, KEY_ROWS)
            spot = pl.ds(start, KEY_ROWS)
            probs = score_ref[:, spot] * share
            score_grad = (probs * (prob_grad_ref[:, spot] - inner) * scale).astype(BF)
            acc = acc + jnp.dot(score_grad, key_ref[spot, :], preferred_element_type=F32)
            key_grad_ref[spot, :] += lax.dot_general(
                score_grad, query, (((0,), (0,)), ((), ())), preferred_element_type=F32
            )
            value_grad_ref[spot, :] += lax.dot_general(
                probs.astype(BF), grad, (((0,), (0,)), ((), ())), preferred_element_type=F32
            )
            return acc

        acc = lax.fori_loop(low, high, gradients, jnp.zeros((stacked, dim), F32))
        cosine, sine = cosine_ref[row_spot, :], sine_ref[row_spot, :]
        for head in range(heads):
            cols = slice(head * dim, (head + 1) * dim)
            part = acc[head * QUERY_ROWS : (head + 1) * QUERY_ROWS]
            part, gain_grad = unrope(
                part, raw_ref[row_spot, cols], query_gain_ref[...], cosine, sine
            )
            query_gain_grad_ref[...] += gain_grad
            part = part.astype(BF)
            for piece in range(pieces):
                out_ref[places[piece], :, cols] = part[piece * half : (piece + 1) * half]
        return carry

    lax.fori_loop(0, seq // QUERY_ROWS, back, 0)

    def finish(index, carry):
        row_start = pl.multiple_of(index * QUERY_ROWS, QUERY_ROWS)
        row_spot = pl.ds(row_start, QUERY_ROWS)
        key_cols = slice(heads * dim, (heads + 1) * dim)
        value_cols = slice((heads + 1) * dim, (heads + 2) * dim)
        part, gain_grad = unrope(
            key_grad_ref[row_spot, :],
            raw_ref[row_spot, key_cols],
            key_gain_ref[...],
            cosine_ref[row_spot, :],
            sine_ref[row_spot, :],
        )
        key_gain_grad_ref[...] += gain_grad
        part = part.astype(BF)
        value = value_grad_ref[row_spot, :].astype(BF)
        for piece in range(pieces):
            place = place_ref[index * pieces + piece]
            out_ref[place, :, key_cols] = part[piece * half : (piece + 1) * half]
            out_ref[place, :, value_cols] = value[piece * half : (piece + 1) * half]
        return carry

    lax.fori_loop(0, seq // QUERY_ROWS, finish, 0)


def move_slots(slot_array):
    return lax.all_to_all(slot_array, ("ctx", "wt"), split_axis=0, concat_axis=0, tiled=True)


def local(
    tokens,
    cotangent,
    segments,
    routes,
    pair_order,
    attn_gain,
    ffn_gain,
    query_gain,
    key_gain,
    w_query,
    key_weight,
    value_weight,
    w_output,
    w_router,
    w_gate,
    w_up,
    w_down,
):
    ctx_count = lax.axis_size("ctx")
    wt_count = lax.axis_size("wt")
    me = lax.axis_index("ctx")
    plane = lax.axis_index("wt")
    inputs = tokens[0].astype(F32)
    tok_rows, model_width = inputs.shape
    half_rows = tok_rows // 2
    head_dim = query_gain.shape[0]
    experts = w_router.shape[1]
    top_count = routes.shape[2]
    seq_len = segments.shape[1]
    total_tokens = tok_rows * ctx_count * wt_count
    heads = w_query.shape[1] // head_dim // ctx_count
    kv_heads = key_weight.shape[1] // head_dim
    share = ctx_count // kv_heads
    head_cols = heads * head_dim
    group = me // share

    kv_start = group * head_dim
    own_weight = jnp.concatenate(
        [
            lax.dynamic_slice_in_dim(w_query, me * head_cols, head_cols, 1),
            lax.dynamic_slice_in_dim(key_weight, kv_start, head_dim, 1),
            lax.dynamic_slice_in_dim(value_weight, kv_start, head_dim, 1),
        ],
        axis=1,
    )
    weight = lax.all_gather(own_weight, "wt", axis=0, tiled=True)
    own_chunks = ctx_count // wt_count
    piece_rows = head_cols // ctx_count
    out_piece = lax.dynamic_index_in_dim(
        w_output.reshape(own_chunks, ctx_count, piece_rows, model_width), me, 1, keepdims=False
    )
    out_pieces = lax.all_gather(out_piece, "wt", axis=0, tiled=True)
    out_weight = lax.all_to_all(out_pieces, "ctx", 0, 0, tiled=True).reshape(
        head_cols, model_width
    )
    w_router_all = lax.all_gather(w_router, "wt", axis=0, tiled=True)

    owner_pair = pair_order[block_owner(ctx_count, me)]
    blocks = jnp.stack([owner_pair, 2 * ctx_count - 1 - owner_pair], 1).reshape(-1)
    order = jnp.arange(2 * ctx_count, dtype=jnp.int32)
    places = jnp.sum(jnp.where(blocks[:, None] == order[None, :], order[:, None], 0), axis=0)
    places = places.astype(jnp.int32)
    seg = segments[0]
    first = jnp.sum(
        (seg[None, :] < seg[::QUERY_ROWS][:, None]).astype(jnp.int32), axis=1
    ).astype(jnp.int32)
    seg_row, seg_col = seg.reshape(1, seq_len), seg.reshape(seq_len, 1)
    cosine, sine = rope_tables(seq_len, head_dim)
    query_gain_row, key_gain_row = query_gain.reshape(1, -1), key_gain.reshape(1, -1)

    normed_one, attn_back = jax.vjp(rms_norm, inputs, attn_gain)
    hidden_all = plane_gather(normed_one.astype(BF))
    width = head_cols + 2 * head_dim
    stacked = heads * QUERY_ROWS
    query, key, value, raw, attn_low = pl.pallas_call(
        functools.partial(attend_kernel, heads),
        out_shape=(
            jax.ShapeDtypeStruct((seq_len, head_cols), BF),
            jax.ShapeDtypeStruct((seq_len, head_dim), BF),
            jax.ShapeDtypeStruct((seq_len, head_dim), BF),
            jax.ShapeDtypeStruct((seq_len, head_cols + head_dim), F32),
            jax.ShapeDtypeStruct((2 * ctx_count, half_rows, head_cols), BF),
        ),
        in_specs=[SMEM_SPEC] * 3 + [VMEM_SPEC] * 8,
        out_specs=[VMEM_SPEC] * 5,
        scratch_shapes=[pltpu.VMEM((stacked, seq_len), F32)],
        cost_estimate=pl.CostEstimate(
            flops=2 * seq_len * model_width * width + 2 * seq_len * seq_len * head_cols,
            bytes_accessed=16 << 20,
            transcendentals=heads * seq_len * seq_len // 2,
        ),
    )(
        blocks,
        places,
        first,
        hidden_all,
        weight,
        query_gain_row,
        key_gain_row,
        cosine,
        sine,
        seg_row,
        seg_col,
    )
    attn_rows = attn_low.reshape(seq_len, head_cols)
    attn_part = low_matmul(attn_rows, out_weight).astype(BF)
    residual = inputs + plane_scatter(attn_part.reshape(ctx_count, tok_rows, model_width))
    normed_two, ffn_back = jax.vjp(rms_norm, residual, ffn_gain)
    normed_two_low = normed_two.astype(BF)
    grad_out = cotangent[0].astype(F32)
    capacity = max(2, half_rows * top_count * 5 // (4 * experts))
    slot_rows = 2 * capacity
    local_experts = w_gate.shape[0]
    logits = low_matmul(normed_two_low, w_router_all)
    local_routes = routes[0]

    def router_fn(logit_values):
        router_probs = jax.nn.softmax(logit_values, axis=-1)
        chosen = jnp.take_along_axis(router_probs, local_routes, axis=1)
        return (chosen / jnp.sum(chosen, axis=1, keepdims=True), router_probs)

    (gate_values, router_probs), router_back = jax.vjp(router_fn, logits)
    route_flat = local_routes.reshape(-1)
    route_hits = (route_flat[:, None] == jnp.arange(experts, dtype=jnp.int32)[None, :]).astype(
        jnp.int32
    )
    counts, prob_sums = lax.psum(
        (jnp.sum(route_hits, axis=0).astype(jnp.float32), jnp.sum(router_probs, axis=0)),
        ("ctx", "wt"),
    )
    shares = counts / (total_tokens * top_count)
    balance = experts * experts * shares * (prob_sums / total_tokens)
    loss_value = jnp.mean(balance)
    halves = route_hits.reshape(2, half_rows * top_count, experts)
    ranks = jnp.sum((jnp.cumsum(halves, axis=1) - halves) * halves, axis=2).reshape(-1)
    half_index = jnp.arange(tok_rows * top_count, dtype=jnp.int32) // (half_rows * top_count)
    slot_index = route_flat * slot_rows + half_index * capacity + ranks
    slot_owner = (
        jnp.full((experts * slot_rows,), tok_rows * top_count, jnp.int32)
        .at[slot_index]
        .set(jnp.arange(tok_rows * top_count, dtype=jnp.int32))
    )
    slot_shape = (experts // local_experts, local_experts, slot_rows, model_width)
    padded = jnp.concatenate([normed_two_low, jnp.zeros((1, model_width), jnp.bfloat16)], axis=0)
    outgoing = padded[slot_owner // top_count].reshape(slot_shape)
    arrived = move_slots(outgoing)
    gate_pre = jnp.einsum("nesd,edf->nesf", arrived, w_gate, preferred_element_type=jnp.float32)
    up_pre = jnp.einsum("nesd,edf->nesf", arrived, w_up, preferred_element_type=jnp.float32)
    hidden_low, swiglu_back = jax.vjp(swiglu, gate_pre, up_pre)
    hidden_low = hidden_low.astype(jnp.bfloat16)
    expert_out = jnp.einsum(
        "nesf,efd->nesd", hidden_low, w_down, preferred_element_type=jnp.float32
    ).astype(jnp.bfloat16)
    returned = move_slots(expert_out).reshape(experts * slot_rows, model_width)
    picked = returned[slot_index].reshape(tok_rows, top_count, model_width)
    mixture = jnp.einsum("tk,tkd->td", gate_values, picked, preferred_element_type=jnp.float32)
    output = (residual + mixture).astype(jnp.bfloat16)
    grad_gates = jnp.einsum("td,tkd->tk", grad_out, picked, preferred_element_type=jnp.float32)
    grad_routed = (
        (gate_values[:, :, None] * grad_out[:, None, :])
        .astype(jnp.bfloat16)
        .reshape(-1, model_width)
    )
    grad_routed = jnp.concatenate([grad_routed, jnp.zeros((1, model_width), jnp.bfloat16)], axis=0)
    grad_arrived = move_slots(grad_routed[slot_owner].reshape(slot_shape))
    grad_hidden = jnp.einsum(
        "nesd,efd->nesf", grad_arrived, w_down, preferred_element_type=jnp.float32
    )
    grad_w_down = jnp.einsum(
        "nesf,nesd->efd", hidden_low, grad_arrived, preferred_element_type=jnp.float32
    )
    grad_gate_pre, grad_up_pre = swiglu_back(grad_hidden)
    gate_grad_low = grad_gate_pre.astype(jnp.bfloat16)
    up_grad_low = grad_up_pre.astype(jnp.bfloat16)
    grad_w_gate = jnp.einsum(
        "nesd,nesf->edf", arrived, gate_grad_low, preferred_element_type=jnp.float32
    )
    grad_w_up = jnp.einsum(
        "nesd,nesf->edf", arrived, up_grad_low, preferred_element_type=jnp.float32
    )
    grad_slots = (
        jnp.einsum("nesf,edf->nesd", gate_grad_low, w_gate, preferred_element_type=jnp.float32)
        + jnp.einsum("nesf,edf->nesd", up_grad_low, w_up, preferred_element_type=jnp.float32)
    ).astype(jnp.bfloat16)
    grad_back = move_slots(grad_slots).reshape(experts * slot_rows, model_width)
    grad_normed_two = jnp.sum(
        grad_back[slot_index].reshape(tok_rows, top_count, model_width).astype(jnp.float32), axis=1
    )
    prob_grad = jnp.broadcast_to(experts * shares / total_tokens, router_probs.shape)
    (grad_logits,) = router_back((grad_gates, prob_grad))
    logits_low = grad_logits.astype(jnp.bfloat16)
    grad_normed_two = grad_normed_two + jnp.einsum(
        "te,de->td", logits_low, w_router_all, preferred_element_type=jnp.float32
    )
    grad_w_router = jnp.einsum(
        "td,te->de", normed_two_low, logits_low, preferred_element_type=jnp.float32
    )
    grad_residual_part, grad_ffn_gain = ffn_back(grad_normed_two)
    grad_residual = grad_out + grad_residual_part
    grad_attn_all = plane_gather(grad_residual.astype(BF)).reshape(seq_len, model_width)
    grad_heads = lax.dot_general(
        grad_attn_all, out_weight, (((1,), (1,)), ((), ())), preferred_element_type=F32
    ).astype(BF)
    head_grads, grad_query_gain, grad_key_gain = pl.pallas_call(
        functools.partial(attend_back_kernel, heads),
        out_shape=(
            jax.ShapeDtypeStruct((2 * ctx_count, half_rows, width), BF),
            jax.ShapeDtypeStruct((1, head_dim), F32),
            jax.ShapeDtypeStruct((1, head_dim), F32),
        ),
        in_specs=[SMEM_SPEC] * 2 + [VMEM_SPEC] * 11,
        out_specs=[VMEM_SPEC] * 3,
        scratch_shapes=[
            pltpu.VMEM((stacked, seq_len), F32),
            pltpu.VMEM((stacked, seq_len), F32),
            pltpu.VMEM((seq_len, head_dim), F32),
            pltpu.VMEM((seq_len, head_dim), F32),
        ],
        cost_estimate=pl.CostEstimate(
            flops=5 * seq_len * seq_len * head_cols,
            bytes_accessed=12 << 20,
            transcendentals=heads * seq_len * seq_len // 2,
        ),
    )(
        places,
        first,
        grad_heads.reshape(2 * ctx_count, half_rows, head_cols),
        query,
        key,
        value,
        raw,
        query_gain_row,
        key_gain_row,
        cosine,
        sine,
        seg_row,
        seg_col,
    )
    head_grads = head_grads.reshape(seq_len, width)
    hidden_rows = hidden_all.reshape(seq_len, model_width)
    weight_grad = lax.dot_general(
        hidden_rows, head_grads, (((0,), (0,)), ((), ())), preferred_element_type=F32
    ).astype(BF)
    weight_grad = lax.psum_scatter(weight_grad, "wt", scatter_dimension=0, tiled=True)
    weight_grads = lax.all_gather(weight_grad, "ctx", axis=0, tiled=False)
    shard_rows = w_query.shape[0]
    grad_w_query = (
        weight_grads[:, :, :head_cols].transpose(1, 0, 2).reshape(shard_rows, -1).astype(F32)
    )

    def pair_sum(cols):
        cols = cols.astype(F32).reshape(kv_heads, share, shard_rows, head_dim)
        return jnp.sum(cols, axis=1).transpose(1, 0, 2).reshape(shard_rows, -1)

    grad_w_key = pair_sum(weight_grads[:, :, head_cols : head_cols + head_dim])
    grad_w_value = pair_sum(weight_grads[:, :, head_cols + head_dim :])
    out_grad = lax.dot_general(
        attn_rows, grad_attn_all, (((0,), (0,)), ((), ())), preferred_element_type=F32
    ).astype(BF)
    out_grad = lax.all_to_all(
        out_grad.reshape(ctx_count, piece_rows, model_width), "ctx", 0, 0, tiled=True
    )
    out_grad = lax.psum_scatter(out_grad, "wt", scatter_dimension=0, tiled=True)
    out_grads = lax.all_gather(out_grad, "ctx", axis=1, tiled=False)
    grad_w_output = out_grads.reshape(w_output.shape).astype(F32)
    grad_hidden_part = lax.dot_general(
        head_grads, weight, (((1,), (1,)), ((), ())), preferred_element_type=F32
    ).astype(BF)
    grad_normed_one = plane_scatter(grad_hidden_part.reshape(ctx_count, tok_rows, model_width))
    grad_inputs_part, grad_attn_gain = attn_back(grad_normed_one)
    grad_inputs = grad_residual + grad_inputs_part
    small = lax.psum(
        (
            grad_w_router,
            grad_attn_gain,
            grad_ffn_gain,
            grad_query_gain[0],
            grad_key_gain[0],
        ),
        ("ctx", "wt"),
    )
    small = [
        lax.dynamic_slice_in_dim(s, plane * (s.shape[0] // wt_count), s.shape[0] // wt_count, 0)
        for s in small
    ]
    return (
        output[None],
        loss_value,
        balance,
        grad_inputs[None],
        small[1],
        small[2],
        small[3],
        small[4],
        grad_w_query,
        grad_w_key,
        grad_w_value,
        grad_w_output,
        small[0],
        grad_w_gate,
        grad_w_up,
        grad_w_down,
    )


def solution(mesh):
    in_specs = (
        P("wt", "ctx", None),
        P("wt", "ctx", None),
        P("wt", None),
        P("wt", "ctx", None),
        P(),
        P(),
        P(),
        P(),
        P(),
        P("wt", None),
        P("wt", None),
        P("wt", None),
        P("wt", None),
        P("wt", None),
        P(("ctx", "wt"), None, None),
        P(("ctx", "wt"), None, None),
        P(("ctx", "wt"), None, None),
    )
    out_specs = (
        P("wt", "ctx", None),
        P(),
        P(),
        P("wt", "ctx", None),
        P("wt"),
        P("wt"),
        P("wt"),
        P("wt"),
        P("wt", None),
        P("wt", None),
        P("wt", None),
        P("wt", None),
        P("wt", None),
        P(("ctx", "wt"), None, None),
        P(("ctx", "wt"), None, None),
        P(("ctx", "wt"), None, None),
    )
    return jax.shard_map(local, mesh=mesh, in_specs=in_specs, out_specs=out_specs, check_vma=False)
```

```python
import functools

import jax
import jax.numpy as jnp
from jax import lax
from jax.experimental import pallas as pl
from jax.experimental.pallas import tpu as pltpu
from jax.sharding import PartitionSpec as P

EPSILON = 1e-06
ROPE_BASE = 1000000.0
MASKED = -1e30
BF = jnp.bfloat16
F32 = jnp.float32
VMEM_SPEC = pl.BlockSpec(memory_space=pltpu.VMEM)
SMEM_SPEC = pl.BlockSpec(memory_space=pltpu.SMEM)
QUERY_ROWS = 128
KEY_ROWS = 256
ATTEND_LIMIT = 40 << 20
COST = pl.CostEstimate(flops=1, bytes_accessed=1, transcendentals=0)


def rms_norm(value_vectors, gain_vector):
    return (
        value_vectors
        * lax.rsqrt(jnp.mean(value_vectors * value_vectors, axis=-1, keepdims=True) + EPSILON)
        * gain_vector
    )


def low_matmul(left, right):
    return jnp.dot(left, right, preferred_element_type=F32)


def swiglu(gate_pre, up_pre):
    return jax.nn.silu(gate_pre) * up_pre


def rope_tables(length, head_width):
    inv_freq = ROPE_BASE ** (-jnp.arange(0, head_width // 2, dtype=F32) * 2.0 / head_width)
    angle_table = jnp.arange(length, dtype=F32)[:, None] * inv_freq[None, :]
    cosine, sine = jnp.cos(angle_table), jnp.sin(angle_table)
    return jnp.concatenate([cosine, cosine], 1), jnp.concatenate([-sine, sine], 1)


RELATIVE = (0, 2, 4, 6, 1, 3, 5, 7)


def swap(value, bit):
    count = lax.axis_size("ctx")
    return lax.ppermute(value, "ctx", [(i, i ^ bit) for i in range(count)])


def block_owner(count, me):
    if count == 8:
        return jnp.asarray(RELATIVE, jnp.int32) ^ me
    return jnp.arange(count, dtype=jnp.int32)


def after(value, *others):
    return lax.optimization_barrier((value,) + others)[0]


def plane_pieces(block):
    half = block.shape[0] // 2
    via_x = swap(block, 2)
    via_y = swap(block, 4)
    return [block, via_x, via_y, swap(via_x[:half], 4), swap(via_y[half:], 2)]


def plane_sends(block):
    half = block.shape[0] // 2
    via_x = swap(block, 2)
    via_y = swap(block, 4)
    from_x, from_y = via_x[:half], via_y[half:]
    return [block, via_x, via_y, swap(from_x, 4), swap(from_y, 2)], (from_x, from_y)


def plane_gather(block):
    count = lax.axis_size("ctx")
    if count != 8:
        return [lax.all_gather(block, "ctx", axis=0, tiled=True)]
    mine = plane_pieces(block)
    return mine + [swap(piece, 1) for piece in mine]


def diag_sends(diag):
    half = diag.shape[0] // 2
    return swap(diag[:half], 4), swap(diag[half:], 2)


def add_diag(part_x, part_y, from_y, from_x):
    half = from_y.shape[0]
    part_x, part_y = part_x.astype(F32), part_y.astype(F32)
    part_x = jnp.concatenate([part_x[:half] + from_y.astype(F32), part_x[half:]], 0).astype(BF)
    part_y = jnp.concatenate([part_y[:half], part_y[half:] + from_x.astype(F32)], 0).astype(BF)
    return part_x, part_y


def plane_sum(own, part_x, part_y, diag):
    part_x, part_y = add_diag(part_x, part_y, *diag_sends(diag))
    return own.astype(F32) + swap(part_x, 2).astype(F32) + swap(part_y, 4).astype(F32)


def plane_scatter(multiply, left, fill=None, *others):
    count = lax.axis_size("ctx")
    if count != 8:
        parts = multiply(left).astype(BF)
        return lax.psum_scatter(parts, "ctx", scatter_dimension=0, tiled=True).astype(F32)
    side = left.shape[0] // 2
    rows = side // 4
    give = multiply(left[side:]).astype(BF)
    got = swap(give, 1)
    keep = multiply(after(left[:side], give))
    kept = keep + after(got, keep).astype(F32)
    if others:
        kept = after(kept, *others)
    diag = kept[3 * rows :].astype(BF)
    half = rows // 2
    sends = diag[:half], diag[half:]
    from_y, from_x = swap(sends[0], 4), swap(sends[1], 2)
    if fill is not None:
        from_y, from_x = after((from_y, from_x), fill(sends))
    part_x, part_y = add_diag(kept[rows : 2 * rows], kept[2 * rows : 3 * rows], from_y, from_x)
    return kept[:rows] + swap(part_x, 2).astype(F32) + swap(part_y, 4).astype(F32)


def ring(value):
    count = lax.axis_size("wt")
    return lax.ppermute(value, "wt", [(i, (i + 1) % count) for i in range(count)])


def ring_chunks(block):
    chunks = [block]
    for _ in range(lax.axis_size("wt") - 1):
        chunks.append(ring(chunks[-1]))
    return chunks


def ring_sum(parts, kind):
    total = parts[1]
    for part in parts[2:] + parts[:1]:
        total = ring(total.astype(kind)).astype(F32) + part
    return total


def axis_sum(value, name):
    count = lax.axis_size(name)
    bit = 1
    while bit < count:
        value = value + lax.ppermute(value, name, [(i, i ^ bit) for i in range(count)])
        bit *= 2
    return value


def head_norm(raw, gain):
    scale = lax.rsqrt(jnp.mean(raw * raw, axis=-1, keepdims=True) + EPSILON)
    return raw * scale * gain


def turn(value):
    return pltpu.roll(value, value.shape[-1] // 2, 1)


def tile_mask(seg_col, seg_row, row_start, col_start):
    shape = (seg_col.shape[0], seg_row.shape[1])
    rows = lax.broadcasted_iota(jnp.int32, shape, 0) + row_start
    cols = lax.broadcasted_iota(jnp.int32, shape, 1) + col_start
    return (seg_col == seg_row) & (cols <= rows)


def attend_kernel(
    heads,
    pieces,
    block_ref,
    place_ref,
    first_ref,
    *refs,
):
    attend_body(heads, block_ref, place_ref, first_ref, refs[:pieces], *refs[pieces:])


def joined(refs, rows):
    group, have = [], 0
    for ref in refs:
        for start in range(0, ref.shape[0], rows):
            stop = min(start + rows, ref.shape[0])
            group.append(ref[start:stop])
            have += stop - start
            if have == rows:
                yield group[0] if len(group) == 1 else jnp.concatenate(group, axis=0)
                group, have = [], 0


def attend_body(
    heads,
    block_ref,
    place_ref,
    first_ref,
    hidden_refs,
    weight_ref,
    query_gain_ref,
    key_gain_ref,
    cosine_ref,
    sine_ref,
    seg_row_ref,
    seg_col_ref,
    query_ref,
    key_ref,
    value_ref,
    raw_ref,
    out_ref,
    score_ref,
):
    half = out_ref.shape[1]
    dim = query_gain_ref.shape[1]
    scale = dim ** (-0.5)

    for pair, lhs in enumerate(joined(hidden_refs, 4 * half)):
        raw = jnp.dot(lhs, weight_ref[...], preferred_element_type=F32)
        for piece in range(4):
            start = pl.multiple_of(block_ref[pair * 4 + piece] * half, half)
            spot = pl.ds(start, half)
            cosine, sine = cosine_ref[spot, :], sine_ref[spot, :]
            part = raw[piece * half : (piece + 1) * half]
            for head in range(heads + 1):
                cols = slice(head * dim, (head + 1) * dim)
                gain = query_gain_ref[...] if head < heads else key_gain_ref[...]
                normed = head_norm(part[:, cols], gain)
                roped = (normed * cosine + turn(normed) * sine).astype(BF)
                if head < heads:
                    query_ref[spot, cols] = roped
                else:
                    key_ref[spot, :] = roped
            raw_ref[spot, :] = part[:, : (heads + 1) * dim]
            value_ref[spot, :] = part[:, (heads + 1) * dim :].astype(BF)

    seq = key_ref.shape[0]
    stacked = heads * QUERY_ROWS

    def attend(index, carry):
        row_start = pl.multiple_of(index * QUERY_ROWS, QUERY_ROWS)
        row_spot = pl.ds(row_start, QUERY_ROWS)
        query = jnp.concatenate(
            [query_ref[row_spot, h * dim : (h + 1) * dim] for h in range(heads)], axis=0
        )
        seg_col = seg_col_ref[row_spot, :]
        low = first_ref[index] // KEY_ROWS
        high = (row_start + QUERY_ROWS + KEY_ROWS - 1) // KEY_ROWS

        def scores(tile, top):
            start = pl.multiple_of(tile * KEY_ROWS, KEY_ROWS)
            spot = pl.ds(start, KEY_ROWS)
            raw = lax.dot_general(
                query, key_ref[spot, :], (((1,), (1,)), ((), ())), preferred_element_type=F32
            )
            allowed = tile_mask(seg_col, seg_row_ref[:, spot], row_start, start)
            raw = raw.reshape(heads, QUERY_ROWS, KEY_ROWS) * scale
            masked = jnp.where(allowed[None], raw, MASKED).reshape(stacked, KEY_ROWS)
            score_ref[:, spot] = masked
            return jnp.maximum(top, jnp.max(masked, axis=1, keepdims=True))

        top = lax.fori_loop(low, high, scores, jnp.full((stacked, 1), MASKED, F32))

        def gather(tile, state):
            total, acc = state
            start = pl.multiple_of(tile * KEY_ROWS, KEY_ROWS)
            spot = pl.ds(start, KEY_ROWS)
            probs = jnp.exp(score_ref[:, spot] - top)
            total = total + jnp.sum(probs, axis=1, keepdims=True)
            acc = acc + jnp.dot(
                probs.astype(BF), value_ref[spot, :], preferred_element_type=F32
            )
            return total, acc

        total, acc = lax.fori_loop(
            low, high, gather, (jnp.zeros((stacked, 1), F32), jnp.zeros((stacked, dim), F32))
        )
        result = (acc / total).astype(BF)
        for head in range(heads):
            for piece in range(QUERY_ROWS // half):
                spot = place_ref[index * (QUERY_ROWS // half) + piece]
                begin = head * QUERY_ROWS + piece * half
                out_ref[spot, :, head * dim : (head + 1) * dim] = result[begin : begin + half]
        return carry

    lax.fori_loop(0, seq // QUERY_ROWS, attend, 0)


def attend_back_kernel(heads, pieces, place_ref, first_ref, *refs):
    attend_back_body(heads, place_ref, first_ref, refs[:pieces], *refs[pieces:])


def attend_back_body(
    heads,
    place_ref,
    first_ref,
    piece_refs,
    out_weight_ref,
    query_ref,
    key_ref,
    value_ref,
    raw_ref,
    query_gain_ref,
    key_gain_ref,
    cosine_ref,
    sine_ref,
    seg_row_ref,
    seg_col_ref,
    out_ref,
    query_gain_grad_ref,
    key_gain_grad_ref,
    score_ref,
    prob_grad_ref,
    key_grad_ref,
    value_grad_ref,
    grad_ref,
):
    half = grad_ref.shape[1]
    spot = 0
    for part in joined(piece_refs, 4 * half):
        part = lax.dot_general(
            part, out_weight_ref[...], (((1,), (1,)), ((), ())), preferred_element_type=F32
        ).astype(BF)
        for piece in range(4):
            grad_ref[spot] = part[piece * half : (piece + 1) * half]
            spot += 1
    dim = query_gain_ref.shape[1]
    scale = dim ** (-0.5)
    seq = key_ref.shape[0]
    stacked = heads * QUERY_ROWS
    pieces = QUERY_ROWS // half
    key_grad_ref[...] = jnp.zeros_like(key_grad_ref)
    value_grad_ref[...] = jnp.zeros_like(value_grad_ref)
    query_gain_grad_ref[...] = jnp.zeros_like(query_gain_grad_ref)
    key_gain_grad_ref[...] = jnp.zeros_like(key_gain_grad_ref)

    def unrope(grad, raw, gain, cosine, sine):
        norm_scale = lax.rsqrt(jnp.mean(raw * raw, axis=-1, keepdims=True) + EPSILON)
        unit = raw * norm_scale
        grad = grad * cosine + turn(grad * sine)
        gain_grad = jnp.sum(grad * unit, axis=0, keepdims=True)
        grad = grad * gain
        grad = norm_scale * (grad - unit * jnp.mean(grad * unit, axis=-1, keepdims=True))
        return grad, gain_grad

    def back(index, carry):
        row_start = pl.multiple_of(index * QUERY_ROWS, QUERY_ROWS)
        row_spot = pl.ds(row_start, QUERY_ROWS)
        places = [place_ref[index * pieces + piece] for piece in range(pieces)]
        query = jnp.concatenate(
            [query_ref[row_spot, h * dim : (h + 1) * dim] for h in range(heads)], axis=0
        )
        grad = jnp.concatenate(
            [
                grad_ref[place, :, h * dim : (h + 1) * dim]
                for h in range(heads)
                for place in places
            ],
            axis=0,
        )
        seg_col = seg_col_ref[row_spot, :]
        low = first_ref[index] // KEY_ROWS
        high = (row_start + QUERY_ROWS + KEY_ROWS - 1) // KEY_ROWS

        def scores(tile, top):
            start = pl.multiple_of(tile * KEY_ROWS, KEY_ROWS)
            spot = pl.ds(start, KEY_ROWS)
            raw = lax.dot_general(
                query, key_ref[spot, :], (((1,), (1,)), ((), ())), preferred_element_type=F32
            )
            allowed = tile_mask(seg_col, seg_row_ref[:, spot], row_start, start)
            raw = raw.reshape(heads, QUERY_ROWS, KEY_ROWS) * scale
            masked = jnp.where(allowed[None], raw, MASKED).reshape(stacked, KEY_ROWS)
            score_ref[:, spot] = masked
            return jnp.maximum(top, jnp.max(masked, axis=1, keepdims=True))

        top = lax.fori_loop(low, high, scores, jnp.full((stacked, 1), MASKED, F32))

        def probabilities(tile, state):
            total, inner = state
            start = pl.multiple_of(tile * KEY_ROWS, KEY_ROWS)
            spot = pl.ds(start, KEY_ROWS)
            probs = jnp.exp(score_ref[:, spot] - top)
            prob_grad = lax.dot_general(
                grad, value_ref[spot, :], (((1,), (1,)), ((), ())), preferred_element_type=F32
            )
            score_ref[:, spot] = probs
            prob_grad_ref[:, spot] = prob_grad
            total = total + jnp.sum(probs, axis=1, keepdims=True)
            inner = inner + jnp.sum(probs * prob_grad, axis=1, keepdims=True)
            return total, inner

        zero = jnp.zeros((stacked, 1), F32)
        total, inner = lax.fori_loop(low, high, probabilities, (zero, zero))
        share = 1.0 / total
        inner = inner * share

        def gradients(tile, acc):
            start = pl.multiple_of(tile * KEY_ROWS, KEY_ROWS)
            spot = pl.ds(start, KEY_ROWS)
            probs = score_ref[:, spot] * share
            score_grad = (probs * (prob_grad_ref[:, spot] - inner) * scale).astype(BF)
            acc = acc + jnp.dot(score_grad, key_ref[spot, :], preferred_element_type=F32)
            key_grad_ref[spot, :] += lax.dot_general(
                score_grad, query, (((0,), (0,)), ((), ())), preferred_element_type=F32
            )
            value_grad_ref[spot, :] += lax.dot_general(
                probs.astype(BF), grad, (((0,), (0,)), ((), ())), preferred_element_type=F32
            )
            return acc

        acc = lax.fori_loop(low, high, gradients, jnp.zeros((stacked, dim), F32))
        cosine, sine = cosine_ref[row_spot, :], sine_ref[row_spot, :]
        for head in range(heads):
            cols = slice(head * dim, (head + 1) * dim)
            part = acc[head * QUERY_ROWS : (head + 1) * QUERY_ROWS]
            part, gain_grad = unrope(
                part, raw_ref[row_spot, cols], query_gain_ref[...], cosine, sine
            )
            query_gain_grad_ref[...] += gain_grad
            part = part.astype(BF)
            for piece in range(pieces):
                out_ref[places[piece], :, cols] = part[piece * half : (piece + 1) * half]
        return carry

    lax.fori_loop(0, seq // QUERY_ROWS, back, 0)

    def finish(index, carry):
        row_start = pl.multiple_of(index * QUERY_ROWS, QUERY_ROWS)
        row_spot = pl.ds(row_start, QUERY_ROWS)
        key_cols = slice(heads * dim, (heads + 1) * dim)
        value_cols = slice((heads + 1) * dim, (heads + 2) * dim)
        part, gain_grad = unrope(
            key_grad_ref[row_spot, :],
            raw_ref[row_spot, key_cols],
            key_gain_ref[...],
            cosine_ref[row_spot, :],
            sine_ref[row_spot, :],
        )
        key_gain_grad_ref[...] += gain_grad
        part = part.astype(BF)
        value = value_grad_ref[row_spot, :].astype(BF)
        for piece in range(pieces):
            place = place_ref[index * pieces + piece]
            out_ref[place, :, key_cols] = part[piece * half : (piece + 1) * half]
            out_ref[place, :, value_cols] = value[piece * half : (piece + 1) * half]
        return carry

    lax.fori_loop(0, seq // QUERY_ROWS, finish, 0)


def one_hot(hit):
    return hit.astype(F32).astype(BF)


def select_kernel(groups, joint, *refs):
    target_ref, mine_ref, other_ref = refs[sum(groups) :]
    slots = mine_ref.shape[0] // 2
    target = target_ref[...]
    half = target.shape[1] // 8
    index = lax.broadcasted_iota(jnp.int32, (2 * slots, target.shape[1]), 0)
    pick = one_hot((index == target[0:1]) | (index == target[1:2]))
    for k in range(2):
        rows = []
        if joint:
            for ref in refs[: groups[0]]:
                for start in range(k * half, ref.shape[0], 2 * half):
                    rows.append(ref[start : start + half])
        else:
            first = k * groups[0]
            rows = [ref[...] for ref in refs[first : first + groups[k]]]
        picked = jnp.dot(pick, jnp.concatenate(rows, axis=0), preferred_element_type=F32)
        picked = picked.astype(BF)
        mine_ref[k * slots : (k + 1) * slots] = picked[:slots]
        other_ref[k * slots : (k + 1) * slots] = picked[slots:]


def select_rows(pieces, others, target, slots):
    width = pieces[0].shape[1]
    return pl.pallas_call(
        functools.partial(select_kernel, (len(pieces), len(others)), not others),
        out_shape=(jax.ShapeDtypeStruct((2 * slots, width), BF),) * 2,
        in_specs=[VMEM_SPEC] * (len(pieces) + len(others) + 1),
        out_specs=[VMEM_SPEC] * 2,
        compiler_params=pltpu.CompilerParams(vmem_limit_bytes=24 << 20),
        cost_estimate=COST,
    )(*pieces, *others, target)


def spread_kernel(chunks, part, *refs):
    mine_refs, other_refs = refs[:chunks], refs[chunks : 2 * chunks]
    target_ref, own_ref, x_ref, y_ref, diag_ref = refs[2 * chunks :]
    slots = mine_refs[0].shape[0] // 2
    rows = own_ref.shape[0] // chunks
    spot = slice(part * slots, (part + 1) * slots)
    for j in range(chunks):
        values = jnp.concatenate([mine_refs[j][spot], other_refs[j][spot]], axis=0)
        target = target_ref[j]
        index = lax.broadcasted_iota(jnp.int32, (4 * rows, 2 * slots), 1)
        pick = one_hot((index == target[:, 0:1]) | (index == target[:, 1:2]))
        spread = jnp.dot(pick, values, preferred_element_type=F32).astype(BF)
        for k, ref in enumerate((own_ref, x_ref, y_ref, diag_ref)):
            ref[j * rows : (j + 1) * rows] = spread[k * rows : (k + 1) * rows]


def spread_rows(mine, other, target, rows, part):
    chunks = len(mine)
    slots, width = mine[0].shape
    return pl.pallas_call(
        functools.partial(spread_kernel, chunks, part),
        out_shape=(jax.ShapeDtypeStruct((chunks * rows, width), BF),) * 4,
        in_specs=[VMEM_SPEC] * (2 * chunks + 1),
        out_specs=[VMEM_SPEC] * 4,
        compiler_params=pltpu.CompilerParams(
            vmem_limit_bytes=(16 << 20) if chunks == 1 else (36 << 20)
        ),
        cost_estimate=COST,
    )(*mine, *other, target)


def expert_kernel(expert_ref, mine_ref, other_ref, *refs):
    slots = mine_ref.shape[0] // 2
    rows, grads = slice(0, slots), slice(slots, 2 * slots)
    expert_body(
        expert_ref, mine_ref.at[rows], other_ref.at[rows], mine_ref.at[grads], other_ref.at[grads], *refs
    )


def expert_body(
    expert_ref,
    mine_ref,
    other_ref,
    grad_mine_ref,
    grad_other_ref,
    target_ref,
    route_ref,
    gate_ref,
    up_ref,
    down_ref,
    router_ref,
    back_mine_ref,
    back_other_ref,
    hidden_ref,
    gate_grad_ref,
    up_grad_ref,
    routed_ref,
    router_grad_ref,
):
    slots = mine_ref.shape[0]
    experts = router_ref.shape[0]
    tokens = target_ref.shape[1]
    rows = jnp.concatenate([mine_ref[...], other_ref[...]], axis=0)
    nt = (((1,), (1,)), ((), ()))
    tn = (((0,), (0,)), ((), ()))
    gate_pre = jnp.dot(rows, gate_ref[...], preferred_element_type=F32)
    up_pre = jnp.dot(rows, up_ref[...], preferred_element_type=F32)
    sigmoid = 1.0 / (1.0 + jnp.exp(-gate_pre))
    silu = gate_pre * sigmoid
    hidden = (silu * up_pre).astype(BF)
    hidden_ref[...] = hidden
    result = jnp.dot(hidden, down_ref[...], preferred_element_type=F32).astype(BF).astype(F32)
    slot_iota = lax.broadcasted_iota(jnp.int32, (slots, tokens), 0)
    expert_iota = lax.broadcasted_iota(jnp.int32, (experts, tokens), 0)
    masks = []
    for side in range(2):
        pick = one_hot(slot_iota == target_ref[side : side + 1, :])
        chosen = expert_iota == route_ref[side, 0:1, :]
        for k in range(1, route_ref.shape[1]):
            chosen = chosen | (expert_iota == route_ref[side, k : k + 1, :])
        masks.append(lax.dot_general(pick, one_hot(chosen), nt, preferred_element_type=F32))
    chosen = jnp.concatenate(masks, axis=0) > 0.5
    logits = lax.dot_general(rows, router_ref[...], nt, preferred_element_type=F32)
    top = jnp.max(jnp.where(chosen, logits, MASKED), axis=1, keepdims=True)
    weights = jnp.where(chosen, jnp.exp(logits - top), 0.0)
    total = jnp.sum(weights, axis=1, keepdims=True)
    gates = weights / jnp.where(total > 0.0, total, 1.0)
    mine = lax.broadcasted_iota(jnp.int32, gates.shape, 1) == expert_ref[0]
    gate = jnp.sum(jnp.where(mine, gates, 0.0), axis=1, keepdims=True)
    gated = (result * gate).astype(BF)
    back_mine_ref[slots:] = gated[:slots]
    back_other_ref[slots:] = gated[slots:]
    grad = jnp.concatenate([grad_mine_ref[...], grad_other_ref[...]], axis=0).astype(F32)
    gate_value_grad = jnp.sum(grad * result, axis=1, keepdims=True)
    routed = (grad * gate).astype(BF)
    routed_ref[...] = routed
    hidden_grad = lax.dot_general(routed, down_ref[...], nt, preferred_element_type=F32)
    gate_low = (hidden_grad * up_pre * sigmoid * (1.0 + gate_pre * (1.0 - sigmoid))).astype(BF)
    up_low = (hidden_grad * silu).astype(BF)
    gate_grad_ref[...] = gate_low
    up_grad_ref[...] = up_low
    logit_grad = (gate_value_grad * gate) * (jnp.where(mine, 1.0, 0.0) - gates)
    high = logit_grad.astype(BF)
    low = (logit_grad - high.astype(F32)).astype(BF)
    both = jnp.concatenate([high, low], axis=1)
    router = router_ref[...]
    slot_grad = lax.dot_general(gate_low, gate_ref[...], nt, preferred_element_type=F32)
    slot_grad = slot_grad + lax.dot_general(up_low, up_ref[...], nt, preferred_element_type=F32)
    slot_grad = slot_grad + jnp.dot(
        both, jnp.concatenate([router, router], axis=0), preferred_element_type=F32
    )
    slot_grad = slot_grad.astype(BF)
    back_mine_ref[:slots] = slot_grad[:slots]
    back_other_ref[:slots] = slot_grad[slots:]
    router_grad = lax.dot_general(both, rows, tn, preferred_element_type=F32)
    router_grad_ref[...] = router_grad[:experts] + router_grad[experts:]


def expert_rows(expert, mine, other, target, route, *weights):
    count, width = mine.shape
    ff = weights[0].shape[1]
    experts = weights[3].shape[0]
    low = lambda cols: jax.ShapeDtypeStruct((count, cols), BF)
    return pl.pallas_call(
        expert_kernel,
        out_shape=(
            low(width),
            low(width),
            low(ff),
            low(ff),
            low(ff),
            low(width),
            jax.ShapeDtypeStruct((experts, width), F32),
        ),
        in_specs=[SMEM_SPEC] + [VMEM_SPEC] * 8,
        out_specs=[VMEM_SPEC] * 7,
        compiler_params=pltpu.CompilerParams(vmem_limit_bytes=40 << 20),
        cost_estimate=COST,
    )(expert, mine, other, target, route, *weights)


def place_kernel(share, order_ref, owner_ref, part_ref, query_ref, key_ref, value_ref):
    cols = query_ref.shape[1]
    dim = key_ref.shape[1]
    part = part_ref[0]
    query_ref[...] = part[:, :cols].astype(F32)
    key = part[:, cols : cols + dim].astype(F32)
    value = part[:, cols + dim :].astype(F32)
    first = pl.program_id(0) % share == 0

    @pl.when(first)
    def _():
        key_ref[...] = key
        value_ref[...] = value

    @pl.when(jnp.logical_not(first))
    def _():
        key_ref[...] += key
        value_ref[...] += value


def place_weight_grads(parts, owner, share, dim):
    count, rows, width = parts.shape
    cols = width - 2 * dim
    if count == 8 and share == 2:
        order = jnp.asarray([0, 4, 1, 5, 2, 6, 3, 7], jnp.int32)
    else:
        order = jnp.arange(count, dtype=jnp.int32)
    owner = owner[order]
    group = lambda g, order, owner: (0, owner[g] // share)
    return pl.pallas_call(
        functools.partial(place_kernel, share),
        grid_spec=pltpu.PrefetchScalarGridSpec(
            num_scalar_prefetch=2,
            grid=(count,),
            in_specs=[pl.BlockSpec((1, rows, width), lambda g, order, owner: (order[g], 0, 0))],
            out_specs=[
                pl.BlockSpec((rows, cols), lambda g, order, owner: (0, owner[g])),
                pl.BlockSpec((rows, dim), group),
                pl.BlockSpec((rows, dim), group),
            ],
        ),
        out_shape=(
            jax.ShapeDtypeStruct((rows, cols * count), F32),
            jax.ShapeDtypeStruct((rows, dim * count // share), F32),
            jax.ShapeDtypeStruct((rows, dim * count // share), F32),
        ),
        compiler_params=pltpu.CompilerParams(vmem_limit_bytes=20 << 20),
        cost_estimate=COST,
    )(order, owner, parts)


def rows_kernel(owner_ref, part_ref, out_ref):
    out_ref[:, 0] = part_ref[0].astype(F32)


def place_rows(parts, owner):
    count, chunks, rows, width = parts.shape
    return pl.pallas_call(
        rows_kernel,
        grid_spec=pltpu.PrefetchScalarGridSpec(
            num_scalar_prefetch=1,
            grid=(count,),
            in_specs=[pl.BlockSpec((1, chunks, rows, width), lambda g, owner: (g, 0, 0, 0))],
            out_specs=pl.BlockSpec(
                (chunks, 1, rows, width), lambda g, owner: (0, owner[g], 0, 0)
            ),
        ),
        out_shape=jax.ShapeDtypeStruct((chunks, count, rows, width), F32),
        compiler_params=pltpu.CompilerParams(vmem_limit_bytes=20 << 20),
        cost_estimate=COST,
    )(owner, parts)


def move_slots(slot_array):
    return lax.all_to_all(slot_array, ("ctx", "wt"), split_axis=0, concat_axis=0, tiled=True)


def local(
    tokens,
    cotangent,
    segments,
    routes,
    pair_order,
    attn_gain,
    ffn_gain,
    query_gain,
    key_gain,
    w_query,
    key_weight,
    value_weight,
    w_output,
    w_router,
    w_gate,
    w_up,
    w_down,
):
    ctx_count = lax.axis_size("ctx")
    wt_count = lax.axis_size("wt")
    me = lax.axis_index("ctx")
    plane = lax.axis_index("wt")
    inputs = tokens[0].astype(F32)
    tok_rows, model_width = inputs.shape
    half_rows = tok_rows // 2
    head_dim = query_gain.shape[0]
    experts = w_router.shape[1]
    top_count = routes.shape[2]
    seq_len = segments.shape[1]
    total_tokens = tok_rows * ctx_count * wt_count
    heads = w_query.shape[1] // head_dim // ctx_count
    kv_heads = key_weight.shape[1] // head_dim
    share = ctx_count // kv_heads
    head_cols = heads * head_dim
    group = me // share
    shard_width = model_width // wt_count
    capacity = max(2, half_rows * top_count * 5 // (4 * experts))
    dense = ctx_count == 8 and w_gate.shape[0] == 1
    nt = (((1,), (1,)), ((), ()))
    tn = (((0,), (0,)), ((), ()))
    owners = block_owner(ctx_count, me)
    planes = (plane - jnp.arange(wt_count, dtype=jnp.int32)) % wt_count

    normed_one, attn_back = jax.vjp(rms_norm, inputs, attn_gain)
    normed_low = normed_one.astype(BF)
    kv_start = group * head_dim
    own_weight = jnp.concatenate(
        [
            lax.dynamic_slice_in_dim(w_query, me * head_cols, head_cols, 1),
            lax.dynamic_slice_in_dim(key_weight, kv_start, head_dim, 1),
            lax.dynamic_slice_in_dim(value_weight, kv_start, head_dim, 1),
        ],
        axis=1,
    )
    own_chunks = ctx_count // wt_count
    piece_rows = head_cols // ctx_count
    out_piece = lax.dynamic_index_in_dim(
        w_output.reshape(own_chunks, ctx_count, piece_rows, model_width), me, 1, keepdims=False
    )
    cot = cotangent[0]
    if dense:
        cap_rows = 2 * capacity
        slots = 4 * cap_rows
        expert = me * wt_count + plane
        triangle = jnp.triu(jnp.ones((tok_rows, tok_rows), F32)).astype(BF)
        offsets = (jnp.arange(ctx_count, dtype=jnp.int32) % 4) * cap_rows

        def tables(near):
            near = near.astype(jnp.int32).reshape(-1, ctx_count, top_count, tok_rows)

            def slot_of(routed_to):
                hits = jnp.any(near == routed_to, axis=2)
                ranks = jnp.dot(hits.astype(BF), triangle, preferred_element_type=F32)
                place = ranks.astype(jnp.int32) - 1 + offsets[None, :, None]
                return jnp.where(hits, place, -1).reshape(-1, 2, 4 * tok_rows)

            own_slot = slot_of(expert)
            other_slot = slot_of((me ^ 1) * wt_count + plane)[:, 0]
            target = jnp.stack(
                [own_slot[:, 0], jnp.where(other_slot < 0, -1, other_slot + slots)], axis=1
            )
            near_routes = (
                near.reshape(-1, 2, 4, top_count, tok_rows)
                .transpose(0, 1, 3, 2, 4)
                .reshape(-1, 2, top_count, 4 * tok_rows)
            )
            indices = jnp.arange(experts, dtype=jnp.int32)[:, None, None, None, None]
            counts = jnp.sum((near[None] == indices).astype(F32), axis=(1, 2, 3, 4))
            return own_slot, target, target.transpose(0, 2, 1), near_routes, counts

        near = routes[0].T.astype(BF)
        near_x, near_y = swap(near, 2), swap(near, 4)
        near = jnp.concatenate([near, near_x, near_y, swap(near_x, 4)], axis=0)
        near = jnp.concatenate([near, swap(near, 1)], axis=0)
        via_x, via_y = swap(normed_low, 2), swap(normed_low, 4)
        router_rows = w_router.T.reshape(-1, model_width)
        block_rows = own_chunks * piece_rows
        shard = jnp.concatenate([out_piece.reshape(block_rows, model_width), router_rows], axis=0)
        out_pieces = jnp.zeros((ctx_count * piece_rows, model_width), BF)
        router = jnp.zeros((wt_count,) + router_rows.shape, BF)
        weight = jnp.zeros((model_width, own_weight.shape[1]), BF)

        def keep(j, out_pieces, router, weight, shard, own_weight):
            put = lax.dynamic_update_slice_in_dim
            return (
                put(out_pieces, shard[:block_rows], planes[j] * block_rows, 0),
                put(router, shard[None, block_rows:], planes[j], 0),
                put(weight, own_weight, planes[j] * shard_width, 0),
            )

        ticks = [(shard, own_weight), (ring(shard), ring(own_weight))]
        diag_a, diag_b = swap(via_x[:half_rows], 4), swap(via_y[half_rows:], 2)
        hidden_pieces = [normed_low, via_x, via_y, diag_a, diag_b]
        hidden_pieces = hidden_pieces + [swap(piece, 1) for piece in hidden_pieces]
        ticks[1], near, cot_block = after((ticks[1], near, cot), ticks[1], hidden_pieces, near)
        nears = [near, ring(near)]
        cot_x, cot_y = swap(cot_block, 2), swap(cot_block, 4)
        ticks.append((ring(ticks[1][0]), ring(ticks[1][1])))
        first_tables = tables(near)
        ticks[2], cot_x, cot_y, nears[1] = after(
            (ticks[2], cot_x, cot_y, nears[1]), ticks[2], cot_x, cot_y, nears[1], first_tables
        )
        nears.append(ring(nears[1]))
        cot_sent = cot_x[:half_rows], cot_y[half_rows:]
        diag_a, diag_b = swap(cot_sent[0], 4), swap(cot_sent[1], 2)
        ticks.append((ring(ticks[2][0]), ring(ticks[2][1])))
        for j in range(wt_count - 1):
            out_pieces, router, weight = keep(j, out_pieces, router, weight, *ticks[j])
        cot_all = jnp.concatenate([cot, cot_x, cot_y, diag_a, diag_b], axis=0)
        ticks[3] = after(ticks[3], cot_all, nears[2], weight, out_pieces)
        out_pieces, router, weight = keep(3, out_pieces, router, weight, *ticks[3])
        router = router.reshape(wt_count, experts, shard_width).transpose(1, 0, 2)
        router = router.reshape(experts, model_width)
        nears.append(ring(after(nears[2], weight)))
        cots = [cot_all, ring(after(cot_all, weight))]
    else:
        hidden_pieces = plane_gather(normed_low)
        out_pieces = lax.all_gather(out_piece, "wt", axis=0, tiled=True)
        weight = lax.all_gather(own_weight, "wt", axis=0, tiled=True)
        router = lax.all_gather(w_router, "wt", axis=0, tiled=True).T
    out_weight = lax.all_to_all(
        out_pieces.reshape(ctx_count, piece_rows, model_width), "ctx", 0, 0, tiled=True
    ).reshape(head_cols, model_width)

    owner_pair = pair_order[owners]
    blocks = jnp.stack([owner_pair, 2 * ctx_count - 1 - owner_pair], 1).reshape(-1)
    order = jnp.arange(2 * ctx_count, dtype=jnp.int32)
    places = jnp.sum(jnp.where(blocks[:, None] == order[None, :], order[:, None], 0), axis=0)
    places = places.astype(jnp.int32)
    seg = segments[0]
    first = jnp.sum(
        (seg[None, :] < seg[::QUERY_ROWS][:, None]).astype(jnp.int32), axis=1
    ).astype(jnp.int32)
    seg_row, seg_col = seg.reshape(1, seq_len), seg.reshape(seq_len, 1)
    cosine, sine = rope_tables(seq_len, head_dim)
    query_gain_row, key_gain_row = query_gain.reshape(1, -1), key_gain.reshape(1, -1)

    width = head_cols + 2 * head_dim
    stacked = heads * QUERY_ROWS
    piece_count = len(hidden_pieces)
    query, key, value, raw, attn_low = pl.pallas_call(
        functools.partial(attend_kernel, heads, piece_count),
        out_shape=(
            jax.ShapeDtypeStruct((seq_len, head_cols), BF),
            jax.ShapeDtypeStruct((seq_len, head_dim), BF),
            jax.ShapeDtypeStruct((seq_len, head_dim), BF),
            jax.ShapeDtypeStruct((seq_len, head_cols + head_dim), F32),
            jax.ShapeDtypeStruct((2 * ctx_count, half_rows, head_cols), BF),
        ),
        in_specs=[SMEM_SPEC] * 3 + [VMEM_SPEC] * (7 + piece_count),
        out_specs=[VMEM_SPEC] * 5,
        scratch_shapes=[pltpu.VMEM((stacked, seq_len), F32)],
        compiler_params=pltpu.CompilerParams(vmem_limit_bytes=ATTEND_LIMIT),
        cost_estimate=COST,
    )(
        blocks,
        places,
        first,
        *hidden_pieces,
        weight,
        query_gain_row,
        key_gain_row,
        cosine,
        sine,
        seg_row,
        seg_col,
    )
    attn_rows = attn_low.reshape(seq_len, head_cols)
    later_tables = []

    def fill(sends):
        if dense:
            later_tables.extend(tables(after(jnp.concatenate(nears[1:], axis=0), sends)))
        return tuple(later_tables)

    residual = inputs + plane_scatter(
        lambda rows: low_matmul(rows, out_weight), attn_rows, fill
    )
    normed_two, ffn_back = jax.vjp(rms_norm, residual, ffn_gain)
    normed_two_low = normed_two.astype(BF)
    grad_out = cotangent[0].astype(F32)
    if dense:
        own_slot, target_rows, target_cols, near_routes = (
            jnp.concatenate([f, r], axis=0) for f, r in zip(first_tables[:4], later_tables[:4])
        )
        counts = first_tables[4] + later_tables[4]
        logits = lax.dot_general(normed_two_low, router, nt, preferred_element_type=F32)
        router_probs = jax.nn.softmax(logits, axis=-1)
        shares = counts / (total_tokens * top_count)
        prob_grad = (experts * shares / total_tokens)[None, :]
        logits_grad = router_probs * (
            prob_grad - jnp.sum(router_probs * prob_grad, axis=1, keepdims=True)
        )
        logits_grad_low = logits_grad.astype(BF)
        last = wt_count - 1
        mine_backs, other_backs, results = [], [], []

        def compute(j, pieces, others, gates):
            pieces = after(pieces, *gates)
            mine, other = select_rows(pieces, others, target_rows[j], slots)
            received = swap(other, 1)
            result = expert_rows(
                expert.reshape(1),
                mine,
                received,
                own_slot[j],
                near_routes[j],
                w_gate[0],
                w_up[0],
                w_down[0],
                router,
            )
            mine_backs.append(result[0])
            other_backs.append(swap(result[1], 1))
            results.append((mine[:slots], received[:slots]) + tuple(result[2:]))
            return result[0]

        chunk, pieces, done = normed_two_low, None, None
        for j in range(wt_count):
            if j > 0:
                chunk = ring(chunk)
            payload = chunk
            if j == last:
                cot_last = ring(cots[j - 1][:tok_rows])
                halves = chunk[:half_rows], cot_last[:half_rows], chunk[half_rows:], cot_last[half_rows:]
                payload = jnp.concatenate(halves, axis=0)
            elif j > 1:
                cots.append(ring(cots[-1]))
            if j > 0:
                payload = after(payload, sent)
            via_x, via_y = swap(payload, 2), swap(payload, 4)
            if done is not None:
                via_x, via_y = after((via_x, via_y), done)
            middle = via_x.shape[0] // 2
            sent = via_x[:middle], via_y[middle:]
            before, pieces = pieces, [payload, via_x, via_y, swap(sent[0], 4), swap(sent[1], 2)]
            if before is not None:
                done = compute(j - 1, before, [cots[j - 1]], (sent,))
        parts = spread_rows(mine_backs, other_backs, target_cols[:last], tok_rows, 0)
        half = parts[3].shape[0] // 2
        group_sent = parts[3][:half], parts[3][half:]
        group_diag = swap(group_sent[0], 4), swap(group_sent[1], 2)
        done = compute(last, pieces, [], (group_sent,))
        group_x, group_y = add_diag(*after((parts[1], parts[2]), done), *after(group_diag, done))
        got_x, got_y = swap(group_x, 2), swap(group_y, 4)
        tail = spread_rows(
            mine_backs[last:], other_backs[last:], after(target_cols[last:], group_x, group_y), tok_rows, 0
        )
        tail_sent = tail[3][:half_rows], tail[3][half_rows:]
        tail_diag = swap(tail_sent[0], 4), swap(tail_sent[1], 2)
        rows_all = jnp.concatenate([r for res in results for r in res[:2]], axis=0)
        hidden_low, gate_low, up_low, routed = (
            jnp.concatenate([res[k] for res in results], axis=0) for k in range(2, 6)
        )
        rows_all = after(rows_all, tail_sent)
        grad_w_gate = lax.dot_general(rows_all, gate_low, tn, preferred_element_type=F32)[None]
        tail_x, tail_y = add_diag(
            *after((tail[1], tail[2]), grad_w_gate), *after(tail_diag, grad_w_gate)
        )
        tail_got = swap(tail_x, 2), swap(tail_y, 4)
        rows_all = after(rows_all, tail_x, tail_y)
        grad_w_up = lax.dot_general(rows_all, up_low, tn, preferred_element_type=F32)[None]
        hidden_low = after(hidden_low, grad_w_up)
        grad_w_down = lax.dot_general(hidden_low, routed, tn, preferred_element_type=F32)[None]
        got_x, got_y = after((got_x, got_y), grad_w_down)
        sums = parts[0].astype(F32) + got_x.astype(F32) + got_y.astype(F32)
        sums = sums.reshape(last, tok_rows, model_width)
        total = sums[1].astype(BF)
        backs = after(mine_backs[0], total)
        total = ring(total)
        parts = spread_rows([backs] + mine_backs[1:], other_backs, target_cols, tok_rows, 1)
        total = after(total, parts)
        tail_got = after(tail_got, parts)
        for j in range(2, last):
            total = ring((total.astype(F32) + sums[j]).astype(BF)).astype(F32)
        tail_sum = tail[0].astype(F32) + tail_got[0].astype(F32) + tail_got[1].astype(F32)
        total = ring((total.astype(F32) + tail_sum).astype(BF)).astype(F32) + sums[0]
        grad_normed_two = total + jnp.dot(logits_grad_low, router, preferred_element_type=F32)
        router_grad = sum(res[6] for res in results) + lax.dot_general(
            logits_grad_low, normed_two_low, tn, preferred_element_type=F32
        )
    else:
        w_router_all = router.T
        slot_rows = 2 * capacity
        local_experts = w_gate.shape[0]
        logits = low_matmul(normed_two_low, w_router_all)
        local_routes = routes[0]

        def router_fn(logit_values):
            router_probs = jax.nn.softmax(logit_values, axis=-1)
            chosen = jnp.take_along_axis(router_probs, local_routes, axis=1)
            return (chosen / jnp.sum(chosen, axis=1, keepdims=True), router_probs)

        (gate_values, router_probs), router_back = jax.vjp(router_fn, logits)
        route_flat = local_routes.reshape(-1)
        route_hits = (route_flat[:, None] == jnp.arange(experts, dtype=jnp.int32)[None, :]).astype(
            jnp.int32
        )
        counts = lax.psum(jnp.sum(route_hits, axis=0).astype(jnp.float32), ("ctx", "wt"))
        shares = counts / (total_tokens * top_count)
        halves = route_hits.reshape(2, half_rows * top_count, experts)
        ranks = jnp.sum((jnp.cumsum(halves, axis=1) - halves) * halves, axis=2).reshape(-1)
        half_index = jnp.arange(tok_rows * top_count, dtype=jnp.int32) // (half_rows * top_count)
        slot_index = route_flat * slot_rows + half_index * capacity + ranks
        slot_owner = (
            jnp.full((experts * slot_rows,), tok_rows * top_count, jnp.int32)
            .at[slot_index]
            .set(jnp.arange(tok_rows * top_count, dtype=jnp.int32))
        )
        slot_shape = (experts // local_experts, local_experts, slot_rows, model_width)
        padded = jnp.concatenate([normed_two_low, jnp.zeros((1, model_width), jnp.bfloat16)], axis=0)
        outgoing = padded[slot_owner // top_count].reshape(slot_shape)
        arrived = move_slots(outgoing)
        gate_pre = jnp.einsum("nesd,edf->nesf", arrived, w_gate, preferred_element_type=jnp.float32)
        up_pre = jnp.einsum("nesd,edf->nesf", arrived, w_up, preferred_element_type=jnp.float32)
        hidden_low, swiglu_back = jax.vjp(swiglu, gate_pre, up_pre)
        hidden_low = hidden_low.astype(jnp.bfloat16)
        expert_out = jnp.einsum(
            "nesf,efd->nesd", hidden_low, w_down, preferred_element_type=jnp.float32
        ).astype(jnp.bfloat16)
        returned = move_slots(expert_out).reshape(experts * slot_rows, model_width)
        picked = returned[slot_index].reshape(tok_rows, top_count, model_width)
        mixture = jnp.einsum("tk,tkd->td", gate_values, picked, preferred_element_type=jnp.float32)
        output = (residual + mixture).astype(jnp.bfloat16)
        grad_gates = jnp.einsum("td,tkd->tk", grad_out, picked, preferred_element_type=jnp.float32)
        grad_routed = (
            (gate_values[:, :, None] * grad_out[:, None, :])
            .astype(jnp.bfloat16)
            .reshape(-1, model_width)
        )
        grad_routed = jnp.concatenate([grad_routed, jnp.zeros((1, model_width), jnp.bfloat16)], axis=0)
        grad_arrived = move_slots(grad_routed[slot_owner].reshape(slot_shape))
        grad_hidden = jnp.einsum(
            "nesd,efd->nesf", grad_arrived, w_down, preferred_element_type=jnp.float32
        )
        grad_w_down = jnp.einsum(
            "nesf,nesd->efd", hidden_low, grad_arrived, preferred_element_type=jnp.float32
        )
        grad_gate_pre, grad_up_pre = swiglu_back(grad_hidden)
        gate_grad_low = grad_gate_pre.astype(jnp.bfloat16)
        up_grad_low = grad_up_pre.astype(jnp.bfloat16)
        grad_w_gate = jnp.einsum(
            "nesd,nesf->edf", arrived, gate_grad_low, preferred_element_type=jnp.float32
        )
        grad_w_up = jnp.einsum(
            "nesd,nesf->edf", arrived, up_grad_low, preferred_element_type=jnp.float32
        )
        grad_slots = (
            jnp.einsum("nesf,edf->nesd", gate_grad_low, w_gate, preferred_element_type=jnp.float32)
            + jnp.einsum("nesf,edf->nesd", up_grad_low, w_up, preferred_element_type=jnp.float32)
        ).astype(jnp.bfloat16)
        grad_back = move_slots(grad_slots).reshape(experts * slot_rows, model_width)
        grad_normed_two = jnp.sum(
            grad_back[slot_index].reshape(tok_rows, top_count, model_width).astype(jnp.float32), axis=1
        )
        prob_grad = jnp.broadcast_to(experts * shares / total_tokens, router_probs.shape)
        (grad_logits,) = router_back((grad_gates, prob_grad))
        logits_low = grad_logits.astype(jnp.bfloat16)
        grad_normed_two = grad_normed_two + jnp.einsum(
            "te,de->td", logits_low, w_router_all, preferred_element_type=jnp.float32
        )
        grad_w_router = jnp.einsum(
            "td,te->de", normed_two_low, logits_low, preferred_element_type=jnp.float32
        )
        router_grad = grad_w_router.T
    grad_residual_part, grad_ffn_gain = ffn_back(grad_normed_two)
    grad_residual = grad_out + grad_residual_part
    grad_pieces = plane_gather(grad_residual.astype(BF))
    out_grad = lax.dot_general(
        attn_rows, jnp.concatenate(grad_pieces, axis=0), tn, preferred_element_type=F32
    ).astype(BF)
    if dense:
        half = parts[3].shape[0] // 2
        out_sent = after((parts[3][:half], parts[3][half:]), grad_pieces)
        out_diag = swap(out_sent[0], 4), swap(out_sent[1], 2)
        query = after(query, out_sent, out_grad)
    out_grad = lax.all_to_all(
        out_grad.reshape(ctx_count, piece_rows, model_width), "ctx", 0, 0, tiled=True
    )
    head_grads, grad_query_gain, grad_key_gain = pl.pallas_call(
        functools.partial(attend_back_kernel, heads, piece_count),
        out_shape=(
            jax.ShapeDtypeStruct((2 * ctx_count, half_rows, width), BF),
            jax.ShapeDtypeStruct((1, head_dim), F32),
            jax.ShapeDtypeStruct((1, head_dim), F32),
        ),
        in_specs=[SMEM_SPEC] * 2 + [VMEM_SPEC] * (11 + piece_count),
        out_specs=[VMEM_SPEC] * 3,
        scratch_shapes=[
            pltpu.VMEM((stacked, seq_len), F32),
            pltpu.VMEM((stacked, seq_len), F32),
            pltpu.VMEM((seq_len, head_dim), F32),
            pltpu.VMEM((seq_len, head_dim), F32),
            pltpu.VMEM((2 * ctx_count, half_rows, head_cols), BF),
        ],
        compiler_params=pltpu.CompilerParams(vmem_limit_bytes=ATTEND_LIMIT),
        cost_estimate=COST,
    )(
        places,
        first,
        *grad_pieces,
        out_weight,
        query,
        key,
        value,
        raw,
        query_gain_row,
        key_gain_row,
        cosine,
        sine,
        seg_row,
        seg_col,
    )
    head_grads = head_grads.reshape(seq_len, width)
    hidden_rows = jnp.concatenate(hidden_pieces, axis=0)
    last_gates = ()
    if dense:
        def weight_part(j, grads):
            cols = lax.dynamic_slice_in_dim(hidden_rows, planes[j] * shard_width, shard_width, 1)
            return lax.dot_general(cols, grads, tn, preferred_element_type=F32)

        part = weight_part(1, head_grads).astype(BF)
        total = ring(part)
        out_x, out_y = add_diag(*after((parts[1], parts[2]), part), *after(out_diag, part))
        got_x, got_y = swap(out_x, 2), swap(out_y, 4)
        head_grads = after(head_grads, out_x, out_y)
        part = weight_part(2, head_grads)
        more = [weight_part(j, after(head_grads, part)) for j in (3, 0)]
        total = after(total, more).astype(F32) + part
        total_low = total.astype(BF)
        total = ring(total_low)
        head_grads = after(head_grads, total_low, out_grad)
        total = total.astype(F32) + more[0]
        total_low = total.astype(BF)
        total = ring(total_low)
        got_x, got_y = after((got_x, got_y), total_low)
        out_parts = parts[0].astype(F32) + got_x.astype(F32) + got_y.astype(F32)
        out_parts = out_parts.reshape(wt_count, tok_rows, model_width)
        weight_grad = (total.astype(F32) + more[1]).astype(BF)
        out_parts = after([out_parts[j] for j in range(wt_count)], weight_grad)
        output = (residual + ring_sum(out_parts, BF)).astype(BF)
        out_grad = after(out_grad, weight_grad)
        last_gates = (got_x, got_y)
    else:
        weight_grad = lax.dot_general(hidden_rows, head_grads, tn, preferred_element_type=F32)
        weight_grad = lax.psum_scatter(
            weight_grad.astype(BF), "wt", scatter_dimension=0, tiled=True
        )
    weight_grads = jnp.concatenate(plane_gather(weight_grad), axis=0)
    grad_w_query, grad_w_key, grad_w_value = place_weight_grads(
        weight_grads.reshape(ctx_count, -1, width), owners, share, head_dim
    )
    if dense:
        parts = out_grad.reshape(wt_count, own_chunks * piece_rows, model_width)[planes]
        out_grad = ring_sum([parts[j] for j in range(wt_count)], BF).astype(BF)
    else:
        out_grad = lax.psum_scatter(out_grad, "wt", scatter_dimension=0, tiled=True)
    out_grads = jnp.concatenate(plane_gather(out_grad.reshape(-1, model_width)), axis=0)
    grad_w_output = place_rows(
        out_grads.reshape(ctx_count, own_chunks, piece_rows, model_width), owners
    ).reshape(w_output.shape)
    grad_normed_one = plane_scatter(
        lambda rows: lax.dot_general(rows, weight, nt, preferred_element_type=F32),
        head_grads,
        None,
        *last_gates,
    )
    grad_inputs_part, grad_attn_gain = attn_back(grad_normed_one)
    grad_inputs = grad_residual + grad_inputs_part

    part = head_dim // wt_count
    prob_sums = jnp.sum(router_probs, axis=0)
    prob_row = jnp.zeros((shard_width - 2 * part,), F32)
    if dense:
        prob_row = lax.dynamic_update_slice_in_dim(prob_row, prob_sums, plane * experts, 0)
    gains = jnp.concatenate(
        [
            grad_query_gain.reshape(wt_count, part),
            grad_key_gain.reshape(wt_count, part),
            jnp.broadcast_to(prob_row[None], (wt_count, shard_width - 2 * part)),
        ],
        axis=1,
    )
    small = jnp.concatenate([router_grad, grad_ffn_gain[None], grad_attn_gain[None]], axis=0)
    small = small.reshape(experts + 2, wt_count, shard_width).transpose(1, 0, 2)
    small = jnp.concatenate([small, gains[:, None]], axis=1)[planes]
    small = ring_sum([small[j] for j in range(wt_count)], F32)
    small = axis_sum(small, "ctx")
    if dense:
        prob_sums = small[experts + 2, 2 * part : 2 * part + wt_count * experts]
        prob_sums = jnp.sum(prob_sums.reshape(wt_count, experts), axis=0)
    else:
        prob_sums = axis_sum(axis_sum(prob_sums[None], "ctx"), "wt")[0]
    balance = experts * experts * shares * (prob_sums / total_tokens)
    loss_value = jnp.mean(balance)
    return (
        output[None],
        loss_value,
        balance,
        grad_inputs[None],
        small[experts + 1],
        small[experts],
        small[experts + 2, :part],
        small[experts + 2, part : 2 * part],
        grad_w_query,
        grad_w_key,
        grad_w_value,
        grad_w_output,
        small[:experts].T,
        grad_w_gate,
        grad_w_up,
        grad_w_down,
    )


def solution(mesh):
    in_specs = (
        P("wt", "ctx", None),
        P("wt", "ctx", None),
        P("wt", None),
        P("wt", "ctx", None),
        P(),
        P(),
        P(),
        P(),
        P(),
        P("wt", None),
        P("wt", None),
        P("wt", None),
        P("wt", None),
        P("wt", None),
        P(("ctx", "wt"), None, None),
        P(("ctx", "wt"), None, None),
        P(("ctx", "wt"), None, None),
    )
    out_specs = (
        P("wt", "ctx", None),
        P(),
        P(),
        P("wt", "ctx", None),
        P("wt"),
        P("wt"),
        P("wt"),
        P("wt"),
        P("wt", None),
        P("wt", None),
        P("wt", None),
        P("wt", None),
        P("wt", None),
        P(("ctx", "wt"), None, None),
        P(("ctx", "wt"), None, None),
        P(("ctx", "wt"), None, None),
    )
    return jax.shard_map(local, mesh=mesh, in_specs=in_specs, out_specs=out_specs, check_vma=False)
```

```python
import functools

import jax
import jax.numpy as jnp
from jax import lax
from jax.experimental import pallas as pl
from jax.experimental.pallas import tpu as pltpu
from jax.sharding import PartitionSpec as P

EPSILON = 1e-06
ROPE_BASE = 1000000.0
MASKED = -1e30
BF = jnp.bfloat16
F32 = jnp.float32
VMEM_SPEC = pl.BlockSpec(memory_space=pltpu.VMEM)
SMEM_SPEC = pl.BlockSpec(memory_space=pltpu.SMEM)
QUERY_ROWS = 128
KEY_ROWS = 256
ATTEND_LIMIT = 60 << 20
COST = pl.CostEstimate(flops=1, bytes_accessed=1, transcendentals=0)


def rms_norm(value_vectors, gain_vector):
    return (
        value_vectors
        * lax.rsqrt(jnp.mean(value_vectors * value_vectors, axis=-1, keepdims=True) + EPSILON)
        * gain_vector
    )


def low_matmul(left, right):
    return jnp.dot(left, right, preferred_element_type=F32)


def swiglu(gate_pre, up_pre):
    return jax.nn.silu(gate_pre) * up_pre


def rope_tables(length, head_width, zero):
    inv_freq = ROPE_BASE ** (-jnp.arange(0, head_width // 2, dtype=F32) * 2.0 / head_width)
    angle_table = (jnp.arange(length, dtype=F32) + zero)[:, None] * inv_freq[None, :]
    cosine, sine = jnp.cos(angle_table), jnp.sin(angle_table)
    return jnp.concatenate([cosine, cosine], 1), jnp.concatenate([-sine, sine], 1)


RELATIVE = (0, 2, 4, 6, 1, 3, 5, 7)


def swap(value, bit):
    count = lax.axis_size("ctx")
    return lax.ppermute(value, "ctx", [(i, i ^ bit) for i in range(count)])


def block_owner(count, me):
    if count == 8:
        return jnp.asarray(RELATIVE, jnp.int32) ^ me
    return jnp.arange(count, dtype=jnp.int32)


def after(value, *others):
    return lax.optimization_barrier((value,) + others)[0]


def plane_pieces(block):
    half = block.shape[0] // 2
    via_x = swap(block, 2)
    via_y = swap(block, 4)
    return [block, via_x, via_y, swap(via_x[:half], 4), swap(via_y[half:], 2)]


def plane_sends(block):
    half = block.shape[0] // 2
    via_x = swap(block, 2)
    via_y = swap(block, 4)
    from_x, from_y = via_x[:half], via_y[half:]
    return [block, via_x, via_y, swap(from_x, 4), swap(from_y, 2)], (from_x, from_y)


def plane_gather(block):
    count = lax.axis_size("ctx")
    if count != 8:
        return [lax.all_gather(block, "ctx", axis=0, tiled=True)]
    mine = plane_pieces(block)
    return mine + [swap(piece, 1) for piece in mine]


def sum_kernel(*refs):
    total = refs[0][...].astype(F32)
    for ref in refs[1:-1]:
        total = total + ref[...].astype(F32)
    refs[-1][...] = total.astype(refs[-1].dtype)


def sum_of(values, kind, limit=24):
    return pl.pallas_call(
        sum_kernel,
        out_shape=jax.ShapeDtypeStruct(values[0].shape, kind),
        in_specs=[VMEM_SPEC] * len(values),
        out_specs=VMEM_SPEC,
        compiler_params=pltpu.CompilerParams(vmem_limit_bytes=limit << 20),
        cost_estimate=COST,
    )(*values)


def add_diag_kernel(part_x_ref, part_y_ref, from_y_ref, from_x_ref, out_x_ref, out_y_ref):
    half = from_y_ref.shape[0]
    low = lambda a, b: (a.astype(F32) + b.astype(F32)).astype(BF)
    out_x_ref[:half] = low(part_x_ref[:half], from_y_ref[...])
    out_x_ref[half:] = part_x_ref[half:].astype(BF)
    out_y_ref[:half] = part_y_ref[:half].astype(BF)
    out_y_ref[half:] = low(part_y_ref[half:], from_x_ref[...])


def add_diag(part_x, part_y, from_y, from_x):
    return pl.pallas_call(
        add_diag_kernel,
        out_shape=(jax.ShapeDtypeStruct(part_x.shape, BF),) * 2,
        in_specs=[VMEM_SPEC] * 4,
        out_specs=[VMEM_SPEC] * 2,
        compiler_params=pltpu.CompilerParams(vmem_limit_bytes=24 << 20),
        cost_estimate=COST,
    )(part_x, part_y, from_y, from_x)


def plane_scatter(multiply, left, fill=None, others=(), last=()):
    count = lax.axis_size("ctx")
    if count != 8:
        parts = multiply(left, BF)
        return lax.psum_scatter(parts, "ctx", scatter_dimension=0, tiled=True).astype(F32)
    side = left.shape[0] // 2
    rows = side // 4
    half = rows // 2
    give = multiply(left[side:], BF)
    got = swap(give, 1)
    keep = multiply(after(left[:side], give), BF)
    kept = sum_of(after([keep, got], others), BF)
    sends = kept[3 * rows : -half], kept[-half:]
    from_y, from_x = swap(sends[0], 4), swap(sends[1], 2)
    from_y, from_x = after((from_y, from_x), fill(sends))
    part_x, part_y = add_diag(kept[rows : 2 * rows], kept[2 * rows : 3 * rows], from_y, from_x)
    got = after((swap(part_x, 2), swap(part_y, 4)), last)
    return kept[:rows].astype(F32) + got[0].astype(F32) + got[1].astype(F32)


class Order:
    def __init__(self, *values):
        self.last = values

    def take(self, value):
        return after(value, *self.last)

    def give(self, *values):
        self.last = values


def ring(value):
    count = lax.axis_size("wt")
    return lax.ppermute(value, "wt", [(i, (i + 1) % count) for i in range(count)])


def ring_chunks(block):
    chunks = [block]
    for _ in range(lax.axis_size("wt") - 1):
        chunks.append(ring(chunks[-1]))
    return chunks


def ring_sum(parts, kind):
    total = parts[1]
    for part in parts[2:] + parts[:1]:
        total = ring(total.astype(kind)).astype(F32) + part
    return total


def axis_sum(value, name):
    count = lax.axis_size(name)
    bit = 1
    while bit < count:
        value = value + lax.ppermute(value, name, [(i, i ^ bit) for i in range(count)])
        bit *= 2
    return value


def head_norm(raw, gain):
    scale = lax.rsqrt(jnp.mean(raw * raw, axis=-1, keepdims=True) + EPSILON)
    return raw * scale * gain


def turn(value):
    return pltpu.roll(value, value.shape[-1] // 2, 1)


def tile_mask(seg_col, seg_row, row_start, col_start):
    shape = (seg_col.shape[0], seg_row.shape[1])
    rows = lax.broadcasted_iota(jnp.int32, shape, 0) + row_start
    cols = lax.broadcasted_iota(jnp.int32, shape, 1) + col_start
    return (seg_col == seg_row) & (cols <= rows)


def attend_kernel(
    heads,
    pieces,
    block_ref,
    place_ref,
    first_ref,
    *refs,
):
    attend_body(heads, block_ref, place_ref, first_ref, refs[:pieces], *refs[pieces:])


def joined(refs, rows):
    group, have = [], 0
    for ref in refs:
        for start in range(0, ref.shape[0], rows):
            stop = min(start + rows, ref.shape[0])
            group.append(ref[start:stop])
            have += stop - start
            if have == rows:
                yield group[0] if len(group) == 1 else jnp.concatenate(group, axis=0)
                group, have = [], 0


def attend_body(
    heads,
    block_ref,
    place_ref,
    first_ref,
    hidden_refs,
    weight_ref,
    query_gain_ref,
    key_gain_ref,
    cosine_ref,
    sine_ref,
    seg_row_ref,
    seg_col_ref,
    query_ref,
    key_ref,
    value_ref,
    raw_ref,
    out_ref,
    score_ref,
):
    half = out_ref.shape[1]
    dim = query_gain_ref.shape[1]
    scale = dim ** (-0.5)

    for pair, lhs in enumerate(joined(hidden_refs, 4 * half)):
        raw = jnp.dot(lhs, weight_ref[...], preferred_element_type=F32)
        for piece in range(4):
            start = pl.multiple_of(block_ref[pair * 4 + piece] * half, half)
            spot = pl.ds(start, half)
            cosine, sine = cosine_ref[spot, :], sine_ref[spot, :]
            part = raw[piece * half : (piece + 1) * half]
            for head in range(heads + 1):
                cols = slice(head * dim, (head + 1) * dim)
                gain = query_gain_ref[...] if head < heads else key_gain_ref[...]
                normed = head_norm(part[:, cols], gain)
                roped = (normed * cosine + turn(normed) * sine).astype(BF)
                if head < heads:
                    query_ref[spot, cols] = roped
                else:
                    key_ref[spot, :] = roped
            raw_ref[spot, :] = part[:, : (heads + 1) * dim]
            value_ref[spot, :] = part[:, (heads + 1) * dim :].astype(BF)

    seq = key_ref.shape[0]
    stacked = heads * QUERY_ROWS

    def attend(index, carry):
        row_start = pl.multiple_of(index * QUERY_ROWS, QUERY_ROWS)
        row_spot = pl.ds(row_start, QUERY_ROWS)
        query = jnp.concatenate(
            [query_ref[row_spot, h * dim : (h + 1) * dim] for h in range(heads)], axis=0
        )
        seg_col = seg_col_ref[row_spot, :]
        low = first_ref[index] // KEY_ROWS
        high = (row_start + QUERY_ROWS + KEY_ROWS - 1) // KEY_ROWS

        def scores(tile, top):
            start = pl.multiple_of(tile * KEY_ROWS, KEY_ROWS)
            spot = pl.ds(start, KEY_ROWS)
            raw = lax.dot_general(
                query, key_ref[spot, :], (((1,), (1,)), ((), ())), preferred_element_type=F32
            )
            allowed = tile_mask(seg_col, seg_row_ref[:, spot], row_start, start)
            raw = raw.reshape(heads, QUERY_ROWS, KEY_ROWS) * scale
            masked = jnp.where(allowed[None], raw, MASKED).reshape(stacked, KEY_ROWS)
            score_ref[:, spot] = masked
            return jnp.maximum(top, jnp.max(masked, axis=1, keepdims=True))

        top = lax.fori_loop(low, high, scores, jnp.full((stacked, 1), MASKED, F32))

        def gather(tile, state):
            total, acc = state
            start = pl.multiple_of(tile * KEY_ROWS, KEY_ROWS)
            spot = pl.ds(start, KEY_ROWS)
            probs = jnp.exp(score_ref[:, spot] - top)
            total = total + jnp.sum(probs, axis=1, keepdims=True)
            acc = acc + jnp.dot(
                probs.astype(BF), value_ref[spot, :], preferred_element_type=F32
            )
            return total, acc

        total, acc = lax.fori_loop(
            low, high, gather, (jnp.zeros((stacked, 1), F32), jnp.zeros((stacked, dim), F32))
        )
        result = (acc / total).astype(BF)
        for head in range(heads):
            for piece in range(QUERY_ROWS // half):
                spot = place_ref[index * (QUERY_ROWS // half) + piece]
                begin = head * QUERY_ROWS + piece * half
                out_ref[spot, :, head * dim : (head + 1) * dim] = result[begin : begin + half]
        return carry

    lax.fori_loop(0, seq // QUERY_ROWS, attend, 0)


def attend_back_kernel(heads, pieces, place_ref, first_ref, *refs):
    attend_back_body(heads, place_ref, first_ref, refs[:pieces], *refs[pieces:])


def attend_back_body(
    heads,
    place_ref,
    first_ref,
    piece_refs,
    out_weight_ref,
    query_ref,
    key_ref,
    value_ref,
    raw_ref,
    query_gain_ref,
    key_gain_ref,
    cosine_ref,
    sine_ref,
    seg_row_ref,
    seg_col_ref,
    out_ref,
    query_gain_grad_ref,
    key_gain_grad_ref,
    score_ref,
    prob_grad_ref,
    key_grad_ref,
    value_grad_ref,
    grad_ref,
):
    half = grad_ref.shape[1]
    spot = 0
    for part in joined(piece_refs, 4 * half):
        part = lax.dot_general(
            part, out_weight_ref[...], (((1,), (1,)), ((), ())), preferred_element_type=F32
        ).astype(BF)
        for piece in range(4):
            grad_ref[spot] = part[piece * half : (piece + 1) * half]
            spot += 1
    dim = query_gain_ref.shape[1]
    scale = dim ** (-0.5)
    seq = key_ref.shape[0]
    stacked = heads * QUERY_ROWS
    pieces = QUERY_ROWS // half
    key_grad_ref[...] = jnp.zeros_like(key_grad_ref)
    value_grad_ref[...] = jnp.zeros_like(value_grad_ref)
    query_gain_grad_ref[...] = jnp.zeros_like(query_gain_grad_ref)
    key_gain_grad_ref[...] = jnp.zeros_like(key_gain_grad_ref)

    def unrope(grad, raw, gain, cosine, sine):
        norm_scale = lax.rsqrt(jnp.mean(raw * raw, axis=-1, keepdims=True) + EPSILON)
        unit = raw * norm_scale
        grad = grad * cosine + turn(grad * sine)
        gain_grad = jnp.sum(grad * unit, axis=0, keepdims=True)
        grad = grad * gain
        grad = norm_scale * (grad - unit * jnp.mean(grad * unit, axis=-1, keepdims=True))
        return grad, gain_grad

    def back(index, carry):
        row_start = pl.multiple_of(index * QUERY_ROWS, QUERY_ROWS)
        row_spot = pl.ds(row_start, QUERY_ROWS)
        places = [place_ref[index * pieces + piece] for piece in range(pieces)]
        query = jnp.concatenate(
            [query_ref[row_spot, h * dim : (h + 1) * dim] for h in range(heads)], axis=0
        )
        grad = jnp.concatenate(
            [
                grad_ref[place, :, h * dim : (h + 1) * dim]
                for h in range(heads)
                for place in places
            ],
            axis=0,
        )
        seg_col = seg_col_ref[row_spot, :]
        low = first_ref[index] // KEY_ROWS
        high = (row_start + QUERY_ROWS + KEY_ROWS - 1) // KEY_ROWS

        def scores(tile, top):
            start = pl.multiple_of(tile * KEY_ROWS, KEY_ROWS)
            spot = pl.ds(start, KEY_ROWS)
            raw = lax.dot_general(
                query, key_ref[spot, :], (((1,), (1,)), ((), ())), preferred_element_type=F32
            )
            allowed = tile_mask(seg_col, seg_row_ref[:, spot], row_start, start)
            raw = raw.reshape(heads, QUERY_ROWS, KEY_ROWS) * scale
            masked = jnp.where(allowed[None], raw, MASKED).reshape(stacked, KEY_ROWS)
            score_ref[:, spot] = masked
            return jnp.maximum(top, jnp.max(masked, axis=1, keepdims=True))

        top = lax.fori_loop(low, high, scores, jnp.full((stacked, 1), MASKED, F32))

        def probabilities(tile, state):
            total, inner = state
            start = pl.multiple_of(tile * KEY_ROWS, KEY_ROWS)
            spot = pl.ds(start, KEY_ROWS)
            probs = jnp.exp(score_ref[:, spot] - top)
            prob_grad = lax.dot_general(
                grad, value_ref[spot, :], (((1,), (1,)), ((), ())), preferred_element_type=F32
            )
            score_ref[:, spot] = probs
            prob_grad_ref[:, spot] = prob_grad
            total = total + jnp.sum(probs, axis=1, keepdims=True)
            inner = inner + jnp.sum(probs * prob_grad, axis=1, keepdims=True)
            return total, inner

        zero = jnp.zeros((stacked, 1), F32)
        total, inner = lax.fori_loop(low, high, probabilities, (zero, zero))
        share = 1.0 / total
        inner = inner * share

        def gradients(tile, acc):
            start = pl.multiple_of(tile * KEY_ROWS, KEY_ROWS)
            spot = pl.ds(start, KEY_ROWS)
            probs = score_ref[:, spot] * share
            score_grad = (probs * (prob_grad_ref[:, spot] - inner) * scale).astype(BF)
            acc = acc + jnp.dot(score_grad, key_ref[spot, :], preferred_element_type=F32)
            key_grad_ref[spot, :] += lax.dot_general(
                score_grad, query, (((0,), (0,)), ((), ())), preferred_element_type=F32
            )
            value_grad_ref[spot, :] += lax.dot_general(
                probs.astype(BF), grad, (((0,), (0,)), ((), ())), preferred_element_type=F32
            )
            return acc

        acc = lax.fori_loop(low, high, gradients, jnp.zeros((stacked, dim), F32))
        cosine, sine = cosine_ref[row_spot, :], sine_ref[row_spot, :]
        for head in range(heads):
            cols = slice(head * dim, (head + 1) * dim)
            part = acc[head * QUERY_ROWS : (head + 1) * QUERY_ROWS]
            part, gain_grad = unrope(
                part, raw_ref[row_spot, cols], query_gain_ref[...], cosine, sine
            )
            query_gain_grad_ref[...] += gain_grad
            part = part.astype(BF)
            for piece in range(pieces):
                out_ref[places[piece], :, cols] = part[piece * half : (piece + 1) * half]
        return carry

    lax.fori_loop(0, seq // QUERY_ROWS, back, 0)

    def finish(index, carry):
        row_start = pl.multiple_of(index * QUERY_ROWS, QUERY_ROWS)
        row_spot = pl.ds(row_start, QUERY_ROWS)
        key_cols = slice(heads * dim, (heads + 1) * dim)
        value_cols = slice((heads + 1) * dim, (heads + 2) * dim)
        part, gain_grad = unrope(
            key_grad_ref[row_spot, :],
            raw_ref[row_spot, key_cols],
            key_gain_ref[...],
            cosine_ref[row_spot, :],
            sine_ref[row_spot, :],
        )
        key_gain_grad_ref[...] += gain_grad
        part = part.astype(BF)
        value = value_grad_ref[row_spot, :].astype(BF)
        for piece in range(pieces):
            place = place_ref[index * pieces + piece]
            out_ref[place, :, key_cols] = part[piece * half : (piece + 1) * half]
            out_ref[place, :, value_cols] = value[piece * half : (piece + 1) * half]
        return carry

    lax.fori_loop(0, seq // QUERY_ROWS, finish, 0)


def one_hot(hit):
    return hit.astype(F32).astype(BF)


def select_kernel(groups, joint, *refs):
    target_ref, mine_ref, other_ref = refs[sum(groups) :]
    slots = mine_ref.shape[0] // 2
    target = target_ref[...]
    half = target.shape[1] // 8
    index = lax.broadcasted_iota(jnp.int32, (2 * slots, target.shape[1]), 0)
    pick = one_hot((index == target[0:1]) | (index == target[1:2]))
    for k in range(2):
        rows = []
        if joint:
            for ref in refs[: groups[0]]:
                for start in range(k * half, ref.shape[0], 2 * half):
                    rows.append(ref[start : start + half])
        else:
            first = k * groups[0]
            rows = [ref[...] for ref in refs[first : first + groups[k]]]
        picked = jnp.dot(pick, jnp.concatenate(rows, axis=0), preferred_element_type=F32)
        picked = picked.astype(BF)
        mine_ref[k * slots : (k + 1) * slots] = picked[:slots]
        other_ref[k * slots : (k + 1) * slots] = picked[slots:]


def select_rows(pieces, others, target, slots):
    width = pieces[0].shape[1]
    return pl.pallas_call(
        functools.partial(select_kernel, (len(pieces), len(others)), not others),
        out_shape=(jax.ShapeDtypeStruct((2 * slots, width), BF),) * 2,
        in_specs=[VMEM_SPEC] * (len(pieces) + len(others) + 1),
        out_specs=[VMEM_SPEC] * 2,
        compiler_params=pltpu.CompilerParams(vmem_limit_bytes=24 << 20),
        cost_estimate=COST,
    )(*pieces, *others, target)


def spread_kernel(chunks, part, grouped, *refs):
    mine_refs, other_refs = refs[:chunks], refs[chunks : 2 * chunks]
    target_ref, first_ref, second_ref = refs[2 * chunks : 2 * chunks + 3]
    outs = refs[2 * chunks + 3 :]
    slots = mine_refs[0].shape[0] // 2
    half = first_ref.shape[0] // chunks
    rows = 2 * half
    spot = slice(part * slots, (part + 1) * slots)
    for j in range(chunks):
        values = jnp.concatenate([mine_refs[j][spot], other_refs[j][spot]], axis=0)
        target = target_ref[j]
        index = lax.broadcasted_iota(jnp.int32, (4 * rows, 2 * slots), 1)
        pick = one_hot((index == target[:, 0:1]) | (index == target[:, 1:2]))
        spread = jnp.dot(pick, values, preferred_element_type=F32).astype(BF)
        for k in range(3):
            ref, start = (outs[k], j * rows) if grouped else (outs[3 * j + k], 0)
            ref[start : start + rows] = spread[k * rows : (k + 1) * rows]
        if grouped:
            ref = first_ref if 2 * j < chunks else second_ref
            start = j % (chunks // 2) * rows
            ref[start : start + rows] = spread[3 * rows :]
        else:
            first_ref[j * half : (j + 1) * half] = spread[3 * rows : 3 * rows + half]
            second_ref[j * half : (j + 1) * half] = spread[3 * rows + half :]


def spread_rows(mine, other, target, rows, part, grouped):
    chunks = len(mine)
    slots, width = mine[0].shape
    low = lambda count: jax.ShapeDtypeStruct((count, width), BF)
    blocks = (low(chunks * rows),) * 3 if grouped else (low(rows),) * (3 * chunks)
    outs = pl.pallas_call(
        functools.partial(spread_kernel, chunks, part, grouped),
        out_shape=(low(chunks * rows // 2),) * 2 + blocks,
        in_specs=[VMEM_SPEC] * (2 * chunks + 1),
        out_specs=[VMEM_SPEC] * (2 + len(blocks)),
        compiler_params=pltpu.CompilerParams(
            vmem_limit_bytes=(16 << 20) if chunks == 1 else (36 << 20)
        ),
        cost_estimate=COST,
    )(*mine, *other, target)
    return outs[:2], outs[2:]


def expert_kernel(expert_ref, mine_ref, other_ref, *refs):
    slots = mine_ref.shape[0] // 2
    rows, grads = slice(0, slots), slice(slots, 2 * slots)
    expert_body(
        expert_ref, mine_ref.at[rows], other_ref.at[rows], mine_ref.at[grads], other_ref.at[grads], *refs
    )


def expert_body(
    expert_ref,
    mine_ref,
    other_ref,
    grad_mine_ref,
    grad_other_ref,
    target_ref,
    route_ref,
    gate_ref,
    up_ref,
    down_ref,
    router_ref,
    back_mine_ref,
    back_other_ref,
    hidden_ref,
    gate_grad_ref,
    up_grad_ref,
    routed_ref,
    router_grad_ref,
):
    slots = mine_ref.shape[0]
    experts = router_ref.shape[0]
    tokens = target_ref.shape[1]
    rows = jnp.concatenate([mine_ref[...], other_ref[...]], axis=0)
    nt = (((1,), (1,)), ((), ()))
    tn = (((0,), (0,)), ((), ()))
    gate_pre = jnp.dot(rows, gate_ref[...], preferred_element_type=F32)
    up_pre = jnp.dot(rows, up_ref[...], preferred_element_type=F32)
    sigmoid = 1.0 / (1.0 + jnp.exp(-gate_pre))
    silu = gate_pre * sigmoid
    hidden = (silu * up_pre).astype(BF)
    hidden_ref[...] = hidden
    result = jnp.dot(hidden, down_ref[...], preferred_element_type=F32).astype(BF).astype(F32)
    slot_iota = lax.broadcasted_iota(jnp.int32, (slots, tokens), 0)
    expert_iota = lax.broadcasted_iota(jnp.int32, (experts, tokens), 0)
    masks = []
    for side in range(2):
        pick = one_hot(slot_iota == target_ref[side : side + 1, :])
        chosen = expert_iota == route_ref[side, 0:1, :]
        for k in range(1, route_ref.shape[1]):
            chosen = chosen | (expert_iota == route_ref[side, k : k + 1, :])
        masks.append(lax.dot_general(pick, one_hot(chosen), nt, preferred_element_type=F32))
    chosen = jnp.concatenate(masks, axis=0) > 0.5
    logits = lax.dot_general(rows, router_ref[...], nt, preferred_element_type=F32)
    top = jnp.max(jnp.where(chosen, logits, MASKED), axis=1, keepdims=True)
    weights = jnp.where(chosen, jnp.exp(logits - top), 0.0)
    total = jnp.sum(weights, axis=1, keepdims=True)
    gates = weights / jnp.where(total > 0.0, total, 1.0)
    mine = lax.broadcasted_iota(jnp.int32, gates.shape, 1) == expert_ref[0]
    gate = jnp.sum(jnp.where(mine, gates, 0.0), axis=1, keepdims=True)
    gated = (result * gate).astype(BF)
    back_mine_ref[slots:] = gated[:slots]
    back_other_ref[slots:] = gated[slots:]
    grad = jnp.concatenate([grad_mine_ref[...], grad_other_ref[...]], axis=0).astype(F32)
    gate_value_grad = jnp.sum(grad * result, axis=1, keepdims=True)
    routed = (grad * gate).astype(BF)
    routed_ref[...] = routed
    hidden_grad = lax.dot_general(routed, down_ref[...], nt, preferred_element_type=F32)
    gate_low = (hidden_grad * up_pre * sigmoid * (1.0 + gate_pre * (1.0 - sigmoid))).astype(BF)
    up_low = (hidden_grad * silu).astype(BF)
    gate_grad_ref[...] = gate_low
    up_grad_ref[...] = up_low
    logit_grad = (gate_value_grad * gate) * (jnp.where(mine, 1.0, 0.0) - gates)
    high = logit_grad.astype(BF)
    low = (logit_grad - high.astype(F32)).astype(BF)
    both = jnp.concatenate([high, low], axis=1)
    router = router_ref[...]
    slot_grad = lax.dot_general(gate_low, gate_ref[...], nt, preferred_element_type=F32)
    slot_grad = slot_grad + lax.dot_general(up_low, up_ref[...], nt, preferred_element_type=F32)
    slot_grad = slot_grad + jnp.dot(
        both, jnp.concatenate([router, router], axis=0), preferred_element_type=F32
    )
    slot_grad = slot_grad.astype(BF)
    back_mine_ref[:slots] = slot_grad[:slots]
    back_other_ref[:slots] = slot_grad[slots:]
    router_grad = lax.dot_general(both, rows, tn, preferred_element_type=F32)
    router_grad_ref[...] = router_grad[:experts] + router_grad[experts:]


def expert_rows(expert, mine, other, target, route, *weights):
    count, width = mine.shape
    ff = weights[0].shape[1]
    experts = weights[3].shape[0]
    low = lambda cols: jax.ShapeDtypeStruct((count, cols), BF)
    return pl.pallas_call(
        expert_kernel,
        out_shape=(
            low(width),
            low(width),
            low(ff),
            low(ff),
            low(ff),
            low(width),
            jax.ShapeDtypeStruct((experts, width), F32),
        ),
        in_specs=[SMEM_SPEC] + [VMEM_SPEC] * 8,
        out_specs=[VMEM_SPEC] * 7,
        compiler_params=pltpu.CompilerParams(vmem_limit_bytes=40 << 20),
        cost_estimate=COST,
    )(expert, mine, other, target, route, *weights)


def place_kernel(share, order_ref, owner_ref, part_ref, query_ref, key_ref, value_ref):
    cols = query_ref.shape[1]
    dim = key_ref.shape[1]
    part = part_ref[0]
    query_ref[...] = part[:, :cols].astype(F32)
    key = part[:, cols : cols + dim].astype(F32)
    value = part[:, cols + dim :].astype(F32)
    first = pl.program_id(0) % share == 0

    @pl.when(first)
    def _():
        key_ref[...] = key
        value_ref[...] = value

    @pl.when(jnp.logical_not(first))
    def _():
        key_ref[...] += key
        value_ref[...] += value


def place_weight_grads(parts, owner, share, dim):
    count, rows, width = parts.shape
    cols = width - 2 * dim
    if count == 8 and share == 2:
        order = jnp.asarray([0, 4, 1, 5, 2, 6, 3, 7], jnp.int32)
    else:
        order = jnp.arange(count, dtype=jnp.int32)
    owner = owner[order]
    group = lambda g, order, owner: (0, owner[g] // share)
    return pl.pallas_call(
        functools.partial(place_kernel, share),
        grid_spec=pltpu.PrefetchScalarGridSpec(
            num_scalar_prefetch=2,
            grid=(count,),
            in_specs=[pl.BlockSpec((1, rows, width), lambda g, order, owner: (order[g], 0, 0))],
            out_specs=[
                pl.BlockSpec((rows, cols), lambda g, order, owner: (0, owner[g])),
                pl.BlockSpec((rows, dim), group),
                pl.BlockSpec((rows, dim), group),
            ],
        ),
        out_shape=(
            jax.ShapeDtypeStruct((rows, cols * count), F32),
            jax.ShapeDtypeStruct((rows, dim * count // share), F32),
            jax.ShapeDtypeStruct((rows, dim * count // share), F32),
        ),
        compiler_params=pltpu.CompilerParams(vmem_limit_bytes=ATTEND_LIMIT),
        cost_estimate=COST,
    )(order, owner, parts)


def rows_kernel(owner_ref, part_ref, out_ref):
    out_ref[:, 0] = part_ref[0].astype(F32)


def place_rows(parts, owner):
    count, chunks, rows, width = parts.shape
    return pl.pallas_call(
        rows_kernel,
        grid_spec=pltpu.PrefetchScalarGridSpec(
            num_scalar_prefetch=1,
            grid=(count,),
            in_specs=[pl.BlockSpec((1, chunks, rows, width), lambda g, owner: (g, 0, 0, 0))],
            out_specs=pl.BlockSpec(
                (chunks, 1, rows, width), lambda g, owner: (0, owner[g], 0, 0)
            ),
        ),
        out_shape=jax.ShapeDtypeStruct((chunks, count, rows, width), F32),
        compiler_params=pltpu.CompilerParams(vmem_limit_bytes=ATTEND_LIMIT),
        cost_estimate=COST,
    )(owner, parts)


def place_pieces_kernel(share, owner_ref, *refs):
    pieces, (query_ref, key_ref, value_ref) = refs[:-3], refs[-3:]
    rows, dim = query_ref.shape[0], key_ref.shape[1] * share // 8
    cols = query_ref.shape[1] // 8
    for k in range(4):
        both = [
            [ref[...].astype(F32) for ref in refs_of]
            for refs_of in (block_refs(pieces, k), block_refs(pieces, k + 4))
        ]
        both = [p[0] if len(p) == 1 else jnp.concatenate(p, axis=0) for p in both]
        for side in range(2):
            start = pl.multiple_of(owner_ref[k + 4 * side] * cols, cols)
            query_ref[:, pl.ds(start, cols)] = both[side][:, :cols]
        start = pl.multiple_of(owner_ref[k] // share * dim, dim)
        key_ref[:, pl.ds(start, dim)] = both[0][:, cols : cols + dim] + both[1][:, cols : cols + dim]
        value_ref[:, pl.ds(start, dim)] = both[0][:, cols + dim :] + both[1][:, cols + dim :]


def block_refs(pieces, k):
    first = k // 4 * 5 + k % 4
    return pieces[first : first + 2] if k % 4 == 3 else pieces[first : first + 1]


def place_weight_pieces(pieces, owner, share, dim):
    rows, width = pieces[0].shape
    cols = width - 2 * dim
    return pl.pallas_call(
        functools.partial(place_pieces_kernel, share),
        out_shape=(
            jax.ShapeDtypeStruct((rows, cols * 8), F32),
            jax.ShapeDtypeStruct((rows, dim * 8 // share), F32),
            jax.ShapeDtypeStruct((rows, dim * 8 // share), F32),
        ),
        in_specs=[SMEM_SPEC] + [VMEM_SPEC] * len(pieces),
        out_specs=[VMEM_SPEC] * 3,
        compiler_params=pltpu.CompilerParams(vmem_limit_bytes=ATTEND_LIMIT),
        cost_estimate=COST,
    )(owner, *pieces)


def row_pieces_kernel(owner_ref, *refs):
    pieces, out_ref = refs[:-1], refs[-1]
    chunks, _, rows, _ = out_ref.shape
    for k in range(8):
        parts = [ref[...] for ref in block_refs(pieces, k)]
        part = parts[0] if len(parts) == 1 else jnp.concatenate(parts, axis=0)
        for chunk in range(chunks):
            out_ref[chunk, owner_ref[k]] = part[chunk * rows : (chunk + 1) * rows].astype(F32)


def place_row_pieces(pieces, owner, chunks):
    rows, width = pieces[0].shape
    return pl.pallas_call(
        row_pieces_kernel,
        out_shape=jax.ShapeDtypeStruct((chunks, 8, rows // chunks, width), F32),
        in_specs=[SMEM_SPEC] + [VMEM_SPEC] * len(pieces),
        out_specs=VMEM_SPEC,
        compiler_params=pltpu.CompilerParams(vmem_limit_bytes=ATTEND_LIMIT),
        cost_estimate=COST,
    )(owner, *pieces)


def product_kernel(dims, rows, left_count, right_count, starts, start_ref, *refs):
    lefts, rights = refs[:left_count], refs[left_count : left_count + right_count]
    outs = refs[left_count + right_count :]
    join = lambda parts: parts[0] if len(parts) == 1 else jnp.concatenate(parts, axis=0)
    right = join([ref[...] for ref in rights])
    for k, out_ref in enumerate(outs):
        if starts:
            width = out_ref.shape[0]
            cols = pl.ds(pl.multiple_of(start_ref[k] * width, width), width)
            left = join([ref[:, cols] for ref in lefts])
        else:
            left = join([ref[...] if rows is None else ref[:rows] for ref in lefts])
        out = lax.dot_general(left, right, (dims, ((), ())), preferred_element_type=F32)
        out_ref[...] = out.astype(out_ref.dtype)


def product(lefts, rights, dims, out_shape, kind=F32, rows=None, starts=None, limit=60, tile=None):
    count = 1 if starts is None else starts.shape[0]
    start_arg = jnp.zeros((1,), jnp.int32) if starts is None else starts
    if tile is None:
        left_specs, right_specs = [VMEM_SPEC] * len(lefts), [VMEM_SPEC] * len(rights)
        out_spec = VMEM_SPEC
    else:
        left_specs = [
            pl.BlockSpec((rows or left.shape[0], tile), lambda i: (0, i)) for left in lefts
        ]
        right_specs = [pl.BlockSpec(right.shape, lambda i: (0, 0)) for right in rights]
        out_spec = pl.BlockSpec((tile, out_shape[1]), lambda i: (i, 0))
    outs = pl.pallas_call(
        functools.partial(
            product_kernel, dims, None, len(lefts), len(rights), starts is not None
        ),
        grid=() if tile is None else (out_shape[0] // tile,),
        out_shape=(jax.ShapeDtypeStruct(out_shape, kind),) * count,
        in_specs=[SMEM_SPEC] + left_specs + right_specs,
        out_specs=[out_spec] * count,
        compiler_params=pltpu.CompilerParams(vmem_limit_bytes=limit << 20),
        cost_estimate=COST,
    )(start_arg, *lefts, *rights)
    return outs[0] if starts is None else outs


def move_slots(slot_array):
    return lax.all_to_all(slot_array, ("ctx", "wt"), split_axis=0, concat_axis=0, tiled=True)


def local(
    tokens,
    cotangent,
    segments,
    routes,
    pair_order,
    attn_gain,
    ffn_gain,
    query_gain,
    key_gain,
    w_query,
    key_weight,
    value_weight,
    w_output,
    w_router,
    w_gate,
    w_up,
    w_down,
):
    ctx_count = lax.axis_size("ctx")
    wt_count = lax.axis_size("wt")
    me = lax.axis_index("ctx")
    plane = lax.axis_index("wt")
    inputs = tokens[0].astype(F32)
    tok_rows, model_width = inputs.shape
    half_rows = tok_rows // 2
    head_dim = query_gain.shape[0]
    experts = w_router.shape[1]
    top_count = routes.shape[2]
    seq_len = segments.shape[1]
    total_tokens = tok_rows * ctx_count * wt_count
    heads = w_query.shape[1] // head_dim // ctx_count
    kv_heads = key_weight.shape[1] // head_dim
    share = ctx_count // kv_heads
    head_cols = heads * head_dim
    group = me // share
    shard_width = model_width // wt_count
    capacity = max(2, half_rows * top_count * 5 // (4 * experts))
    dense = ctx_count == 8 and wt_count == 4 and w_gate.shape[0] == 1
    nt = (((1,), (1,)), ((), ()))
    tn = (((0,), (0,)), ((), ()))
    owners = block_owner(ctx_count, me)
    planes = (plane - jnp.arange(wt_count, dtype=jnp.int32)) % wt_count

    normed_one, attn_back = jax.vjp(rms_norm, inputs, attn_gain)
    normed_low = normed_one.astype(BF)
    kv_start = group * head_dim
    own_weight = jnp.concatenate(
        [
            lax.dynamic_slice_in_dim(w_query, me * head_cols, head_cols, 1),
            lax.dynamic_slice_in_dim(key_weight, kv_start, head_dim, 1),
            lax.dynamic_slice_in_dim(value_weight, kv_start, head_dim, 1),
        ],
        axis=1,
    )
    own_chunks = ctx_count // wt_count
    piece_rows = head_cols // ctx_count
    out_piece = lax.dynamic_index_in_dim(
        w_output.reshape(own_chunks, ctx_count, piece_rows, model_width), me, 1, keepdims=False
    )
    cot = cotangent[0]
    if dense:
        cap_rows = 2 * capacity
        slots = 4 * cap_rows
        expert = me * wt_count + plane
        triangle = jnp.triu(jnp.ones((tok_rows, tok_rows), F32)).astype(BF)
        offsets = (jnp.arange(ctx_count, dtype=jnp.int32) % 4) * cap_rows

        def tables(near):
            near = near.astype(jnp.int32).reshape(-1, ctx_count, top_count, tok_rows)

            def slot_of(routed_to):
                hits = jnp.any(near == routed_to, axis=2)
                ranks = jnp.dot(hits.astype(BF), triangle, preferred_element_type=F32)
                place = ranks.astype(jnp.int32) - 1 + offsets[None, :, None]
                return jnp.where(hits, place, -1).reshape(-1, 2, 4 * tok_rows)

            own_slot = slot_of(expert)
            other_slot = slot_of((me ^ 1) * wt_count + plane)[:, 0]
            target = jnp.stack(
                [own_slot[:, 0], jnp.where(other_slot < 0, -1, other_slot + slots)], axis=1
            )
            near_routes = (
                near.reshape(-1, 2, 4, top_count, tok_rows)
                .transpose(0, 1, 3, 2, 4)
                .reshape(-1, 2, top_count, 4 * tok_rows)
            )
            indices = jnp.arange(experts, dtype=jnp.int32)[:, None, None, None, None]
            counts = jnp.sum((near[None] == indices).astype(F32), axis=(1, 2, 3, 4))
            return own_slot, target, target.transpose(0, 2, 1), near_routes, counts

        block_rows = own_chunks * piece_rows
        out_piece = out_piece.reshape(block_rows, model_width)
        ticks = [(out_piece, own_weight), (ring(out_piece), ring(own_weight))]
        own = after(normed_low, out_piece, own_weight)
        via_x, via_y = swap(own, 2), swap(own, 4)
        near = after(routes[0].T.astype(BF), own)
        near_x, near_y = swap(near, 2), swap(near, 4)
        sent = via_x[:half_rows], via_y[half_rows:]
        diag_a, diag_b = swap(sent[0], 4), swap(sent[1], 2)
        near_x, near_y = after((near_x, near_y), sent)
        near = jnp.concatenate([near, near_x, near_y, swap(near_x, 4)], axis=0)
        near = jnp.concatenate([near, swap(near, 1)], axis=0)
        hidden_pieces = [own, via_x, via_y, diag_a, diag_b]
        hidden_pieces = hidden_pieces + [swap(piece, 1) for piece in hidden_pieces]
        ticks[1], near, cot_block = after((ticks[1], near, cot), ticks[1], hidden_pieces, near)
        near_rows = near.shape[0]
        tiny = jnp.concatenate([near, w_router.T.reshape(-1, tok_rows)], axis=0)
        tinies = [tiny, ring(tiny)]
        cot_x, cot_y = swap(cot_block, 2), swap(cot_block, 4)
        ticks.append((ring(ticks[1][0]), ring(ticks[1][1])))
        first_tables = tables(near)
        zero = ticks[1][0][0, 0].astype(F32) * 0.0
        tables_done = cosine, sine = rope_tables(seq_len, head_dim, zero)
        def keep(j, buffers, shards):
            put = lax.dynamic_update_slice_in_dim
            return (
                put(buffers[0], shards[0], planes[j] * block_rows, 0),
                put(buffers[1], shards[1], planes[j] * shard_width, 0),
            )

        cot_sent = cot_x[:half_rows], cot_y[half_rows:]
        ticks[2], cot_sent, tinies[1] = after(
            (ticks[2], cot_sent, tinies[1]), ticks[2], cot_sent, tinies[1], first_tables, tables_done
        )
        ticks.append((ring(ticks[2][0]), ring(ticks[2][1])))
        tinies.append(ring(tinies[1]))
        diag_a, diag_b = swap(cot_sent[0], 4), swap(cot_sent[1], 2)
        seed = ticks[2][0][:1, :1] * 0
        buffers = (
            jnp.broadcast_to(seed, (ctx_count * piece_rows, model_width)),
            jnp.broadcast_to(seed, (model_width, own_weight.shape[1])),
        )

        for j in range(3):
            buffers = keep(j, buffers, ticks[j])
        cot_pieces = [cot, cot_x, cot_y, diag_a, diag_b]
        cot_diag = jnp.concatenate([diag_a, diag_b], axis=0)
        ticks[3] = after(ticks[3], cot_diag, tinies[2], buffers)
        out_pieces, weight = keep(3, buffers, ticks[3])
        tinies.append(ring(after(tinies[2], weight)))
        cot_next = [ring(after(p, weight)) for p in (cot, cot_x, cot_y, cot_diag)]
        nears = [tiny[:near_rows] for tiny in tinies]
        router = jnp.stack([tiny[near_rows:].reshape(experts, shard_width) for tiny in tinies])
        router = router[planes].transpose(1, 0, 2).reshape(experts, model_width)
    else:
        hidden_pieces = plane_gather(normed_low)
        out_pieces = lax.all_gather(out_piece, "wt", axis=0, tiled=True)
        weight = lax.all_gather(own_weight, "wt", axis=0, tiled=True)
        router = lax.all_gather(w_router, "wt", axis=0, tiled=True).T
        cosine, sine = rope_tables(seq_len, head_dim, 0.0)
    out_weight = lax.all_to_all(
        out_pieces.reshape(ctx_count, piece_rows, model_width), "ctx", 0, 0, tiled=True
    ).reshape(head_cols, model_width)

    owner_pair = pair_order[owners]
    blocks = jnp.stack([owner_pair, 2 * ctx_count - 1 - owner_pair], 1).reshape(-1)
    order = jnp.arange(2 * ctx_count, dtype=jnp.int32)
    places = jnp.sum(jnp.where(blocks[:, None] == order[None, :], order[:, None], 0), axis=0)
    places = places.astype(jnp.int32)
    seg = segments[0]
    first = jnp.sum(
        (seg[None, :] < seg[::QUERY_ROWS][:, None]).astype(jnp.int32), axis=1
    ).astype(jnp.int32)
    seg_row, seg_col = seg.reshape(1, seq_len), seg.reshape(seq_len, 1)
    query_gain_row, key_gain_row = query_gain.reshape(1, -1), key_gain.reshape(1, -1)

    width = head_cols + 2 * head_dim
    stacked = heads * QUERY_ROWS
    piece_count = len(hidden_pieces)
    query, key, value, raw, attn_low = pl.pallas_call(
        functools.partial(attend_kernel, heads, piece_count),
        out_shape=(
            jax.ShapeDtypeStruct((seq_len, head_cols), BF),
            jax.ShapeDtypeStruct((seq_len, head_dim), BF),
            jax.ShapeDtypeStruct((seq_len, head_dim), BF),
            jax.ShapeDtypeStruct((seq_len, head_cols + head_dim), F32),
            jax.ShapeDtypeStruct((2 * ctx_count, half_rows, head_cols), BF),
        ),
        in_specs=[SMEM_SPEC] * 3 + [VMEM_SPEC] * (7 + piece_count),
        out_specs=[VMEM_SPEC] * 5,
        scratch_shapes=[pltpu.VMEM((stacked, seq_len), F32)],
        compiler_params=pltpu.CompilerParams(vmem_limit_bytes=ATTEND_LIMIT),
        cost_estimate=COST,
    )(
        blocks,
        places,
        first,
        *hidden_pieces,
        weight,
        query_gain_row,
        key_gain_row,
        cosine,
        sine,
        seg_row,
        seg_col,
    )
    attn_rows = attn_low.reshape(seq_len, head_cols)
    later_tables = []
    out_project = lambda rows, kind: low_matmul(rows, out_weight).astype(kind)
    if dense:
        attn_rows = after(attn_rows, cot_next[:2])
        out_project = lambda rows, kind: product(
            [rows], [out_weight], ((1,), (0,)), (rows.shape[0], model_width), kind
        )

        def fill(sends):
            later_tables.extend(tables(after(jnp.concatenate(nears[1:], axis=0), sends)))
            return tuple(later_tables) + (cot_next[2],)

        attn = plane_scatter(out_project, attn_rows, fill, (), (cot_next[3],))
    else:
        attn = plane_scatter(out_project, attn_rows)
    residual = inputs + attn
    normed_two, ffn_back = jax.vjp(rms_norm, residual, ffn_gain)
    normed_two_low = normed_two.astype(BF)
    grad_out = cotangent[0].astype(F32)
    if dense:
        own_slot, target_rows, target_cols, near_routes = (
            jnp.concatenate([f, r], axis=0) for f, r in zip(first_tables[:4], later_tables[:4])
        )
        counts = first_tables[4] + later_tables[4]
        logits = lax.dot_general(normed_two_low, router, nt, preferred_element_type=F32)
        router_probs = jax.nn.softmax(logits, axis=-1)
        shares = counts / (total_tokens * top_count)
        prob_grad = (experts * shares / total_tokens)[None, :]
        logits_grad = router_probs * (
            prob_grad - jnp.sum(router_probs * prob_grad, axis=1, keepdims=True)
        )
        logits_grad_low = logits_grad.astype(BF)
        last = wt_count - 1
        mine_backs, other_backs, results = [], [], []

        def compute(j, pieces, others, gates, second=()):
            pieces = after(pieces, *gates)
            mine, other = select_rows(pieces, others, target_rows[j], slots)
            received = after(swap(other, 1), second)
            result = expert_rows(
                expert.reshape(1),
                mine,
                received,
                own_slot[j],
                near_routes[j],
                w_gate[0],
                w_up[0],
                w_down[0],
                router,
            )
            mine_backs.append(result[0])
            other_backs.append(swap(result[1], 1))
            results.append((mine, received) + tuple(result[2:]))
            return result[0]

        payload, before, done = normed_two_low, None, None
        for j in range(wt_count):
            if j == 2:
                cot_own = cot_next[0]
                halves = payload[:half_rows], cot_own[:half_rows], payload[half_rows:], cot_own[half_rows:]
                payload = jnp.concatenate(halves, axis=0)
            if j > 0:
                payload = ring(payload)
            block = payload if j == 0 else after(payload, before[3:])
            via_x, via_y = swap(block, 2), swap(block, 4)
            if done is not None:
                via_x, via_y = after((via_x, via_y), done)
            middle = via_x.shape[0] // 2
            sent = via_x[:middle], via_y[middle:]
            pieces = [block, via_x, via_y, swap(sent[0], 4), swap(sent[1], 2)]
            if before is not None:
                done = compute(j - 1, before, [cot_pieces, cot_next, []][j - 1], (sent,), pieces[3:])
            before = pieces
        group_sent, blocks = spread_rows(
            mine_backs, other_backs, target_cols[:last], tok_rows, 0, False
        )
        group_sent = after(group_sent, sent)
        group_diag = swap(group_sent[0], 4), swap(group_sent[1], 2)
        done = compute(last, pieces, [], (done,), group_sent)
        step = Order(done)

        def add_chunk(own, part_x, part_y, from_y, from_x):
            part_x, part_y, from_y, from_x = step.take((part_x, part_y, from_y, from_x))
            part_x, part_y = add_diag(part_x, part_y, from_y, from_x)
            step.give(part_x, part_y)
            return own, swap(part_x, 2), swap(part_y, 4)

        def chunk_sum(own, got_x, got_y):
            return [own] + list(step.take((got_x, got_y)))

        def chunk_diag(j):
            return [part[j * half_rows : (j + 1) * half_rows] for part in group_diag]

        partial = {j: add_chunk(*blocks[3 * j : 3 * j + 3], *chunk_diag(j)) for j in range(1, last)}
        tail_sent, tail = spread_rows(
            step.take(mine_backs[last:]), other_backs[last:], target_cols[last:], tok_rows, 0, False
        )
        step.give(tail_sent)
        tail_diag = swap(tail_sent[0], 4), swap(tail_sent[1], 2)
        rows_all = [r for res in results for r in res[:2]]
        hidden_low, gate_low, up_low, routed = ([res[k] for res in results] for k in range(2, 6))
        ff = w_gate.shape[2]
        grad_w_gate = product(step.take(rows_all), gate_low, ((0,), (0,)), (model_width, ff), F32, slots, tile=512, limit=40)
        step.give(grad_w_gate)
        total = sum_of(chunk_sum(*partial[1]), BF)
        step.give(total)
        total = ring(total)
        grad_w_up = product(step.take(rows_all), up_low, ((0,), (0,)), (model_width, ff), F32, slots, tile=512, limit=40)
        step.give(grad_w_up)
        for j in range(2, last):
            total = sum_of([step.take(total)] + chunk_sum(*partial[j]), BF)
            step.give(total)
            total = ring(total)
        partial[last] = add_chunk(*tail, *tail_diag)
        partial[0] = add_chunk(*blocks[:3], *chunk_diag(0))
        grad_w_down = product(
            step.take(hidden_low), routed, ((0,), (0,)), (ff, model_width), F32, tile=256, limit=40
        )
        step.give(grad_w_down)
        total = sum_of([step.take(total)] + chunk_sum(*partial[last]), BF)
        step.give(total)
        total = ring(total)
        out_sent, out_blocks = spread_rows(
            step.take(mine_backs), other_backs, target_cols, tok_rows, 1, True
        )
        step.give(out_sent)
        total = sum_of([step.take(total)] + chunk_sum(*partial[0]), F32)
        grad_normed_two = total + jnp.dot(logits_grad_low, router, preferred_element_type=F32)
        grad_w_gate, grad_w_up, grad_w_down = grad_w_gate[None], grad_w_up[None], grad_w_down[None]
        router_grad = sum(res[6] for res in results) + lax.dot_general(
            logits_grad_low, normed_two_low, tn, preferred_element_type=F32
        )
    else:
        w_router_all = router.T
        slot_rows = 2 * capacity
        local_experts = w_gate.shape[0]
        logits = low_matmul(normed_two_low, w_router_all)
        local_routes = routes[0]

        def router_fn(logit_values):
            router_probs = jax.nn.softmax(logit_values, axis=-1)
            chosen = jnp.take_along_axis(router_probs, local_routes, axis=1)
            return (chosen / jnp.sum(chosen, axis=1, keepdims=True), router_probs)

        (gate_values, router_probs), router_back = jax.vjp(router_fn, logits)
        route_flat = local_routes.reshape(-1)
        route_hits = (route_flat[:, None] == jnp.arange(experts, dtype=jnp.int32)[None, :]).astype(
            jnp.int32
        )
        counts = lax.psum(jnp.sum(route_hits, axis=0).astype(jnp.float32), ("ctx", "wt"))
        shares = counts / (total_tokens * top_count)
        halves = route_hits.reshape(2, half_rows * top_count, experts)
        ranks = jnp.sum((jnp.cumsum(halves, axis=1) - halves) * halves, axis=2).reshape(-1)
        half_index = jnp.arange(tok_rows * top_count, dtype=jnp.int32) // (half_rows * top_count)
        slot_index = route_flat * slot_rows + half_index * capacity + ranks
        slot_owner = (
            jnp.full((experts * slot_rows,), tok_rows * top_count, jnp.int32)
            .at[slot_index]
            .set(jnp.arange(tok_rows * top_count, dtype=jnp.int32))
        )
        slot_shape = (experts // local_experts, local_experts, slot_rows, model_width)
        padded = jnp.concatenate([normed_two_low, jnp.zeros((1, model_width), jnp.bfloat16)], axis=0)
        outgoing = padded[slot_owner // top_count].reshape(slot_shape)
        arrived = move_slots(outgoing)
        gate_pre = jnp.einsum("nesd,edf->nesf", arrived, w_gate, preferred_element_type=jnp.float32)
        up_pre = jnp.einsum("nesd,edf->nesf", arrived, w_up, preferred_element_type=jnp.float32)
        hidden_low, swiglu_back = jax.vjp(swiglu, gate_pre, up_pre)
        hidden_low = hidden_low.astype(jnp.bfloat16)
        expert_out = jnp.einsum(
            "nesf,efd->nesd", hidden_low, w_down, preferred_element_type=jnp.float32
        ).astype(jnp.bfloat16)
        returned = move_slots(expert_out).reshape(experts * slot_rows, model_width)
        picked = returned[slot_index].reshape(tok_rows, top_count, model_width)
        mixture = jnp.einsum("tk,tkd->td", gate_values, picked, preferred_element_type=jnp.float32)
        output = (residual + mixture).astype(jnp.bfloat16)
        grad_gates = jnp.einsum("td,tkd->tk", grad_out, picked, preferred_element_type=jnp.float32)
        grad_routed = (
            (gate_values[:, :, None] * grad_out[:, None, :])
            .astype(jnp.bfloat16)
            .reshape(-1, model_width)
        )
        grad_routed = jnp.concatenate([grad_routed, jnp.zeros((1, model_width), jnp.bfloat16)], axis=0)
        grad_arrived = move_slots(grad_routed[slot_owner].reshape(slot_shape))
        grad_hidden = jnp.einsum(
            "nesd,efd->nesf", grad_arrived, w_down, preferred_element_type=jnp.float32
        )
        grad_w_down = jnp.einsum(
            "nesf,nesd->efd", hidden_low, grad_arrived, preferred_element_type=jnp.float32
        )
        grad_gate_pre, grad_up_pre = swiglu_back(grad_hidden)
        gate_grad_low = grad_gate_pre.astype(jnp.bfloat16)
        up_grad_low = grad_up_pre.astype(jnp.bfloat16)
        grad_w_gate = jnp.einsum(
            "nesd,nesf->edf", arrived, gate_grad_low, preferred_element_type=jnp.float32
        )
        grad_w_up = jnp.einsum(
            "nesd,nesf->edf", arrived, up_grad_low, preferred_element_type=jnp.float32
        )
        grad_slots = (
            jnp.einsum("nesf,edf->nesd", gate_grad_low, w_gate, preferred_element_type=jnp.float32)
            + jnp.einsum("nesf,edf->nesd", up_grad_low, w_up, preferred_element_type=jnp.float32)
        ).astype(jnp.bfloat16)
        grad_back = move_slots(grad_slots).reshape(experts * slot_rows, model_width)
        grad_normed_two = jnp.sum(
            grad_back[slot_index].reshape(tok_rows, top_count, model_width).astype(jnp.float32), axis=1
        )
        prob_grad = jnp.broadcast_to(experts * shares / total_tokens, router_probs.shape)
        (grad_logits,) = router_back((grad_gates, prob_grad))
        logits_low = grad_logits.astype(jnp.bfloat16)
        grad_normed_two = grad_normed_two + jnp.einsum(
            "te,de->td", logits_low, w_router_all, preferred_element_type=jnp.float32
        )
        grad_w_router = jnp.einsum(
            "td,te->de", normed_two_low, logits_low, preferred_element_type=jnp.float32
        )
        router_grad = grad_w_router.T
    grad_residual_part, grad_ffn_gain = ffn_back(grad_normed_two)
    grad_residual = grad_out + grad_residual_part
    grad_pieces = plane_gather(grad_residual.astype(BF))
    if dense:
        out_grad = product(
            [attn_rows], grad_pieces, ((0,), (0,)), (head_cols, model_width), BF, limit=40
        )
    else:
        out_grad = lax.dot_general(
            attn_rows, jnp.concatenate(grad_pieces, axis=0), tn, preferred_element_type=F32
        ).astype(BF)
    if dense:
        out_sent = after(out_sent, grad_pieces)
        out_diag = swap(out_sent[0], 4), swap(out_sent[1], 2)
        query = after(query, out_sent, out_grad)
    out_grad = lax.all_to_all(
        out_grad.reshape(ctx_count, piece_rows, model_width), "ctx", 0, 0, tiled=True
    )
    head_grads, grad_query_gain, grad_key_gain = pl.pallas_call(
        functools.partial(attend_back_kernel, heads, piece_count),
        out_shape=(
            jax.ShapeDtypeStruct((2 * ctx_count, half_rows, width), BF),
            jax.ShapeDtypeStruct((1, head_dim), F32),
            jax.ShapeDtypeStruct((1, head_dim), F32),
        ),
        in_specs=[SMEM_SPEC] * 2 + [VMEM_SPEC] * (11 + piece_count),
        out_specs=[VMEM_SPEC] * 3,
        scratch_shapes=[
            pltpu.VMEM((stacked, seq_len), F32),
            pltpu.VMEM((stacked, seq_len), F32),
            pltpu.VMEM((seq_len, head_dim), F32),
            pltpu.VMEM((seq_len, head_dim), F32),
            pltpu.VMEM((2 * ctx_count, half_rows, head_cols), BF),
        ],
        compiler_params=pltpu.CompilerParams(vmem_limit_bytes=40 << 20),
        cost_estimate=COST,
    )(
        places,
        first,
        *grad_pieces,
        out_weight,
        query,
        key,
        value,
        raw,
        query_gain_row,
        key_gain_row,
        cosine,
        sine,
        seg_row,
        seg_col,
    )
    head_grads = head_grads.reshape(seq_len, width)
    heads_back = lambda rows, kind: lax.dot_general(
        rows, weight, nt, preferred_element_type=F32
    ).astype(kind)
    if dense:
        step = Order(out_grad)

        def weight_parts(places, kind):
            return product(
                hidden_pieces,
                [step.take(head_grads)],
                ((0,), (0,)),
                (shard_width, width),
                kind,
                starts=places,
            )

        def add_send(got, part, kind=BF):
            total = sum_of([step.take(got), part], kind)
            step.give(total)
            return ring(total)

        (first,) = weight_parts(planes[1:2], BF)
        step.give(first)
        total = ring(first)
        out_x, out_y = add_diag(*step.take((out_blocks[1], out_blocks[2])), *step.take(out_diag))
        step.give(out_x, out_y)
        out_got = swap(out_x, 2), swap(out_y, 4)
        more = weight_parts(planes[jnp.asarray([2, 3, 0])], F32)
        step.give(more)
        total = add_send(total, more[0])
        side = seq_len // 2
        give = product(
            [step.take(head_grads[side:])], [weight], ((1,), (1,)), (side, model_width), BF
        )
        step.give(give)
        got = swap(give, 1)
        keep_part = product(
            [step.take(head_grads[:side])], [weight], ((1,), (1,)), (side, model_width), BF
        )
        step.give(keep_part)
        total = add_send(total, more[1])
        out_parts = step.take(out_grad).reshape(wt_count, block_rows, model_width)
        out_parts = [
            lax.dynamic_index_in_dim(out_parts, planes[j], 0, keepdims=False)
            for j in range(wt_count)
        ]
        step.give(out_parts[1])
        out_total = ring(out_parts[1])
        sums = sum_of([out_blocks[0]] + list(step.take(out_got)), F32)
        step.give(sums)
        sums = sums.reshape(wt_count, tok_rows, model_width)
        kept = sum_of([keep_part, step.take(got)], BF)
        kept_sent = kept[3 * tok_rows : -half_rows], kept[-half_rows:]
        step.give(kept_sent)
        kept_diag = swap(kept_sent[0], 4), swap(kept_sent[1], 2)
        mixed_low = step.take(sums[1]).astype(BF)
        step.give(mixed_low)
        mixed_total = ring(mixed_low)
        weight_grad = sum_of([step.take(total), more[2]], BF)
        step.give(weight_grad)
        weight_x, weight_y = swap(weight_grad, 2), swap(weight_grad, 4)
        half = weight_grad.shape[0] // 2
        weight_x, weight_y = step.take((weight_x, weight_y))
        weight_sent = weight_x[:half], weight_y[half:]
        step.give(weight_sent)
        weight_pieces = [
            weight_grad,
            weight_x,
            weight_y,
            swap(weight_sent[0], 4),
            swap(weight_sent[1], 2),
        ]
        weight_pieces = weight_pieces + [swap(piece, 1) for piece in weight_pieces]
        kept_x, kept_y = add_diag(
            kept[tok_rows : 2 * tok_rows], kept[2 * tok_rows : 3 * tok_rows], *step.take(kept_diag)
        )
        step.give(kept_x, kept_y)
        kept_got = swap(kept_x, 2), swap(kept_y, 4)
        out_total = add_send(out_total, out_parts[2])
        mixed_total = add_send(mixed_total, sums[2])
        kept_got = step.take(kept_got)
        grad_normed_one = sum_of([kept[:tok_rows]] + list(kept_got), F32)
    else:
        hidden_rows = jnp.concatenate(hidden_pieces, axis=0)
        weight_grad = lax.dot_general(hidden_rows, head_grads, tn, preferred_element_type=F32)
        weight_grad = lax.psum_scatter(
            weight_grad.astype(BF), "wt", scatter_dimension=0, tiled=True
        )
        weight_grads = jnp.concatenate(plane_gather(weight_grad), axis=0)
        grad_w_query, grad_w_key, grad_w_value = place_weight_grads(
            weight_grads.reshape(ctx_count, -1, width), owners, share, head_dim
        )
        out_grad = lax.psum_scatter(out_grad, "wt", scatter_dimension=0, tiled=True)
        out_grads = jnp.concatenate(plane_gather(out_grad.reshape(-1, model_width)), axis=0)
        grad_w_output = place_rows(
            out_grads.reshape(ctx_count, own_chunks, piece_rows, model_width), owners
        ).reshape(w_output.shape)
        grad_normed_one = plane_scatter(heads_back, head_grads)
    grad_inputs_part, grad_attn_gain = attn_back(grad_normed_one)
    grad_inputs = grad_residual + grad_inputs_part

    part = head_dim // wt_count
    prob_sums = jnp.sum(router_probs, axis=0)
    prob_row = jnp.zeros((shard_width - 2 * part,), F32)
    if dense:
        prob_row = lax.dynamic_update_slice_in_dim(prob_row, prob_sums, plane * experts, 0)
    gains = jnp.concatenate(
        [
            grad_query_gain.reshape(wt_count, part),
            grad_key_gain.reshape(wt_count, part),
            jnp.broadcast_to(prob_row[None], (wt_count, shard_width - 2 * part)),
        ],
        axis=1,
    )
    small = jnp.concatenate([router_grad, grad_ffn_gain[None], grad_attn_gain[None]], axis=0)
    small = small.reshape(experts + 2, wt_count, shard_width).transpose(1, 0, 2)
    small = jnp.concatenate([small, gains[:, None]], axis=1)[planes]
    if dense:
        out_total = add_send(out_total, out_parts[3])
        mixed_total = add_send(mixed_total, sums[3])
        small_low = step.take(small[1])
        small_total = ring(small_low)
        out_total = sum_of([step.take(out_total), out_parts[0]], BF)
        step.give(out_total)
        out_x, out_y = swap(out_total, 2), swap(out_total, 4)
        small_total = add_send(small_total, small[2], F32)
        grad_w_query, grad_w_key, grad_w_value = place_weight_pieces(
            step.take(weight_pieces), owners, share, head_dim
        )
        step.give(grad_w_value)
        out_x, out_y = step.take((out_x, out_y))
        half = out_total.shape[0] // 2
        out_sent = out_x[:half], out_y[half:]
        step.give(out_sent)
        out_pieces = [out_total, out_x, out_y, swap(out_sent[0], 4), swap(out_sent[1], 2)]
        out_pieces = out_pieces + [swap(piece, 1) for piece in out_pieces]
        small_total = add_send(small_total, small[3], F32)
        output = step.take(mixed_total).astype(F32) + sums[0]
        output = (residual + output).astype(BF)
        step.give(output)
        small = step.take(small_total) + small[0]
        step.give(small)
        grad_w_output = place_row_pieces(step.take(out_pieces), owners, own_chunks)
        grad_w_output = grad_w_output.reshape(w_output.shape)
        small = axis_sum(small, "ctx")
    else:
        small = ring_sum([small[j] for j in range(wt_count)], F32)
        small = axis_sum(small, "ctx")
    if dense:
        prob_sums = small[experts + 2, 2 * part : 2 * part + wt_count * experts]
        prob_sums = jnp.sum(prob_sums.reshape(wt_count, experts), axis=0)
    else:
        prob_sums = axis_sum(axis_sum(prob_sums[None], "ctx"), "wt")[0]
    balance = experts * experts * shares * (prob_sums / total_tokens)
    loss_value = jnp.mean(balance)
    return (
        output[None],
        loss_value,
        balance,
        grad_inputs[None],
        small[experts + 1],
        small[experts],
        small[experts + 2, :part],
        small[experts + 2, part : 2 * part],
        grad_w_query,
        grad_w_key,
        grad_w_value,
        grad_w_output,
        small[:experts].T,
        grad_w_gate,
        grad_w_up,
        grad_w_down,
    )


def solution(mesh):
    in_specs = (
        P("wt", "ctx", None),
        P("wt", "ctx", None),
        P("wt", None),
        P("wt", "ctx", None),
        P(),
        P(),
        P(),
        P(),
        P(),
        P("wt", None),
        P("wt", None),
        P("wt", None),
        P("wt", None),
        P("wt", None),
        P(("ctx", "wt"), None, None),
        P(("ctx", "wt"), None, None),
        P(("ctx", "wt"), None, None),
    )
    out_specs = (
        P("wt", "ctx", None),
        P(),
        P(),
        P("wt", "ctx", None),
        P("wt"),
        P("wt"),
        P("wt"),
        P("wt"),
        P("wt", None),
        P("wt", None),
        P("wt", None),
        P("wt", None),
        P("wt", None),
        P(("ctx", "wt"), None, None),
        P(("ctx", "wt"), None, None),
        P(("ctx", "wt"), None, None),
    )
    return jax.shard_map(local, mesh=mesh, in_specs=in_specs, out_specs=out_specs, check_vma=False)
```

```python
import functools

import jax
import jax.numpy as jnp
from jax import lax
from jax.experimental import pallas as pl
from jax.experimental.pallas import tpu as pltpu
from jax.sharding import PartitionSpec as P

EPSILON = 1e-06
ROPE_BASE = 1000000.0
MASKED = -1e30
BF = jnp.bfloat16
F32 = jnp.float32
VMEM_SPEC = pl.BlockSpec(memory_space=pltpu.VMEM)
SMEM_SPEC = pl.BlockSpec(memory_space=pltpu.SMEM)
QUERY_ROWS = 128
KEY_ROWS = 256
ATTEND_LIMIT = 60 << 20
COST = pl.CostEstimate(flops=1, bytes_accessed=1, transcendentals=0)


def rms_norm(value_vectors, gain_vector):
    return (
        value_vectors
        * lax.rsqrt(jnp.mean(value_vectors * value_vectors, axis=-1, keepdims=True) + EPSILON)
        * gain_vector
    )


def low_matmul(left, right):
    return jnp.dot(left, right, preferred_element_type=F32)


def swiglu(gate_pre, up_pre):
    return jax.nn.silu(gate_pre) * up_pre


def rope_tables(length, head_width, zero):
    inv_freq = ROPE_BASE ** (-jnp.arange(0, head_width // 2, dtype=F32) * 2.0 / head_width)
    angle_table = (jnp.arange(length, dtype=F32) + zero)[:, None] * inv_freq[None, :]
    cosine, sine = jnp.cos(angle_table), jnp.sin(angle_table)
    return jnp.concatenate([cosine, cosine], 1), jnp.concatenate([-sine, sine], 1)


RELATIVE = (0, 2, 4, 6, 1, 3, 5, 7)


def swap(value, bit):
    count = lax.axis_size("ctx")
    return lax.ppermute(value, "ctx", [(i, i ^ bit) for i in range(count)])


def block_owner(count, me):
    if count == 8:
        return jnp.asarray(RELATIVE, jnp.int32) ^ me
    return jnp.arange(count, dtype=jnp.int32)


def after(value, *others):
    return lax.optimization_barrier((value,) + others)[0]


def plane_pieces(block):
    half = block.shape[0] // 2
    via_x = swap(block, 2)
    via_y = swap(block, 4)
    return [block, via_x, via_y, swap(via_x[:half], 4), swap(via_y[half:], 2)]


def plane_sends(block):
    half = block.shape[0] // 2
    via_x = swap(block, 2)
    via_y = swap(block, 4)
    from_x, from_y = via_x[:half], via_y[half:]
    return [block, via_x, via_y, swap(from_x, 4), swap(from_y, 2)], (from_x, from_y)


def plane_gather(block):
    count = lax.axis_size("ctx")
    if count != 8:
        return [lax.all_gather(block, "ctx", axis=0, tiled=True)]
    mine = plane_pieces(block)
    return mine + [swap(piece, 1) for piece in mine]


def sum_kernel(*refs):
    total = refs[0][...].astype(F32)
    for ref in refs[1:-1]:
        total = total + ref[...].astype(F32)
    refs[-1][...] = total.astype(refs[-1].dtype)


def sum_of(values, kind, limit=24):
    return pl.pallas_call(
        sum_kernel,
        out_shape=jax.ShapeDtypeStruct(values[0].shape, kind),
        in_specs=[VMEM_SPEC] * len(values),
        out_specs=VMEM_SPEC,
        compiler_params=pltpu.CompilerParams(vmem_limit_bytes=limit << 20),
        cost_estimate=COST,
    )(*values)


def add_diag_kernel(part_x_ref, part_y_ref, from_y_ref, from_x_ref, out_x_ref, out_y_ref):
    half = from_y_ref.shape[0]
    low = lambda a, b: (a.astype(F32) + b.astype(F32)).astype(BF)
    out_x_ref[:half] = low(part_x_ref[:half], from_y_ref[...])
    out_x_ref[half:] = part_x_ref[half:].astype(BF)
    out_y_ref[:half] = part_y_ref[:half].astype(BF)
    out_y_ref[half:] = low(part_y_ref[half:], from_x_ref[...])


def add_diag(part_x, part_y, from_y, from_x, limit=24):
    return pl.pallas_call(
        add_diag_kernel,
        out_shape=(jax.ShapeDtypeStruct(part_x.shape, BF),) * 2,
        in_specs=[VMEM_SPEC] * 4,
        out_specs=[VMEM_SPEC] * 2,
        compiler_params=pltpu.CompilerParams(vmem_limit_bytes=limit << 20),
        cost_estimate=COST,
    )(part_x, part_y, from_y, from_x)


def plane_scatter(multiply, left, fill=None, others=(), last=()):
    count = lax.axis_size("ctx")
    if count != 8:
        parts = multiply(left, BF)
        return lax.psum_scatter(parts, "ctx", scatter_dimension=0, tiled=True).astype(F32)
    rows = left.shape[0] // 8
    half = rows // 2
    give = multiply(left, BF, 1)
    got = swap(give, 1)
    keep = multiply(after(left, give), BF, 0)
    kept = sum_of(after([keep, got], others), BF, 60)
    sends = kept[3 * rows : -half], kept[-half:]
    from_y, from_x = swap(sends[0], 4), swap(sends[1], 2)
    from_y, from_x = after((from_y, from_x), fill(sends))
    part_x, part_y = add_diag(kept[rows : 2 * rows], kept[2 * rows : 3 * rows], from_y, from_x)
    got = after((swap(part_x, 2), swap(part_y, 4)), last)
    return kept[:rows].astype(F32) + got[0].astype(F32) + got[1].astype(F32)


class Order:
    def __init__(self, *values):
        self.last = values

    def take(self, value):
        return after(value, *self.last)

    def give(self, *values):
        self.last = values


def ring(value):
    count = lax.axis_size("wt")
    return lax.ppermute(value, "wt", [(i, (i + 1) % count) for i in range(count)])


def ring_chunks(block):
    chunks = [block]
    for _ in range(lax.axis_size("wt") - 1):
        chunks.append(ring(chunks[-1]))
    return chunks


def ring_sum(parts, kind):
    total = parts[1]
    for part in parts[2:] + parts[:1]:
        total = ring(total.astype(kind)).astype(F32) + part
    return total


def axis_sum(value, name):
    count = lax.axis_size(name)
    bit = 1
    while bit < count:
        value = value + lax.ppermute(value, name, [(i, i ^ bit) for i in range(count)])
        bit *= 2
    return value


def head_norm(raw, gain):
    scale = lax.rsqrt(jnp.mean(raw * raw, axis=-1, keepdims=True) + EPSILON)
    return raw * scale * gain


def turn(value):
    return pltpu.roll(value, value.shape[-1] // 2, 1)


def tile_mask(seg_col, seg_row, row_start, col_start):
    shape = (seg_col.shape[0], seg_row.shape[1])
    rows = lax.broadcasted_iota(jnp.int32, shape, 0) + row_start
    cols = lax.broadcasted_iota(jnp.int32, shape, 1) + col_start
    return (seg_col == seg_row) & (cols <= rows)


def attend_kernel(
    heads,
    pieces,
    block_ref,
    place_ref,
    first_ref,
    *refs,
):
    attend_body(heads, block_ref, place_ref, first_ref, refs[:pieces], *refs[pieces:])


def joined(refs, rows):
    group, have = [], 0
    for ref in refs:
        for start in range(0, ref.shape[0], rows):
            stop = min(start + rows, ref.shape[0])
            group.append(ref[start:stop])
            have += stop - start
            if have == rows:
                yield group[0] if len(group) == 1 else jnp.concatenate(group, axis=0)
                group, have = [], 0


def attend_body(
    heads,
    block_ref,
    place_ref,
    first_ref,
    hidden_refs,
    weight_ref,
    query_gain_ref,
    key_gain_ref,
    cosine_ref,
    sine_ref,
    seg_row_ref,
    seg_col_ref,
    query_ref,
    key_ref,
    value_ref,
    raw_ref,
    out_ref,
    score_ref,
):
    half = out_ref.shape[1]
    dim = query_gain_ref.shape[1]
    scale = dim ** (-0.5)

    for pair, lhs in enumerate(joined(hidden_refs, 4 * half)):
        raw = jnp.dot(lhs, weight_ref[...], preferred_element_type=F32)
        for piece in range(4):
            start = pl.multiple_of(block_ref[pair * 4 + piece] * half, half)
            spot = pl.ds(start, half)
            cosine, sine = cosine_ref[spot, :], sine_ref[spot, :]
            part = raw[piece * half : (piece + 1) * half]
            for head in range(heads + 1):
                cols = slice(head * dim, (head + 1) * dim)
                gain = query_gain_ref[...] if head < heads else key_gain_ref[...]
                normed = head_norm(part[:, cols], gain)
                roped = (normed * cosine + turn(normed) * sine).astype(BF)
                if head < heads:
                    query_ref[spot, cols] = roped
                else:
                    key_ref[spot, :] = roped
            raw_ref[spot, :] = part[:, : (heads + 1) * dim]
            value_ref[spot, :] = part[:, (heads + 1) * dim :].astype(BF)

    seq = key_ref.shape[0]
    stacked = heads * QUERY_ROWS

    def attend(index, carry):
        row_start = pl.multiple_of(index * QUERY_ROWS, QUERY_ROWS)
        row_spot = pl.ds(row_start, QUERY_ROWS)
        query = jnp.concatenate(
            [query_ref[row_spot, h * dim : (h + 1) * dim] for h in range(heads)], axis=0
        )
        seg_col = seg_col_ref[row_spot, :]
        low = first_ref[index] // KEY_ROWS
        high = (row_start + QUERY_ROWS + KEY_ROWS - 1) // KEY_ROWS

        def scores(tile, top):
            start = pl.multiple_of(tile * KEY_ROWS, KEY_ROWS)
            spot = pl.ds(start, KEY_ROWS)
            raw = lax.dot_general(
                query, key_ref[spot, :], (((1,), (1,)), ((), ())), preferred_element_type=F32
            )
            allowed = tile_mask(seg_col, seg_row_ref[:, spot], row_start, start)
            raw = raw.reshape(heads, QUERY_ROWS, KEY_ROWS) * scale
            masked = jnp.where(allowed[None], raw, MASKED).reshape(stacked, KEY_ROWS)
            score_ref[:, spot] = masked
            return jnp.maximum(top, jnp.max(masked, axis=1, keepdims=True))

        top = lax.fori_loop(low, high, scores, jnp.full((stacked, 1), MASKED, F32))

        def gather(tile, state):
            total, acc = state
            start = pl.multiple_of(tile * KEY_ROWS, KEY_ROWS)
            spot = pl.ds(start, KEY_ROWS)
            probs = jnp.exp(score_ref[:, spot] - top)
            total = total + jnp.sum(probs, axis=1, keepdims=True)
            acc = acc + jnp.dot(
                probs.astype(BF), value_ref[spot, :], preferred_element_type=F32
            )
            return total, acc

        total, acc = lax.fori_loop(
            low, high, gather, (jnp.zeros((stacked, 1), F32), jnp.zeros((stacked, dim), F32))
        )
        result = (acc / total).astype(BF)
        for head in range(heads):
            for piece in range(QUERY_ROWS // half):
                spot = place_ref[index * (QUERY_ROWS // half) + piece]
                begin = head * QUERY_ROWS + piece * half
                out_ref[spot, :, head * dim : (head + 1) * dim] = result[begin : begin + half]
        return carry

    lax.fori_loop(0, seq // QUERY_ROWS, attend, 0)


def attend_back_kernel(heads, pieces, place_ref, first_ref, *refs):
    attend_back_body(heads, place_ref, first_ref, refs[:pieces], *refs[pieces:])


def attend_back_body(
    heads,
    place_ref,
    first_ref,
    piece_refs,
    out_weight_ref,
    query_ref,
    key_ref,
    value_ref,
    raw_ref,
    query_gain_ref,
    key_gain_ref,
    cosine_ref,
    sine_ref,
    seg_row_ref,
    seg_col_ref,
    out_ref,
    query_gain_grad_ref,
    key_gain_grad_ref,
    score_ref,
    prob_grad_ref,
    key_grad_ref,
    value_grad_ref,
    grad_ref,
):
    half = grad_ref.shape[1]
    spot = 0
    for part in joined(piece_refs, 4 * half):
        part = lax.dot_general(
            part, out_weight_ref[...], (((1,), (1,)), ((), ())), preferred_element_type=F32
        ).astype(BF)
        for piece in range(4):
            grad_ref[spot] = part[piece * half : (piece + 1) * half]
            spot += 1
    dim = query_gain_ref.shape[1]
    scale = dim ** (-0.5)
    seq = key_ref.shape[0]
    stacked = heads * QUERY_ROWS
    pieces = QUERY_ROWS // half
    key_grad_ref[...] = jnp.zeros_like(key_grad_ref)
    value_grad_ref[...] = jnp.zeros_like(value_grad_ref)
    query_gain_grad_ref[...] = jnp.zeros_like(query_gain_grad_ref)
    key_gain_grad_ref[...] = jnp.zeros_like(key_gain_grad_ref)

    def unrope(grad, raw, gain, cosine, sine):
        norm_scale = lax.rsqrt(jnp.mean(raw * raw, axis=-1, keepdims=True) + EPSILON)
        unit = raw * norm_scale
        grad = grad * cosine + turn(grad * sine)
        gain_grad = jnp.sum(grad * unit, axis=0, keepdims=True)
        grad = grad * gain
        grad = norm_scale * (grad - unit * jnp.mean(grad * unit, axis=-1, keepdims=True))
        return grad, gain_grad

    def back(index, carry):
        row_start = pl.multiple_of(index * QUERY_ROWS, QUERY_ROWS)
        row_spot = pl.ds(row_start, QUERY_ROWS)
        places = [place_ref[index * pieces + piece] for piece in range(pieces)]
        query = jnp.concatenate(
            [query_ref[row_spot, h * dim : (h + 1) * dim] for h in range(heads)], axis=0
        )
        grad = jnp.concatenate(
            [
                grad_ref[place, :, h * dim : (h + 1) * dim]
                for h in range(heads)
                for place in places
            ],
            axis=0,
        )
        seg_col = seg_col_ref[row_spot, :]
        low = first_ref[index] // KEY_ROWS
        high = (row_start + QUERY_ROWS + KEY_ROWS - 1) // KEY_ROWS

        def scores(tile, top):
            start = pl.multiple_of(tile * KEY_ROWS, KEY_ROWS)
            spot = pl.ds(start, KEY_ROWS)
            raw = lax.dot_general(
                query, key_ref[spot, :], (((1,), (1,)), ((), ())), preferred_element_type=F32
            )
            allowed = tile_mask(seg_col, seg_row_ref[:, spot], row_start, start)
            raw = raw.reshape(heads, QUERY_ROWS, KEY_ROWS) * scale
            masked = jnp.where(allowed[None], raw, MASKED).reshape(stacked, KEY_ROWS)
            score_ref[:, spot] = masked
            return jnp.maximum(top, jnp.max(masked, axis=1, keepdims=True))

        top = lax.fori_loop(low, high, scores, jnp.full((stacked, 1), MASKED, F32))

        def probabilities(tile, state):
            total, inner = state
            start = pl.multiple_of(tile * KEY_ROWS, KEY_ROWS)
            spot = pl.ds(start, KEY_ROWS)
            probs = jnp.exp(score_ref[:, spot] - top)
            prob_grad = lax.dot_general(
                grad, value_ref[spot, :], (((1,), (1,)), ((), ())), preferred_element_type=F32
            )
            score_ref[:, spot] = probs
            prob_grad_ref[:, spot] = prob_grad
            total = total + jnp.sum(probs, axis=1, keepdims=True)
            inner = inner + jnp.sum(probs * prob_grad, axis=1, keepdims=True)
            return total, inner

        zero = jnp.zeros((stacked, 1), F32)
        total, inner = lax.fori_loop(low, high, probabilities, (zero, zero))
        share = 1.0 / total
        inner = inner * share

        def gradients(tile, acc):
            start = pl.multiple_of(tile * KEY_ROWS, KEY_ROWS)
            spot = pl.ds(start, KEY_ROWS)
            probs = score_ref[:, spot] * share
            score_grad = (probs * (prob_grad_ref[:, spot] - inner) * scale).astype(BF)
            acc = acc + jnp.dot(score_grad, key_ref[spot, :], preferred_element_type=F32)
            key_grad_ref[spot, :] += lax.dot_general(
                score_grad, query, (((0,), (0,)), ((), ())), preferred_element_type=F32
            )
            value_grad_ref[spot, :] += lax.dot_general(
                probs.astype(BF), grad, (((0,), (0,)), ((), ())), preferred_element_type=F32
            )
            return acc

        acc = lax.fori_loop(low, high, gradients, jnp.zeros((stacked, dim), F32))
        cosine, sine = cosine_ref[row_spot, :], sine_ref[row_spot, :]
        for head in range(heads):
            cols = slice(head * dim, (head + 1) * dim)
            part = acc[head * QUERY_ROWS : (head + 1) * QUERY_ROWS]
            part, gain_grad = unrope(
                part, raw_ref[row_spot, cols], query_gain_ref[...], cosine, sine
            )
            query_gain_grad_ref[...] += gain_grad
            part = part.astype(BF)
            for piece in range(pieces):
                out_ref[places[piece], :, cols] = part[piece * half : (piece + 1) * half]
        return carry

    lax.fori_loop(0, seq // QUERY_ROWS, back, 0)

    def finish(index, carry):
        row_start = pl.multiple_of(index * QUERY_ROWS, QUERY_ROWS)
        row_spot = pl.ds(row_start, QUERY_ROWS)
        key_cols = slice(heads * dim, (heads + 1) * dim)
        value_cols = slice((heads + 1) * dim, (heads + 2) * dim)
        part, gain_grad = unrope(
            key_grad_ref[row_spot, :],
            raw_ref[row_spot, key_cols],
            key_gain_ref[...],
            cosine_ref[row_spot, :],
            sine_ref[row_spot, :],
        )
        key_gain_grad_ref[...] += gain_grad
        part = part.astype(BF)
        value = value_grad_ref[row_spot, :].astype(BF)
        for piece in range(pieces):
            place = place_ref[index * pieces + piece]
            out_ref[place, :, key_cols] = part[piece * half : (piece + 1) * half]
            out_ref[place, :, value_cols] = value[piece * half : (piece + 1) * half]
        return carry

    lax.fori_loop(0, seq // QUERY_ROWS, finish, 0)


def one_hot(hit):
    return hit.astype(F32).astype(BF)


def select_kernel(groups, joint, *refs):
    target_ref, mine_ref, other_ref = refs[sum(groups) :]
    slots = mine_ref.shape[0] // 2
    target = target_ref[...]
    half = target.shape[1] // 8
    index = lax.broadcasted_iota(jnp.int32, (2 * slots, target.shape[1]), 0)
    pick = one_hot((index == target[0:1]) | (index == target[1:2]))
    for k in range(2):
        rows = []
        if joint:
            for ref in refs[: groups[0]]:
                for start in range(k * half, ref.shape[0], 2 * half):
                    rows.append(ref[start : start + half])
        else:
            first = k * groups[0]
            rows = [ref[...] for ref in refs[first : first + groups[k]]]
        picked = jnp.dot(pick, jnp.concatenate(rows, axis=0), preferred_element_type=F32)
        picked = picked.astype(BF)
        mine_ref[k * slots : (k + 1) * slots] = picked[:slots]
        other_ref[k * slots : (k + 1) * slots] = picked[slots:]


def select_rows(pieces, others, target, slots):
    width = pieces[0].shape[1]
    return pl.pallas_call(
        functools.partial(select_kernel, (len(pieces), len(others)), not others),
        out_shape=(jax.ShapeDtypeStruct((2 * slots, width), BF),) * 2,
        in_specs=[VMEM_SPEC] * (len(pieces) + len(others) + 1),
        out_specs=[VMEM_SPEC] * 2,
        compiler_params=pltpu.CompilerParams(vmem_limit_bytes=24 << 20),
        cost_estimate=COST,
    )(*pieces, *others, target)


def spread_kernel(chunks, part, grouped, *refs):
    mine_refs, other_refs = refs[:chunks], refs[chunks : 2 * chunks]
    target_ref, first_ref, second_ref = refs[2 * chunks : 2 * chunks + 3]
    outs = refs[2 * chunks + 3 :]
    slots = mine_refs[0].shape[0] // 2
    half = first_ref.shape[0] // chunks
    rows = 2 * half
    spot = slice(part * slots, (part + 1) * slots)
    for j in range(chunks):
        values = jnp.concatenate([mine_refs[j][spot], other_refs[j][spot]], axis=0)
        target = target_ref[j]
        index = lax.broadcasted_iota(jnp.int32, (4 * rows, 2 * slots), 1)
        pick = one_hot((index == target[:, 0:1]) | (index == target[:, 1:2]))
        spread = jnp.dot(pick, values, preferred_element_type=F32).astype(BF)
        for k in range(3):
            ref, start = (outs[k], j * rows) if grouped else (outs[3 * j + k], 0)
            ref[start : start + rows] = spread[k * rows : (k + 1) * rows]
        if grouped:
            ref = first_ref if 2 * j < chunks else second_ref
            start = j % (chunks // 2) * rows
            ref[start : start + rows] = spread[3 * rows :]
        else:
            first_ref[j * half : (j + 1) * half] = spread[3 * rows : 3 * rows + half]
            second_ref[j * half : (j + 1) * half] = spread[3 * rows + half :]


def spread_rows(mine, other, target, rows, part, grouped):
    chunks = len(mine)
    slots, width = mine[0].shape
    low = lambda count: jax.ShapeDtypeStruct((count, width), BF)
    blocks = (low(chunks * rows),) * 3 if grouped else (low(rows),) * (3 * chunks)
    outs = pl.pallas_call(
        functools.partial(spread_kernel, chunks, part, grouped),
        out_shape=(low(chunks * rows // 2),) * 2 + blocks,
        in_specs=[VMEM_SPEC] * (2 * chunks + 1),
        out_specs=[VMEM_SPEC] * (2 + len(blocks)),
        compiler_params=pltpu.CompilerParams(
            vmem_limit_bytes=(16 << 20) if chunks == 1 else (36 << 20)
        ),
        cost_estimate=COST,
    )(*mine, *other, target)
    return outs[:2], outs[2:]


def expert_kernel(expert_ref, mine_ref, other_ref, *refs):
    slots = mine_ref.shape[0] // 2
    rows, grads = slice(0, slots), slice(slots, 2 * slots)
    expert_body(
        expert_ref, mine_ref.at[rows], other_ref.at[rows], mine_ref.at[grads], other_ref.at[grads], *refs
    )


def expert_body(
    expert_ref,
    mine_ref,
    other_ref,
    grad_mine_ref,
    grad_other_ref,
    target_ref,
    route_ref,
    gate_ref,
    up_ref,
    down_ref,
    router_ref,
    back_mine_ref,
    back_other_ref,
    hidden_ref,
    gate_grad_ref,
    up_grad_ref,
    routed_ref,
    router_grad_ref,
):
    slots = mine_ref.shape[0]
    experts = router_ref.shape[0]
    tokens = target_ref.shape[1]
    rows = jnp.concatenate([mine_ref[...], other_ref[...]], axis=0)
    nt = (((1,), (1,)), ((), ()))
    tn = (((0,), (0,)), ((), ()))
    gate_pre = jnp.dot(rows, gate_ref[...], preferred_element_type=F32)
    up_pre = jnp.dot(rows, up_ref[...], preferred_element_type=F32)
    sigmoid = 1.0 / (1.0 + jnp.exp(-gate_pre))
    silu = gate_pre * sigmoid
    hidden = (silu * up_pre).astype(BF)
    hidden_ref[...] = hidden
    result = jnp.dot(hidden, down_ref[...], preferred_element_type=F32).astype(BF).astype(F32)
    slot_iota = lax.broadcasted_iota(jnp.int32, (slots, tokens), 0)
    expert_iota = lax.broadcasted_iota(jnp.int32, (experts, tokens), 0)
    masks = []
    for side in range(2):
        pick = one_hot(slot_iota == target_ref[side : side + 1, :])
        chosen = expert_iota == route_ref[side, 0:1, :]
        for k in range(1, route_ref.shape[1]):
            chosen = chosen | (expert_iota == route_ref[side, k : k + 1, :])
        masks.append(lax.dot_general(pick, one_hot(chosen), nt, preferred_element_type=F32))
    chosen = jnp.concatenate(masks, axis=0) > 0.5
    logits = lax.dot_general(rows, router_ref[...], nt, preferred_element_type=F32)
    top = jnp.max(jnp.where(chosen, logits, MASKED), axis=1, keepdims=True)
    weights = jnp.where(chosen, jnp.exp(logits - top), 0.0)
    total = jnp.sum(weights, axis=1, keepdims=True)
    gates = weights / jnp.where(total > 0.0, total, 1.0)
    mine = lax.broadcasted_iota(jnp.int32, gates.shape, 1) == expert_ref[0]
    gate = jnp.sum(jnp.where(mine, gates, 0.0), axis=1, keepdims=True)
    gated = (result * gate).astype(BF)
    back_mine_ref[slots:] = gated[:slots]
    back_other_ref[slots:] = gated[slots:]
    grad = jnp.concatenate([grad_mine_ref[...], grad_other_ref[...]], axis=0).astype(F32)
    gate_value_grad = jnp.sum(grad * result, axis=1, keepdims=True)
    routed = (grad * gate).astype(BF)
    routed_ref[...] = routed
    hidden_grad = lax.dot_general(routed, down_ref[...], nt, preferred_element_type=F32)
    gate_low = (hidden_grad * up_pre * sigmoid * (1.0 + gate_pre * (1.0 - sigmoid))).astype(BF)
    up_low = (hidden_grad * silu).astype(BF)
    gate_grad_ref[...] = gate_low
    up_grad_ref[...] = up_low
    logit_grad = (gate_value_grad * gate) * (jnp.where(mine, 1.0, 0.0) - gates)
    high = logit_grad.astype(BF)
    low = (logit_grad - high.astype(F32)).astype(BF)
    both = jnp.concatenate([high, low], axis=1)
    router = router_ref[...]
    slot_grad = lax.dot_general(gate_low, gate_ref[...], nt, preferred_element_type=F32)
    slot_grad = slot_grad + lax.dot_general(up_low, up_ref[...], nt, preferred_element_type=F32)
    slot_grad = slot_grad + jnp.dot(
        both, jnp.concatenate([router, router], axis=0), preferred_element_type=F32
    )
    slot_grad = slot_grad.astype(BF)
    back_mine_ref[:slots] = slot_grad[:slots]
    back_other_ref[:slots] = slot_grad[slots:]
    router_grad = lax.dot_general(both, rows, tn, preferred_element_type=F32)
    router_grad_ref[...] = router_grad[:experts] + router_grad[experts:]


def expert_rows(expert, mine, other, target, route, *weights):
    count, width = mine.shape
    ff = weights[0].shape[1]
    experts = weights[3].shape[0]
    low = lambda cols: jax.ShapeDtypeStruct((count, cols), BF)
    return pl.pallas_call(
        expert_kernel,
        out_shape=(
            low(width),
            low(width),
            low(ff),
            low(ff),
            low(ff),
            low(width),
            jax.ShapeDtypeStruct((experts, width), F32),
        ),
        in_specs=[SMEM_SPEC] + [VMEM_SPEC] * 8,
        out_specs=[VMEM_SPEC] * 7,
        compiler_params=pltpu.CompilerParams(vmem_limit_bytes=40 << 20),
        cost_estimate=COST,
    )(expert, mine, other, target, route, *weights)


def place_kernel(share, order_ref, owner_ref, part_ref, query_ref, key_ref, value_ref):
    cols = query_ref.shape[1]
    dim = key_ref.shape[1]
    part = part_ref[0]
    query_ref[...] = part[:, :cols].astype(F32)
    key = part[:, cols : cols + dim].astype(F32)
    value = part[:, cols + dim :].astype(F32)
    first = pl.program_id(0) % share == 0

    @pl.when(first)
    def _():
        key_ref[...] = key
        value_ref[...] = value

    @pl.when(jnp.logical_not(first))
    def _():
        key_ref[...] += key
        value_ref[...] += value


def place_weight_grads(parts, owner, share, dim):
    count, rows, width = parts.shape
    cols = width - 2 * dim
    if count == 8 and share == 2:
        order = jnp.asarray([0, 4, 1, 5, 2, 6, 3, 7], jnp.int32)
    else:
        order = jnp.arange(count, dtype=jnp.int32)
    owner = owner[order]
    group = lambda g, order, owner: (0, owner[g] // share)
    return pl.pallas_call(
        functools.partial(place_kernel, share),
        grid_spec=pltpu.PrefetchScalarGridSpec(
            num_scalar_prefetch=2,
            grid=(count,),
            in_specs=[pl.BlockSpec((1, rows, width), lambda g, order, owner: (order[g], 0, 0))],
            out_specs=[
                pl.BlockSpec((rows, cols), lambda g, order, owner: (0, owner[g])),
                pl.BlockSpec((rows, dim), group),
                pl.BlockSpec((rows, dim), group),
            ],
        ),
        out_shape=(
            jax.ShapeDtypeStruct((rows, cols * count), F32),
            jax.ShapeDtypeStruct((rows, dim * count // share), F32),
            jax.ShapeDtypeStruct((rows, dim * count // share), F32),
        ),
        compiler_params=pltpu.CompilerParams(vmem_limit_bytes=ATTEND_LIMIT),
        cost_estimate=COST,
    )(order, owner, parts)


def rows_kernel(owner_ref, part_ref, out_ref):
    out_ref[:, 0] = part_ref[0].astype(F32)


def place_rows(parts, owner):
    count, chunks, rows, width = parts.shape
    return pl.pallas_call(
        rows_kernel,
        grid_spec=pltpu.PrefetchScalarGridSpec(
            num_scalar_prefetch=1,
            grid=(count,),
            in_specs=[pl.BlockSpec((1, chunks, rows, width), lambda g, owner: (g, 0, 0, 0))],
            out_specs=pl.BlockSpec(
                (chunks, 1, rows, width), lambda g, owner: (0, owner[g], 0, 0)
            ),
        ),
        out_shape=jax.ShapeDtypeStruct((chunks, count, rows, width), F32),
        compiler_params=pltpu.CompilerParams(vmem_limit_bytes=ATTEND_LIMIT),
        cost_estimate=COST,
    )(owner, parts)


def place_pieces_kernel(share, owner_ref, *refs):
    pieces, (query_ref, key_ref, value_ref) = refs[:-3], refs[-3:]
    rows, dim = query_ref.shape[0], key_ref.shape[1] * share // 8
    cols = query_ref.shape[1] // 8
    for k in range(4):
        both = [
            [ref[...].astype(F32) for ref in refs_of]
            for refs_of in (block_refs(pieces, k), block_refs(pieces, k + 4))
        ]
        both = [p[0] if len(p) == 1 else jnp.concatenate(p, axis=0) for p in both]
        for side in range(2):
            start = pl.multiple_of(owner_ref[k + 4 * side] * cols, cols)
            query_ref[:, pl.ds(start, cols)] = both[side][:, :cols]
        start = pl.multiple_of(owner_ref[k] // share * dim, dim)
        key_ref[:, pl.ds(start, dim)] = both[0][:, cols : cols + dim] + both[1][:, cols : cols + dim]
        value_ref[:, pl.ds(start, dim)] = both[0][:, cols + dim :] + both[1][:, cols + dim :]


def block_refs(pieces, k):
    first = k // 4 * 5 + k % 4
    return pieces[first : first + 2] if k % 4 == 3 else pieces[first : first + 1]


def place_weight_pieces(pieces, owner, share, dim):
    rows, width = pieces[0].shape
    cols = width - 2 * dim
    return pl.pallas_call(
        functools.partial(place_pieces_kernel, share),
        out_shape=(
            jax.ShapeDtypeStruct((rows, cols * 8), F32),
            jax.ShapeDtypeStruct((rows, dim * 8 // share), F32),
            jax.ShapeDtypeStruct((rows, dim * 8 // share), F32),
        ),
        in_specs=[SMEM_SPEC] + [VMEM_SPEC] * len(pieces),
        out_specs=[VMEM_SPEC] * 3,
        compiler_params=pltpu.CompilerParams(vmem_limit_bytes=ATTEND_LIMIT),
        cost_estimate=COST,
    )(owner, *pieces)


def row_pieces_kernel(owner_ref, *refs):
    pieces, out_ref = refs[:-1], refs[-1]
    chunks, _, rows, _ = out_ref.shape
    for k in range(8):
        parts = [ref[...] for ref in block_refs(pieces, k)]
        part = parts[0] if len(parts) == 1 else jnp.concatenate(parts, axis=0)
        for chunk in range(chunks):
            out_ref[chunk, owner_ref[k]] = part[chunk * rows : (chunk + 1) * rows].astype(F32)


def place_row_pieces(pieces, owner, chunks):
    rows, width = pieces[0].shape
    return pl.pallas_call(
        row_pieces_kernel,
        out_shape=jax.ShapeDtypeStruct((chunks, 8, rows // chunks, width), F32),
        in_specs=[SMEM_SPEC] + [VMEM_SPEC] * len(pieces),
        out_specs=VMEM_SPEC,
        compiler_params=pltpu.CompilerParams(vmem_limit_bytes=ATTEND_LIMIT),
        cost_estimate=COST,
    )(owner, *pieces)


def product_kernel(dims, rows, left_count, right_count, starts, start_ref, *refs):
    lefts, rights = refs[:left_count], refs[left_count : left_count + right_count]
    outs = refs[left_count + right_count :]
    join = lambda parts: parts[0] if len(parts) == 1 else jnp.concatenate(parts, axis=0)
    right = join([ref[...] for ref in rights])
    for k, out_ref in enumerate(outs):
        if starts:
            width = out_ref.shape[0]
            cols = pl.ds(pl.multiple_of(start_ref[k] * width, width), width)
            left = join([ref[:, cols] for ref in lefts])
        else:
            left = join([ref[...] if rows is None else ref[:rows] for ref in lefts])
        out = lax.dot_general(left, right, (dims, ((), ())), preferred_element_type=F32)
        out_ref[...] = out.astype(out_ref.dtype)


def product(lefts, rights, dims, out_shape, kind=F32, rows=None, starts=None, limit=60, tile=None, block=None):
    count = 1 if starts is None else starts.shape[0]
    start_arg = jnp.zeros((1,), jnp.int32) if starts is None else starts
    if block is not None:
        left_specs = [pl.BlockSpec((rows, left.shape[1]), lambda i: (block, 0)) for left in lefts]
        right_specs = [pl.BlockSpec(right.shape, lambda i: (0, 0)) for right in rights]
        out_spec = pl.BlockSpec(out_shape, lambda i: (0, 0))
    elif tile is None:
        left_specs, right_specs = [VMEM_SPEC] * len(lefts), [VMEM_SPEC] * len(rights)
        out_spec = VMEM_SPEC
    else:
        left_specs = [
            pl.BlockSpec((rows or left.shape[0], tile), lambda i: (0, i)) for left in lefts
        ]
        right_specs = [pl.BlockSpec(right.shape, lambda i: (0, 0)) for right in rights]
        out_spec = pl.BlockSpec((tile, out_shape[1]), lambda i: (i, 0))
    outs = pl.pallas_call(
        functools.partial(
            product_kernel, dims, None, len(lefts), len(rights), starts is not None
        ),
        grid=(1,) if block is not None else () if tile is None else (out_shape[0] // tile,),
        out_shape=(jax.ShapeDtypeStruct(out_shape, kind),) * count,
        in_specs=[SMEM_SPEC] + left_specs + right_specs,
        out_specs=[out_spec] * count,
        compiler_params=pltpu.CompilerParams(vmem_limit_bytes=limit << 20),
        cost_estimate=COST,
    )(start_arg, *lefts, *rights)
    return outs[0] if starts is None else outs


def move_slots(slot_array):
    return lax.all_to_all(slot_array, ("ctx", "wt"), split_axis=0, concat_axis=0, tiled=True)


def local(
    tokens,
    cotangent,
    segments,
    routes,
    pair_order,
    attn_gain,
    ffn_gain,
    query_gain,
    key_gain,
    w_query,
    key_weight,
    value_weight,
    w_output,
    w_router,
    w_gate,
    w_up,
    w_down,
):
    ctx_count = lax.axis_size("ctx")
    wt_count = lax.axis_size("wt")
    me = lax.axis_index("ctx")
    plane = lax.axis_index("wt")
    inputs = tokens[0].astype(F32)
    tok_rows, model_width = inputs.shape
    half_rows = tok_rows // 2
    head_dim = query_gain.shape[0]
    experts = w_router.shape[1]
    top_count = routes.shape[2]
    seq_len = segments.shape[1]
    total_tokens = tok_rows * ctx_count * wt_count
    heads = w_query.shape[1] // head_dim // ctx_count
    kv_heads = key_weight.shape[1] // head_dim
    share = ctx_count // kv_heads
    head_cols = heads * head_dim
    group = me // share
    shard_width = model_width // wt_count
    capacity = max(2, half_rows * top_count * 5 // (4 * experts))
    dense = ctx_count == 8 and wt_count == 4 and w_gate.shape[0] == 1
    nt = (((1,), (1,)), ((), ()))
    tn = (((0,), (0,)), ((), ()))
    owners = block_owner(ctx_count, me)
    planes = (plane - jnp.arange(wt_count, dtype=jnp.int32)) % wt_count

    normed_one, attn_back = jax.vjp(rms_norm, inputs, attn_gain)
    normed_low = normed_one.astype(BF)
    kv_start = group * head_dim
    own_weight = jnp.concatenate(
        [
            lax.dynamic_slice_in_dim(w_query, me * head_cols, head_cols, 1),
            lax.dynamic_slice_in_dim(key_weight, kv_start, head_dim, 1),
            lax.dynamic_slice_in_dim(value_weight, kv_start, head_dim, 1),
        ],
        axis=1,
    )
    own_chunks = ctx_count // wt_count
    piece_rows = head_cols // ctx_count
    out_piece = lax.dynamic_index_in_dim(
        w_output.reshape(own_chunks, ctx_count, piece_rows, model_width), me, 1, keepdims=False
    )
    cot = cotangent[0]
    if dense:
        cap_rows = 2 * capacity
        slots = 4 * cap_rows
        expert = me * wt_count + plane
        triangle = jnp.triu(jnp.ones((tok_rows, tok_rows), F32)).astype(BF)
        offsets = (jnp.arange(ctx_count, dtype=jnp.int32) % 4) * cap_rows

        def tables(near):
            near = near.astype(jnp.int32).reshape(-1, ctx_count, top_count, tok_rows)

            def slot_of(routed_to):
                hits = jnp.any(near == routed_to, axis=2)
                ranks = jnp.dot(hits.astype(BF), triangle, preferred_element_type=F32)
                place = ranks.astype(jnp.int32) - 1 + offsets[None, :, None]
                return jnp.where(hits, place, -1).reshape(-1, 2, 4 * tok_rows)

            own_slot = slot_of(expert)
            other_slot = slot_of((me ^ 1) * wt_count + plane)[:, 0]
            target = jnp.stack(
                [own_slot[:, 0], jnp.where(other_slot < 0, -1, other_slot + slots)], axis=1
            )
            near_routes = (
                near.reshape(-1, 2, 4, top_count, tok_rows)
                .transpose(0, 1, 3, 2, 4)
                .reshape(-1, 2, top_count, 4 * tok_rows)
            )
            indices = jnp.arange(experts, dtype=jnp.int32)[:, None, None, None, None]
            counts = jnp.sum((near[None] == indices).astype(F32), axis=(1, 2, 3, 4))
            return own_slot, target, target.transpose(0, 2, 1), near_routes, counts

        block_rows = own_chunks * piece_rows
        out_piece = out_piece.reshape(block_rows, model_width)
        ticks = [(out_piece, own_weight), (ring(out_piece), ring(own_weight))]
        own = after(normed_low, out_piece, own_weight)
        via_x, via_y = swap(own, 2), swap(own, 4)
        near = after(routes[0].T.astype(BF), own)
        near_x, near_y = swap(near, 2), swap(near, 4)
        sent = via_x[:half_rows], via_y[half_rows:]
        diag_a, diag_b = swap(sent[0], 4), swap(sent[1], 2)
        near_x, near_y = after((near_x, near_y), sent)
        near = jnp.concatenate([near, near_x, near_y, swap(near_x, 4)], axis=0)
        near = jnp.concatenate([near, swap(near, 1)], axis=0)
        hidden_pieces = [own, via_x, via_y, diag_a, diag_b]
        hidden_pieces = hidden_pieces + [swap(piece, 1) for piece in hidden_pieces]
        ticks[1], near, cot_block = after((ticks[1], near, cot), ticks[1], hidden_pieces, near)
        near_rows = near.shape[0]
        tiny = jnp.concatenate([near, w_router.T.reshape(-1, tok_rows)], axis=0)
        tinies = [tiny, ring(tiny)]
        cot_x, cot_y = swap(cot_block, 2), swap(cot_block, 4)
        ticks.append((ring(ticks[1][0]), ring(ticks[1][1])))
        first_tables = tables(near)
        zero = ticks[1][0][0, 0].astype(F32) * 0.0
        tables_done = cosine, sine = rope_tables(seq_len, head_dim, zero)
        def keep(j, buffers, shards):
            put = lax.dynamic_update_slice_in_dim
            return (
                put(buffers[0], shards[0], planes[j] * block_rows, 0),
                put(buffers[1], shards[1], planes[j] * shard_width, 0),
            )

        cot_sent = cot_x[:half_rows], cot_y[half_rows:]
        ticks[2], cot_sent, tinies[1] = after(
            (ticks[2], cot_sent, tinies[1]), ticks[2], cot_sent, tinies[1], first_tables, tables_done
        )
        ticks.append((ring(ticks[2][0]), ring(ticks[2][1])))
        tinies.append(ring(tinies[1]))
        diag_a, diag_b = swap(cot_sent[0], 4), swap(cot_sent[1], 2)
        seed = ticks[2][0][:1, :1] * 0
        buffers = (
            jnp.broadcast_to(seed, (ctx_count * piece_rows, model_width)),
            jnp.broadcast_to(seed, (model_width, own_weight.shape[1])),
        )

        for j in range(3):
            buffers = keep(j, buffers, ticks[j])
        cot_pieces = [cot, cot_x, cot_y, diag_a, diag_b]
        cot_diag = jnp.concatenate([diag_a, diag_b], axis=0)
        ticks[3] = after(ticks[3], cot_diag, tinies[2], buffers)
        out_pieces, weight = keep(3, buffers, ticks[3])
        tinies.append(ring(after(tinies[2], weight)))
        cot_next = [ring(after(p, weight)) for p in (cot, cot_x, cot_y, cot_diag)]
        tinies_later = tinies[1:]
        router = jnp.stack([tiny[near_rows:].reshape(experts, shard_width) for tiny in tinies])
        router = router[planes].transpose(1, 0, 2).reshape(experts, model_width)
    else:
        hidden_pieces = plane_gather(normed_low)
        out_pieces = lax.all_gather(out_piece, "wt", axis=0, tiled=True)
        weight = lax.all_gather(own_weight, "wt", axis=0, tiled=True)
        router = lax.all_gather(w_router, "wt", axis=0, tiled=True).T
        cosine, sine = rope_tables(seq_len, head_dim, 0.0)
    out_weight = lax.all_to_all(
        out_pieces.reshape(ctx_count, piece_rows, model_width), "ctx", 0, 0, tiled=True
    ).reshape(head_cols, model_width)

    owner_pair = pair_order[owners]
    blocks = jnp.stack([owner_pair, 2 * ctx_count - 1 - owner_pair], 1).reshape(-1)
    order = jnp.arange(2 * ctx_count, dtype=jnp.int32)
    places = jnp.sum(jnp.where(blocks[:, None] == order[None, :], order[:, None], 0), axis=0)
    places = places.astype(jnp.int32)
    seg = segments[0]
    first = jnp.sum(
        (seg[None, :] < seg[::QUERY_ROWS][:, None]).astype(jnp.int32), axis=1
    ).astype(jnp.int32)
    seg_row, seg_col = seg.reshape(1, seq_len), seg.reshape(seq_len, 1)
    query_gain_row, key_gain_row = query_gain.reshape(1, -1), key_gain.reshape(1, -1)

    width = head_cols + 2 * head_dim
    stacked = heads * QUERY_ROWS
    piece_count = len(hidden_pieces)
    query, key, value, raw, attn_low = pl.pallas_call(
        functools.partial(attend_kernel, heads, piece_count),
        out_shape=(
            jax.ShapeDtypeStruct((seq_len, head_cols), BF),
            jax.ShapeDtypeStruct((seq_len, head_dim), BF),
            jax.ShapeDtypeStruct((seq_len, head_dim), BF),
            jax.ShapeDtypeStruct((seq_len, head_cols + head_dim), F32),
            jax.ShapeDtypeStruct((2 * ctx_count, half_rows, head_cols), BF),
        ),
        in_specs=[SMEM_SPEC] * 3 + [VMEM_SPEC] * (7 + piece_count),
        out_specs=[VMEM_SPEC] * 5,
        scratch_shapes=[pltpu.VMEM((stacked, seq_len), F32)],
        compiler_params=pltpu.CompilerParams(vmem_limit_bytes=ATTEND_LIMIT),
        cost_estimate=COST,
    )(
        blocks,
        places,
        first,
        *hidden_pieces,
        weight,
        query_gain_row,
        key_gain_row,
        cosine,
        sine,
        seg_row,
        seg_col,
    )
    attn_rows = attn_low.reshape(seq_len, head_cols)
    later_tables = []
    out_project = lambda rows, kind: low_matmul(rows, out_weight).astype(kind)
    if dense:
        attn_rows = after(attn_rows, cot_next[0])
        side = seq_len // 2

        def out_project(rows, kind, block):
            shape = (side, model_width)
            return product([rows], [out_weight], ((1,), (0,)), shape, kind, side, block=block)


        def fill(sends):
            later_tables.extend(tables(jnp.concatenate([t[:near_rows] for t in after(tinies_later, sends)], axis=0)))
            return tuple(later_tables) + (cot_next[2],)

        attn = plane_scatter(out_project, attn_rows, fill, (cot_next[1],), (cot_next[3],))
    else:
        attn = plane_scatter(out_project, attn_rows)
    residual = inputs + attn
    normed_two, ffn_back = jax.vjp(rms_norm, residual, ffn_gain)
    normed_two_low = normed_two.astype(BF)
    grad_out = cotangent[0].astype(F32)
    if dense:
        own_slot, target_rows, target_cols, near_routes = (
            jnp.concatenate([f, r], axis=0) for f, r in zip(first_tables[:4], later_tables[:4])
        )
        counts = first_tables[4] + later_tables[4]
        logits = lax.dot_general(normed_two_low, router, nt, preferred_element_type=F32)
        router_probs = jax.nn.softmax(logits, axis=-1)
        shares = counts / (total_tokens * top_count)
        prob_grad = (experts * shares / total_tokens)[None, :]
        logits_grad = router_probs * (
            prob_grad - jnp.sum(router_probs * prob_grad, axis=1, keepdims=True)
        )
        logits_grad_low = logits_grad.astype(BF)
        last = wt_count - 1
        mine_backs, other_backs, results = [], [], []

        def compute(j, pieces, others, gates, second=()):
            pieces = after(pieces, *gates)
            mine, other = select_rows(pieces, others, target_rows[j], slots)
            received = after(swap(other, 1), second)
            result = expert_rows(
                expert.reshape(1),
                mine,
                received,
                own_slot[j],
                near_routes[j],
                w_gate[0],
                w_up[0],
                w_down[0],
                router,
            )
            mine_backs.append(result[0])
            other_backs.append(swap(result[1], 1))
            results.append((mine, received) + tuple(result[2:]))
            return result[0]

        payload, before, done = normed_two_low, None, None
        for j in range(wt_count):
            if j == 2:
                cot_own = cot_next[0]
                halves = payload[:half_rows], cot_own[:half_rows], payload[half_rows:], cot_own[half_rows:]
                payload = jnp.concatenate(halves, axis=0)
            if j > 0:
                payload = ring(payload)
            block = payload if j == 0 else after(payload, before[3:])
            via_x, via_y = swap(block, 2), swap(block, 4)
            if done is not None:
                via_x, via_y = after((via_x, via_y), done)
            middle = via_x.shape[0] // 2
            sent = via_x[:middle], via_y[middle:]
            pieces = [block, via_x, via_y, swap(sent[0], 4), swap(sent[1], 2)]
            if before is not None:
                done = compute(j - 1, before, [cot_pieces, cot_next, []][j - 1], (sent,), pieces[3:])
            before = pieces
        group_sent, blocks = spread_rows(
            mine_backs, other_backs, target_cols[:last], tok_rows, 0, False
        )
        group_sent = after(group_sent, sent)
        group_diag = swap(group_sent[0], 4), swap(group_sent[1], 2)
        done = compute(last, pieces, [], (done,), group_sent)
        step = Order(done)

        def add_chunk(own, part_x, part_y, from_y, from_x):
            part_x, part_y, from_y, from_x = step.take((part_x, part_y, from_y, from_x))
            part_x, part_y = add_diag(part_x, part_y, from_y, from_x)
            step.give(part_x, part_y)
            return own, swap(part_x, 2), swap(part_y, 4)

        def chunk_sum(own, got_x, got_y):
            return [own] + list(step.take((got_x, got_y)))

        def chunk_diag(j):
            return [part[j * half_rows : (j + 1) * half_rows] for part in group_diag]

        partial = {j: add_chunk(*blocks[3 * j : 3 * j + 3], *chunk_diag(j)) for j in range(1, last)}
        tail_sent, tail = spread_rows(
            step.take(mine_backs[last:]), other_backs[last:], target_cols[last:], tok_rows, 0, False
        )
        step.give(tail_sent)
        tail_diag = swap(tail_sent[0], 4), swap(tail_sent[1], 2)
        rows_all = [r for res in results for r in res[:2]]
        hidden_low, gate_low, up_low, routed = ([res[k] for res in results] for k in range(2, 6))
        ff = w_gate.shape[2]
        grad_w_gate = product(step.take(rows_all), gate_low, ((0,), (0,)), (model_width, ff), F32, slots, tile=512, limit=40)
        step.give(grad_w_gate)
        total = sum_of(chunk_sum(*partial[1]), BF)
        step.give(total)
        total = ring(total)
        grad_w_up = product(step.take(rows_all), up_low, ((0,), (0,)), (model_width, ff), F32, slots, tile=512, limit=40)
        step.give(grad_w_up)
        for j in range(2, last):
            total = sum_of([step.take(total)] + chunk_sum(*partial[j]), BF)
            step.give(total)
            total = ring(total)
        partial[last] = add_chunk(*tail, *tail_diag)
        partial[0] = add_chunk(*blocks[:3], *chunk_diag(0))
        grad_w_down = product(
            step.take(hidden_low), routed, ((0,), (0,)), (ff, model_width), F32, tile=256, limit=40
        )
        step.give(grad_w_down)
        total = sum_of([step.take(total)] + chunk_sum(*partial[last]), BF)
        step.give(total)
        total = ring(total)
        out_sent, out_blocks = spread_rows(
            step.take(mine_backs), other_backs, target_cols, tok_rows, 1, True
        )
        step.give(out_sent)
        total = sum_of([step.take(total)] + chunk_sum(*partial[0]), F32)
        grad_normed_two = total + jnp.dot(logits_grad_low, router, preferred_element_type=F32)
        grad_w_gate, grad_w_up, grad_w_down = grad_w_gate[None], grad_w_up[None], grad_w_down[None]
        router_grad = sum(res[6] for res in results) + lax.dot_general(
            logits_grad_low, normed_two_low, tn, preferred_element_type=F32
        )
    else:
        w_router_all = router.T
        slot_rows = 2 * capacity
        local_experts = w_gate.shape[0]
        logits = low_matmul(normed_two_low, w_router_all)
        local_routes = routes[0]

        def router_fn(logit_values):
            router_probs = jax.nn.softmax(logit_values, axis=-1)
            chosen = jnp.take_along_axis(router_probs, local_routes, axis=1)
            return (chosen / jnp.sum(chosen, axis=1, keepdims=True), router_probs)

        (gate_values, router_probs), router_back = jax.vjp(router_fn, logits)
        route_flat = local_routes.reshape(-1)
        route_hits = (route_flat[:, None] == jnp.arange(experts, dtype=jnp.int32)[None, :]).astype(
            jnp.int32
        )
        counts = lax.psum(jnp.sum(route_hits, axis=0).astype(jnp.float32), ("ctx", "wt"))
        shares = counts / (total_tokens * top_count)
        halves = route_hits.reshape(2, half_rows * top_count, experts)
        ranks = jnp.sum((jnp.cumsum(halves, axis=1) - halves) * halves, axis=2).reshape(-1)
        half_index = jnp.arange(tok_rows * top_count, dtype=jnp.int32) // (half_rows * top_count)
        slot_index = route_flat * slot_rows + half_index * capacity + ranks
        slot_owner = (
            jnp.full((experts * slot_rows,), tok_rows * top_count, jnp.int32)
            .at[slot_index]
            .set(jnp.arange(tok_rows * top_count, dtype=jnp.int32))
        )
        slot_shape = (experts // local_experts, local_experts, slot_rows, model_width)
        padded = jnp.concatenate([normed_two_low, jnp.zeros((1, model_width), jnp.bfloat16)], axis=0)
        outgoing = padded[slot_owner // top_count].reshape(slot_shape)
        arrived = move_slots(outgoing)
        gate_pre = jnp.einsum("nesd,edf->nesf", arrived, w_gate, preferred_element_type=jnp.float32)
        up_pre = jnp.einsum("nesd,edf->nesf", arrived, w_up, preferred_element_type=jnp.float32)
        hidden_low, swiglu_back = jax.vjp(swiglu, gate_pre, up_pre)
        hidden_low = hidden_low.astype(jnp.bfloat16)
        expert_out = jnp.einsum(
            "nesf,efd->nesd", hidden_low, w_down, preferred_element_type=jnp.float32
        ).astype(jnp.bfloat16)
        returned = move_slots(expert_out).reshape(experts * slot_rows, model_width)
        picked = returned[slot_index].reshape(tok_rows, top_count, model_width)
        mixture = jnp.einsum("tk,tkd->td", gate_values, picked, preferred_element_type=jnp.float32)
        output = (residual + mixture).astype(jnp.bfloat16)
        grad_gates = jnp.einsum("td,tkd->tk", grad_out, picked, preferred_element_type=jnp.float32)
        grad_routed = (
            (gate_values[:, :, None] * grad_out[:, None, :])
            .astype(jnp.bfloat16)
            .reshape(-1, model_width)
        )
        grad_routed = jnp.concatenate([grad_routed, jnp.zeros((1, model_width), jnp.bfloat16)], axis=0)
        grad_arrived = move_slots(grad_routed[slot_owner].reshape(slot_shape))
        grad_hidden = jnp.einsum(
            "nesd,efd->nesf", grad_arrived, w_down, preferred_element_type=jnp.float32
        )
        grad_w_down = jnp.einsum(
            "nesf,nesd->efd", hidden_low, grad_arrived, preferred_element_type=jnp.float32
        )
        grad_gate_pre, grad_up_pre = swiglu_back(grad_hidden)
        gate_grad_low = grad_gate_pre.astype(jnp.bfloat16)
        up_grad_low = grad_up_pre.astype(jnp.bfloat16)
        grad_w_gate = jnp.einsum(
            "nesd,nesf->edf", arrived, gate_grad_low, preferred_element_type=jnp.float32
        )
        grad_w_up = jnp.einsum(
            "nesd,nesf->edf", arrived, up_grad_low, preferred_element_type=jnp.float32
        )
        grad_slots = (
            jnp.einsum("nesf,edf->nesd", gate_grad_low, w_gate, preferred_element_type=jnp.float32)
            + jnp.einsum("nesf,edf->nesd", up_grad_low, w_up, preferred_element_type=jnp.float32)
        ).astype(jnp.bfloat16)
        grad_back = move_slots(grad_slots).reshape(experts * slot_rows, model_width)
        grad_normed_two = jnp.sum(
            grad_back[slot_index].reshape(tok_rows, top_count, model_width).astype(jnp.float32), axis=1
        )
        prob_grad = jnp.broadcast_to(experts * shares / total_tokens, router_probs.shape)
        (grad_logits,) = router_back((grad_gates, prob_grad))
        logits_low = grad_logits.astype(jnp.bfloat16)
        grad_normed_two = grad_normed_two + jnp.einsum(
            "te,de->td", logits_low, w_router_all, preferred_element_type=jnp.float32
        )
        grad_w_router = jnp.einsum(
            "td,te->de", normed_two_low, logits_low, preferred_element_type=jnp.float32
        )
        router_grad = grad_w_router.T
    grad_residual_part, grad_ffn_gain = ffn_back(grad_normed_two)
    grad_residual = grad_out + grad_residual_part
    grad_pieces = plane_gather(grad_residual.astype(BF))
    if dense:
        out_sent = after(out_sent, grad_pieces)
        out_diag = swap(out_sent[0], 4), swap(out_sent[1], 2)
        query = after(query, out_sent)
    head_grads, grad_query_gain, grad_key_gain = pl.pallas_call(
        functools.partial(attend_back_kernel, heads, piece_count),
        out_shape=(
            jax.ShapeDtypeStruct((2 * ctx_count, half_rows, width), BF),
            jax.ShapeDtypeStruct((1, head_dim), F32),
            jax.ShapeDtypeStruct((1, head_dim), F32),
        ),
        in_specs=[SMEM_SPEC] * 2 + [VMEM_SPEC] * (11 + piece_count),
        out_specs=[VMEM_SPEC] * 3,
        scratch_shapes=[
            pltpu.VMEM((stacked, seq_len), F32),
            pltpu.VMEM((stacked, seq_len), F32),
            pltpu.VMEM((seq_len, head_dim), F32),
            pltpu.VMEM((seq_len, head_dim), F32),
            pltpu.VMEM((2 * ctx_count, half_rows, head_cols), BF),
        ],
        compiler_params=pltpu.CompilerParams(vmem_limit_bytes=ATTEND_LIMIT),
        cost_estimate=COST,
    )(
        places,
        first,
        *grad_pieces,
        out_weight,
        query,
        key,
        value,
        raw,
        query_gain_row,
        key_gain_row,
        cosine,
        sine,
        seg_row,
        seg_col,
    )
    head_grads = head_grads.reshape(seq_len, width)
    heads_back = lambda rows, kind: lax.dot_general(
        rows, weight, nt, preferred_element_type=F32
    ).astype(kind)
    if dense:
        step = Order(out_diag)

        def weight_parts(places, kind):
            return product(
                hidden_pieces,
                [step.take(head_grads)],
                ((0,), (0,)),
                (shard_width, width),
                kind,
                starts=places,
            )

        def add_send(got, part, kind=BF):
            total = sum_of([step.take(got), part], kind, 60)
            step.give(total)
            return ring(total)

        (first,) = weight_parts(planes[1:2], BF)
        step.give(first)
        total = ring(first)
        out_x, out_y = add_diag(
            *step.take((out_blocks[1], out_blocks[2])), *step.take(out_diag), 60
        )
        step.give(out_x, out_y)
        out_got = swap(out_x, 2), swap(out_y, 4)
        more = weight_parts(planes[jnp.asarray([2, 3, 0])], F32)
        step.give(more)
        total = add_send(total, more[0])
        out_grad = product(
            [step.take(attn_rows)], grad_pieces, ((0,), (0,)), (head_cols, model_width), BF
        )
        step.give(out_grad)
        out_grad = lax.all_to_all(
            out_grad.reshape(ctx_count, piece_rows, model_width), "ctx", 0, 0, tiled=True
        )
        total = add_send(total, more[1])
        shape = (side, model_width)
        give = product(
            [step.take(head_grads)], [weight], ((1,), (1,)), shape, BF, side, block=1
        )
        step.give(give)
        got = swap(give, 1)
        keep_part = product(
            [step.take(head_grads)], [weight], ((1,), (1,)), shape, BF, side, block=0
        )
        step.give(keep_part)
        sums = sum_of([out_blocks[0]] + list(step.take(out_got)), F32, 60)
        step.give(sums)
        sums = sums.reshape(wt_count, tok_rows, model_width)
        weight_grad = sum_of([step.take(total), more[2]], BF, 60)
        step.give(weight_grad)
        weight_x, weight_y = swap(weight_grad, 2), swap(weight_grad, 4)
        kept = sum_of([keep_part, step.take(got)], BF, 60)
        kept_sent = kept[3 * tok_rows : -half_rows], kept[-half_rows:]
        step.give(kept_sent)
        kept_diag = swap(kept_sent[0], 4), swap(kept_sent[1], 2)
        out_parts = step.take(out_grad).reshape(wt_count, block_rows, model_width)
        out_parts = [
            lax.dynamic_index_in_dim(out_parts, planes[j], 0, keepdims=False)
            for j in range(wt_count)
        ]
        step.give(out_parts[1])
        out_total = ring(out_parts[1])
        mixed_low = step.take(sums[1]).astype(BF)
        step.give(mixed_low)
        mixed_total = ring(mixed_low)
        half = weight_grad.shape[0] // 2
        weight_x, weight_y = step.take((weight_x, weight_y))
        weight_sent = weight_x[:half], weight_y[half:]
        step.give(weight_sent)
        weight_pieces = [
            weight_grad,
            weight_x,
            weight_y,
            swap(weight_sent[0], 4),
            swap(weight_sent[1], 2),
        ]
        weight_pieces = weight_pieces + [swap(piece, 1) for piece in weight_pieces]
        out_total = add_send(out_total, out_parts[2])
        kept_x, kept_y = add_diag(
            kept[tok_rows : 2 * tok_rows],
            kept[2 * tok_rows : 3 * tok_rows],
            *step.take(kept_diag),
            60,
        )
        step.give(kept_x, kept_y)
        kept_got = swap(kept_x, 2), swap(kept_y, 4)
        out_total = add_send(out_total, out_parts[3])
        mixed_total = add_send(mixed_total, sums[2])
        kept_got = step.take(kept_got)
        grad_normed_one = sum_of([kept[:tok_rows]] + list(kept_got), F32, 60)
        step.give(grad_normed_one)
        out_total = sum_of([step.take(out_total), out_parts[0]], BF, 60)
        step.give(out_total)
        out_x, out_y = swap(out_total, 2), swap(out_total, 4)
    else:
        out_grad = lax.dot_general(
            attn_rows, jnp.concatenate(grad_pieces, axis=0), tn, preferred_element_type=F32
        ).astype(BF)
        out_grad = lax.all_to_all(
            out_grad.reshape(ctx_count, piece_rows, model_width), "ctx", 0, 0, tiled=True
        )
        hidden_rows = jnp.concatenate(hidden_pieces, axis=0)
        weight_grad = lax.dot_general(hidden_rows, head_grads, tn, preferred_element_type=F32)
        weight_grad = lax.psum_scatter(
            weight_grad.astype(BF), "wt", scatter_dimension=0, tiled=True
        )
        weight_grads = jnp.concatenate(plane_gather(weight_grad), axis=0)
        grad_w_query, grad_w_key, grad_w_value = place_weight_grads(
            weight_grads.reshape(ctx_count, -1, width), owners, share, head_dim
        )
        out_grad = lax.psum_scatter(out_grad, "wt", scatter_dimension=0, tiled=True)
        out_grads = jnp.concatenate(plane_gather(out_grad.reshape(-1, model_width)), axis=0)
        grad_w_output = place_rows(
            out_grads.reshape(ctx_count, own_chunks, piece_rows, model_width), owners
        ).reshape(w_output.shape)
        grad_normed_one = plane_scatter(heads_back, head_grads)
    grad_inputs_part, grad_attn_gain = attn_back(grad_normed_one)
    grad_inputs = grad_residual + grad_inputs_part

    part = head_dim // wt_count
    prob_sums = jnp.sum(router_probs, axis=0)
    prob_row = jnp.zeros((shard_width - 2 * part,), F32)
    if dense:
        prob_row = lax.dynamic_update_slice_in_dim(prob_row, prob_sums, plane * experts, 0)
    gains = jnp.concatenate(
        [
            grad_query_gain.reshape(wt_count, part),
            grad_key_gain.reshape(wt_count, part),
            jnp.broadcast_to(prob_row[None], (wt_count, shard_width - 2 * part)),
        ],
        axis=1,
    )
    small = jnp.concatenate([router_grad, grad_ffn_gain[None], grad_attn_gain[None]], axis=0)
    small = small.reshape(experts + 2, wt_count, shard_width).transpose(1, 0, 2)
    small = jnp.concatenate([small, gains[:, None]], axis=1)[planes]
    if dense:
        small_low = step.take(small[1])
        step.give(small_low)
        small_total = ring(small_low)
        mixed_total = add_send(mixed_total, sums[3])
        grad_w_query, grad_w_key, grad_w_value = place_weight_pieces(
            step.take(weight_pieces), owners, share, head_dim
        )
        step.give(grad_w_value)
        out_x, out_y = step.take((out_x, out_y))
        half = out_total.shape[0] // 2
        out_sent = out_x[:half], out_y[half:]
        step.give(out_sent)
        out_pieces = [out_total, out_x, out_y, swap(out_sent[0], 4), swap(out_sent[1], 2)]
        out_pieces = out_pieces + [swap(piece, 1) for piece in out_pieces]
        small_total = add_send(small_total, small[2], F32)
        grad_w_output = place_row_pieces(step.take(out_pieces), owners, own_chunks)
        step.give(grad_w_output)
        grad_w_output = grad_w_output.reshape(w_output.shape)
        small_total = add_send(small_total, small[3], F32)
        output = step.take(mixed_total).astype(F32) + sums[0]
        output = (residual + output).astype(BF)
        step.give(output)
        small = axis_sum(step.take(small_total) + small[0], "ctx")
    else:
        small = ring_sum([small[j] for j in range(wt_count)], F32)
        small = axis_sum(small, "ctx")
    if dense:
        prob_sums = small[experts + 2, 2 * part : 2 * part + wt_count * experts]
        prob_sums = jnp.sum(prob_sums.reshape(wt_count, experts), axis=0)
    else:
        prob_sums = axis_sum(axis_sum(prob_sums[None], "ctx"), "wt")[0]
    balance = experts * experts * shares * (prob_sums / total_tokens)
    loss_value = jnp.mean(balance)
    return (
        output[None],
        loss_value,
        balance,
        grad_inputs[None],
        small[experts + 1],
        small[experts],
        small[experts + 2, :part],
        small[experts + 2, part : 2 * part],
        grad_w_query,
        grad_w_key,
        grad_w_value,
        grad_w_output,
        small[:experts].T,
        grad_w_gate,
        grad_w_up,
        grad_w_down,
    )


def solution(mesh):
    in_specs = (
        P("wt", "ctx", None),
        P("wt", "ctx", None),
        P("wt", None),
        P("wt", "ctx", None),
        P(),
        P(),
        P(),
        P(),
        P(),
        P("wt", None),
        P("wt", None),
        P("wt", None),
        P("wt", None),
        P("wt", None),
        P(("ctx", "wt"), None, None),
        P(("ctx", "wt"), None, None),
        P(("ctx", "wt"), None, None),
    )
    out_specs = (
        P("wt", "ctx", None),
        P(),
        P(),
        P("wt", "ctx", None),
        P("wt"),
        P("wt"),
        P("wt"),
        P("wt"),
        P("wt", None),
        P("wt", None),
        P("wt", None),
        P("wt", None),
        P("wt", None),
        P(("ctx", "wt"), None, None),
        P(("ctx", "wt"), None, None),
        P(("ctx", "wt"), None, None),
    )
    return jax.shard_map(local, mesh=mesh, in_specs=in_specs, out_specs=out_specs, check_vma=False)
```

```python
import functools

import jax
import jax.numpy as jnp
from jax import lax
from jax.experimental import pallas as pl
from jax.experimental.pallas import tpu as pltpu
from jax.sharding import PartitionSpec as P

EPSILON = 1e-06
ROPE_BASE = 1000000.0
MASKED = -1e30
BF = jnp.bfloat16
F32 = jnp.float32
VMEM_SPEC = pl.BlockSpec(memory_space=pltpu.VMEM)
SMEM_SPEC = pl.BlockSpec(memory_space=pltpu.SMEM)
QUERY_ROWS = 128
KEY_ROWS = 256
ATTEND_LIMIT = 60 << 20
COST = pl.CostEstimate(flops=1, bytes_accessed=1, transcendentals=0)


def rms_norm(value_vectors, gain_vector):
    return (
        value_vectors
        * lax.rsqrt(jnp.mean(value_vectors * value_vectors, axis=-1, keepdims=True) + EPSILON)
        * gain_vector
    )


def low_matmul(left, right):
    return jnp.dot(left, right, preferred_element_type=F32)


def swiglu(gate_pre, up_pre):
    return jax.nn.silu(gate_pre) * up_pre


def rope_tables(length, head_width, zero):
    inv_freq = ROPE_BASE ** (-jnp.arange(0, head_width // 2, dtype=F32) * 2.0 / head_width)
    angle_table = (jnp.arange(length, dtype=F32) + zero)[:, None] * inv_freq[None, :]
    cosine, sine = jnp.cos(angle_table), jnp.sin(angle_table)
    return jnp.concatenate([cosine, cosine], 1), jnp.concatenate([-sine, sine], 1)


RELATIVE = (0, 2, 4, 6, 1, 3, 5, 7)


def swap(value, bit):
    count = lax.axis_size("ctx")
    return lax.ppermute(value, "ctx", [(i, i ^ bit) for i in range(count)])


def block_owner(count, me):
    if count == 8:
        return jnp.asarray(RELATIVE, jnp.int32) ^ me
    return jnp.arange(count, dtype=jnp.int32)


def after(value, *others):
    return lax.optimization_barrier((value,) + others)[0]


def plane_pieces(block):
    half = block.shape[0] // 2
    via_x = swap(block, 2)
    via_y = swap(block, 4)
    return [block, via_x, via_y, swap(via_x[:half], 4), swap(via_y[half:], 2)]


def plane_sends(block):
    half = block.shape[0] // 2
    via_x = swap(block, 2)
    via_y = swap(block, 4)
    from_x, from_y = via_x[:half], via_y[half:]
    return [block, via_x, via_y, swap(from_x, 4), swap(from_y, 2)], (from_x, from_y)


def plane_gather(block):
    count = lax.axis_size("ctx")
    if count != 8:
        return [lax.all_gather(block, "ctx", axis=0, tiled=True)]
    mine = plane_pieces(block)
    return mine + [swap(piece, 1) for piece in mine]


def sum_kernel(*refs):
    total = refs[0][...].astype(F32)
    for ref in refs[1:-1]:
        total = total + ref[...].astype(F32)
    refs[-1][...] = total.astype(refs[-1].dtype)


def sum_of(values, kind, limit=24):
    return pl.pallas_call(
        sum_kernel,
        out_shape=jax.ShapeDtypeStruct(values[0].shape, kind),
        in_specs=[VMEM_SPEC] * len(values),
        out_specs=VMEM_SPEC,
        compiler_params=pltpu.CompilerParams(vmem_limit_bytes=limit << 20),
        cost_estimate=COST,
    )(*values)


def add_diag_kernel(part_x_ref, part_y_ref, from_y_ref, from_x_ref, out_x_ref, out_y_ref):
    half = from_y_ref.shape[0]
    low = lambda a, b: (a.astype(F32) + b.astype(F32)).astype(BF)
    out_x_ref[:half] = low(part_x_ref[:half], from_y_ref[...])
    out_x_ref[half:] = part_x_ref[half:].astype(BF)
    out_y_ref[:half] = part_y_ref[:half].astype(BF)
    out_y_ref[half:] = low(part_y_ref[half:], from_x_ref[...])


def add_diag(part_x, part_y, from_y, from_x):
    return pl.pallas_call(
        add_diag_kernel,
        out_shape=(jax.ShapeDtypeStruct(part_x.shape, BF),) * 2,
        in_specs=[VMEM_SPEC] * 4,
        out_specs=[VMEM_SPEC] * 2,
        compiler_params=pltpu.CompilerParams(vmem_limit_bytes=24 << 20),
        cost_estimate=COST,
    )(part_x, part_y, from_y, from_x)


def plane_scatter(multiply, left, fill=None, others=(), last=()):
    count = lax.axis_size("ctx")
    if count != 8:
        parts = multiply(left, BF)
        return lax.psum_scatter(parts, "ctx", scatter_dimension=0, tiled=True).astype(F32)
    side = left.shape[0] // 2
    rows = side // 4
    half = rows // 2
    give = multiply(left[side:], BF)
    got = swap(give, 1)
    keep = multiply(after(left[:side], give), BF)
    kept = sum_of(after([keep, got], others), BF)
    sends = kept[3 * rows : -half], kept[-half:]
    from_y, from_x = swap(sends[0], 4), swap(sends[1], 2)
    from_y, from_x = after((from_y, from_x), fill(sends))
    part_x, part_y = add_diag(kept[rows : 2 * rows], kept[2 * rows : 3 * rows], from_y, from_x)
    got = after((swap(part_x, 2), swap(part_y, 4)), last)
    return kept[:rows].astype(F32) + got[0].astype(F32) + got[1].astype(F32)


class Order:
    def __init__(self, *values):
        self.last = values

    def take(self, value):
        return after(value, *self.last)

    def give(self, *values):
        self.last = values


def ring(value):
    count = lax.axis_size("wt")
    return lax.ppermute(value, "wt", [(i, (i + 1) % count) for i in range(count)])


def ring_chunks(block):
    chunks = [block]
    for _ in range(lax.axis_size("wt") - 1):
        chunks.append(ring(chunks[-1]))
    return chunks


def ring_sum(parts, kind):
    total = parts[1]
    for part in parts[2:] + parts[:1]:
        total = ring(total.astype(kind)).astype(F32) + part
    return total


def axis_sum(value, name):
    count = lax.axis_size(name)
    bit = 1
    while bit < count:
        value = value + lax.ppermute(value, name, [(i, i ^ bit) for i in range(count)])
        bit *= 2
    return value


def head_norm(raw, gain):
    scale = lax.rsqrt(jnp.mean(raw * raw, axis=-1, keepdims=True) + EPSILON)
    return raw * scale * gain


def turn(value):
    return pltpu.roll(value, value.shape[-1] // 2, 1)


def tile_mask(seg_col, seg_row, row_start, col_start):
    shape = (seg_col.shape[0], seg_row.shape[1])
    rows = lax.broadcasted_iota(jnp.int32, shape, 0) + row_start
    cols = lax.broadcasted_iota(jnp.int32, shape, 1) + col_start
    return (seg_col == seg_row) & (cols <= rows)


def attend_kernel(
    heads,
    pieces,
    block_ref,
    place_ref,
    first_ref,
    *refs,
):
    attend_body(heads, block_ref, place_ref, first_ref, refs[:pieces], *refs[pieces:])


def joined(refs, rows):
    group, have = [], 0
    for ref in refs:
        for start in range(0, ref.shape[0], rows):
            stop = min(start + rows, ref.shape[0])
            group.append(ref[start:stop])
            have += stop - start
            if have == rows:
                yield group[0] if len(group) == 1 else jnp.concatenate(group, axis=0)
                group, have = [], 0


def attend_body(
    heads,
    block_ref,
    place_ref,
    first_ref,
    hidden_refs,
    weight_ref,
    query_gain_ref,
    key_gain_ref,
    cosine_ref,
    sine_ref,
    seg_row_ref,
    seg_col_ref,
    query_ref,
    key_ref,
    value_ref,
    raw_ref,
    out_ref,
    score_ref,
):
    half = out_ref.shape[1]
    dim = query_gain_ref.shape[1]
    scale = dim ** (-0.5)

    for pair, lhs in enumerate(joined(hidden_refs, 4 * half)):
        raw = jnp.dot(lhs, weight_ref[...], preferred_element_type=F32)
        for piece in range(4):
            start = pl.multiple_of(block_ref[pair * 4 + piece] * half, half)
            spot = pl.ds(start, half)
            cosine, sine = cosine_ref[spot, :], sine_ref[spot, :]
            part = raw[piece * half : (piece + 1) * half]
            for head in range(heads + 1):
                cols = slice(head * dim, (head + 1) * dim)
                gain = query_gain_ref[...] if head < heads else key_gain_ref[...]
                normed = head_norm(part[:, cols], gain)
                roped = (normed * cosine + turn(normed) * sine).astype(BF)
                if head < heads:
                    query_ref[spot, cols] = roped
                else:
                    key_ref[spot, :] = roped
            raw_ref[spot, :] = part[:, : (heads + 1) * dim]
            value_ref[spot, :] = part[:, (heads + 1) * dim :].astype(BF)

    seq = key_ref.shape[0]
    stacked = heads * QUERY_ROWS

    def attend(index, carry):
        row_start = pl.multiple_of(index * QUERY_ROWS, QUERY_ROWS)
        row_spot = pl.ds(row_start, QUERY_ROWS)
        query = jnp.concatenate(
            [query_ref[row_spot, h * dim : (h + 1) * dim] for h in range(heads)], axis=0
        )
        seg_col = seg_col_ref[row_spot, :]
        low = first_ref[index] // KEY_ROWS
        high = (row_start + QUERY_ROWS + KEY_ROWS - 1) // KEY_ROWS

        def scores(tile, top):
            start = pl.multiple_of(tile * KEY_ROWS, KEY_ROWS)
            spot = pl.ds(start, KEY_ROWS)
            raw = lax.dot_general(
                query, key_ref[spot, :], (((1,), (1,)), ((), ())), preferred_element_type=F32
            )
            allowed = tile_mask(seg_col, seg_row_ref[:, spot], row_start, start)
            raw = raw.reshape(heads, QUERY_ROWS, KEY_ROWS) * scale
            masked = jnp.where(allowed[None], raw, MASKED).reshape(stacked, KEY_ROWS)
            score_ref[:, spot] = masked
            return jnp.maximum(top, jnp.max(masked, axis=1, keepdims=True))

        top = lax.fori_loop(low, high, scores, jnp.full((stacked, 1), MASKED, F32))

        def gather(tile, state):
            total, acc = state
            start = pl.multiple_of(tile * KEY_ROWS, KEY_ROWS)
            spot = pl.ds(start, KEY_ROWS)
            probs = jnp.exp(score_ref[:, spot] - top)
            total = total + jnp.sum(probs, axis=1, keepdims=True)
            acc = acc + jnp.dot(
                probs.astype(BF), value_ref[spot, :], preferred_element_type=F32
            )
            return total, acc

        total, acc = lax.fori_loop(
            low, high, gather, (jnp.zeros((stacked, 1), F32), jnp.zeros((stacked, dim), F32))
        )
        result = (acc / total).astype(BF)
        for head in range(heads):
            for piece in range(QUERY_ROWS // half):
                spot = place_ref[index * (QUERY_ROWS // half) + piece]
                begin = head * QUERY_ROWS + piece * half
                out_ref[spot, :, head * dim : (head + 1) * dim] = result[begin : begin + half]
        return carry

    lax.fori_loop(0, seq // QUERY_ROWS, attend, 0)


def attend_back_kernel(heads, pieces, place_ref, first_ref, *refs):
    attend_back_body(heads, place_ref, first_ref, refs[:pieces], *refs[pieces:])


def attend_back_body(
    heads,
    place_ref,
    first_ref,
    piece_refs,
    out_weight_ref,
    query_ref,
    key_ref,
    value_ref,
    raw_ref,
    query_gain_ref,
    key_gain_ref,
    cosine_ref,
    sine_ref,
    seg_row_ref,
    seg_col_ref,
    out_ref,
    query_gain_grad_ref,
    key_gain_grad_ref,
    score_ref,
    prob_grad_ref,
    key_grad_ref,
    value_grad_ref,
    grad_ref,
):
    half = grad_ref.shape[1]
    spot = 0
    for part in joined(piece_refs, 4 * half):
        part = lax.dot_general(
            part, out_weight_ref[...], (((1,), (1,)), ((), ())), preferred_element_type=F32
        ).astype(BF)
        for piece in range(4):
            grad_ref[spot] = part[piece * half : (piece + 1) * half]
            spot += 1
    dim = query_gain_ref.shape[1]
    scale = dim ** (-0.5)
    seq = key_ref.shape[0]
    stacked = heads * QUERY_ROWS
    pieces = QUERY_ROWS // half
    key_grad_ref[...] = jnp.zeros_like(key_grad_ref)
    value_grad_ref[...] = jnp.zeros_like(value_grad_ref)
    query_gain_grad_ref[...] = jnp.zeros_like(query_gain_grad_ref)
    key_gain_grad_ref[...] = jnp.zeros_like(key_gain_grad_ref)

    def unrope(grad, raw, gain, cosine, sine):
        norm_scale = lax.rsqrt(jnp.mean(raw * raw, axis=-1, keepdims=True) + EPSILON)
        unit = raw * norm_scale
        grad = grad * cosine + turn(grad * sine)
        gain_grad = jnp.sum(grad * unit, axis=0, keepdims=True)
        grad = grad * gain
        grad = norm_scale * (grad - unit * jnp.mean(grad * unit, axis=-1, keepdims=True))
        return grad, gain_grad

    def back(index, carry):
        row_start = pl.multiple_of(index * QUERY_ROWS, QUERY_ROWS)
        row_spot = pl.ds(row_start, QUERY_ROWS)
        places = [place_ref[index * pieces + piece] for piece in range(pieces)]
        query = jnp.concatenate(
            [query_ref[row_spot, h * dim : (h + 1) * dim] for h in range(heads)], axis=0
        )
        grad = jnp.concatenate(
            [
                grad_ref[place, :, h * dim : (h + 1) * dim]
                for h in range(heads)
                for place in places
            ],
            axis=0,
        )
        seg_col = seg_col_ref[row_spot, :]
        low = first_ref[index] // KEY_ROWS
        high = (row_start + QUERY_ROWS + KEY_ROWS - 1) // KEY_ROWS

        def scores(tile, top):
            start = pl.multiple_of(tile * KEY_ROWS, KEY_ROWS)
            spot = pl.ds(start, KEY_ROWS)
            raw = lax.dot_general(
                query, key_ref[spot, :], (((1,), (1,)), ((), ())), preferred_element_type=F32
            )
            allowed = tile_mask(seg_col, seg_row_ref[:, spot], row_start, start)
            raw = raw.reshape(heads, QUERY_ROWS, KEY_ROWS) * scale
            masked = jnp.where(allowed[None], raw, MASKED).reshape(stacked, KEY_ROWS)
            score_ref[:, spot] = masked
            return jnp.maximum(top, jnp.max(masked, axis=1, keepdims=True))

        top = lax.fori_loop(low, high, scores, jnp.full((stacked, 1), MASKED, F32))

        def probabilities(tile, state):
            total, inner = state
            start = pl.multiple_of(tile * KEY_ROWS, KEY_ROWS)
            spot = pl.ds(start, KEY_ROWS)
            probs = jnp.exp(score_ref[:, spot] - top)
            prob_grad = lax.dot_general(
                grad, value_ref[spot, :], (((1,), (1,)), ((), ())), preferred_element_type=F32
            )
            score_ref[:, spot] = probs
            prob_grad_ref[:, spot] = prob_grad
            total = total + jnp.sum(probs, axis=1, keepdims=True)
            inner = inner + jnp.sum(probs * prob_grad, axis=1, keepdims=True)
            return total, inner

        zero = jnp.zeros((stacked, 1), F32)
        total, inner = lax.fori_loop(low, high, probabilities, (zero, zero))
        share = 1.0 / total
        inner = inner * share

        def gradients(tile, acc):
            start = pl.multiple_of(tile * KEY_ROWS, KEY_ROWS)
            spot = pl.ds(start, KEY_ROWS)
            probs = score_ref[:, spot] * share
            score_grad = (probs * (prob_grad_ref[:, spot] - inner) * scale).astype(BF)
            acc = acc + jnp.dot(score_grad, key_ref[spot, :], preferred_element_type=F32)
            key_grad_ref[spot, :] += lax.dot_general(
                score_grad, query, (((0,), (0,)), ((), ())), preferred_element_type=F32
            )
            value_grad_ref[spot, :] += lax.dot_general(
                probs.astype(BF), grad, (((0,), (0,)), ((), ())), preferred_element_type=F32
            )
            return acc

        acc = lax.fori_loop(low, high, gradients, jnp.zeros((stacked, dim), F32))
        cosine, sine = cosine_ref[row_spot, :], sine_ref[row_spot, :]
        for head in range(heads):
            cols = slice(head * dim, (head + 1) * dim)
            part = acc[head * QUERY_ROWS : (head + 1) * QUERY_ROWS]
            part, gain_grad = unrope(
                part, raw_ref[row_spot, cols], query_gain_ref[...], cosine, sine
            )
            query_gain_grad_ref[...] += gain_grad
            part = part.astype(BF)
            for piece in range(pieces):
                out_ref[places[piece], :, cols] = part[piece * half : (piece + 1) * half]
        return carry

    lax.fori_loop(0, seq // QUERY_ROWS, back, 0)

    def finish(index, carry):
        row_start = pl.multiple_of(index * QUERY_ROWS, QUERY_ROWS)
        row_spot = pl.ds(row_start, QUERY_ROWS)
        key_cols = slice(heads * dim, (heads + 1) * dim)
        value_cols = slice((heads + 1) * dim, (heads + 2) * dim)
        part, gain_grad = unrope(
            key_grad_ref[row_spot, :],
            raw_ref[row_spot, key_cols],
            key_gain_ref[...],
            cosine_ref[row_spot, :],
            sine_ref[row_spot, :],
        )
        key_gain_grad_ref[...] += gain_grad
        part = part.astype(BF)
        value = value_grad_ref[row_spot, :].astype(BF)
        for piece in range(pieces):
            place = place_ref[index * pieces + piece]
            out_ref[place, :, key_cols] = part[piece * half : (piece + 1) * half]
            out_ref[place, :, value_cols] = value[piece * half : (piece + 1) * half]
        return carry

    lax.fori_loop(0, seq // QUERY_ROWS, finish, 0)


def one_hot(hit):
    return hit.astype(F32).astype(BF)


def select_kernel(groups, joint, *refs):
    target_ref, mine_ref, other_ref = refs[sum(groups) :]
    slots = mine_ref.shape[0] // 2
    target = target_ref[...]
    half = target.shape[1] // 8
    index = lax.broadcasted_iota(jnp.int32, (2 * slots, target.shape[1]), 0)
    pick = one_hot((index == target[0:1]) | (index == target[1:2]))
    for k in range(2):
        rows = []
        if joint:
            for ref in refs[: groups[0]]:
                for start in range(k * half, ref.shape[0], 2 * half):
                    rows.append(ref[start : start + half])
        else:
            first = k * groups[0]
            rows = [ref[...] for ref in refs[first : first + groups[k]]]
        picked = jnp.dot(pick, jnp.concatenate(rows, axis=0), preferred_element_type=F32)
        picked = picked.astype(BF)
        mine_ref[k * slots : (k + 1) * slots] = picked[:slots]
        other_ref[k * slots : (k + 1) * slots] = picked[slots:]


def select_rows(pieces, others, target, slots):
    width = pieces[0].shape[1]
    return pl.pallas_call(
        functools.partial(select_kernel, (len(pieces), len(others)), not others),
        out_shape=(jax.ShapeDtypeStruct((2 * slots, width), BF),) * 2,
        in_specs=[VMEM_SPEC] * (len(pieces) + len(others) + 1),
        out_specs=[VMEM_SPEC] * 2,
        compiler_params=pltpu.CompilerParams(vmem_limit_bytes=24 << 20),
        cost_estimate=COST,
    )(*pieces, *others, target)


def spread_kernel(chunks, part, grouped, *refs):
    mine_refs, other_refs = refs[:chunks], refs[chunks : 2 * chunks]
    target_ref, first_ref, second_ref = refs[2 * chunks : 2 * chunks + 3]
    outs = refs[2 * chunks + 3 :]
    slots = mine_refs[0].shape[0] // 2
    half = first_ref.shape[0] // chunks
    rows = 2 * half
    spot = slice(part * slots, (part + 1) * slots)
    for j in range(chunks):
        values = jnp.concatenate([mine_refs[j][spot], other_refs[j][spot]], axis=0)
        target = target_ref[j]
        index = lax.broadcasted_iota(jnp.int32, (4 * rows, 2 * slots), 1)
        pick = one_hot((index == target[:, 0:1]) | (index == target[:, 1:2]))
        spread = jnp.dot(pick, values, preferred_element_type=F32).astype(BF)
        for k in range(3):
            ref, start = (outs[k], j * rows) if grouped else (outs[3 * j + k], 0)
            ref[start : start + rows] = spread[k * rows : (k + 1) * rows]
        if grouped:
            ref = first_ref if 2 * j < chunks else second_ref
            start = j % (chunks // 2) * rows
            ref[start : start + rows] = spread[3 * rows :]
        else:
            first_ref[j * half : (j + 1) * half] = spread[3 * rows : 3 * rows + half]
            second_ref[j * half : (j + 1) * half] = spread[3 * rows + half :]


def spread_rows(mine, other, target, rows, part, grouped):
    chunks = len(mine)
    slots, width = mine[0].shape
    low = lambda count: jax.ShapeDtypeStruct((count, width), BF)
    blocks = (low(chunks * rows),) * 3 if grouped else (low(rows),) * (3 * chunks)
    outs = pl.pallas_call(
        functools.partial(spread_kernel, chunks, part, grouped),
        out_shape=(low(chunks * rows // 2),) * 2 + blocks,
        in_specs=[VMEM_SPEC] * (2 * chunks + 1),
        out_specs=[VMEM_SPEC] * (2 + len(blocks)),
        compiler_params=pltpu.CompilerParams(
            vmem_limit_bytes=(16 << 20) if chunks == 1 else (36 << 20)
        ),
        cost_estimate=COST,
    )(*mine, *other, target)
    return outs[:2], outs[2:]


def expert_kernel(expert_ref, mine_ref, other_ref, *refs):
    slots = mine_ref.shape[0] // 2
    rows, grads = slice(0, slots), slice(slots, 2 * slots)
    expert_body(
        expert_ref, mine_ref.at[rows], other_ref.at[rows], mine_ref.at[grads], other_ref.at[grads], *refs
    )


def expert_body(
    expert_ref,
    mine_ref,
    other_ref,
    grad_mine_ref,
    grad_other_ref,
    target_ref,
    route_ref,
    gate_ref,
    up_ref,
    down_ref,
    router_ref,
    back_mine_ref,
    back_other_ref,
    hidden_ref,
    gate_grad_ref,
    up_grad_ref,
    routed_ref,
    router_grad_ref,
):
    slots = mine_ref.shape[0]
    experts = router_ref.shape[0]
    tokens = target_ref.shape[1]
    rows = jnp.concatenate([mine_ref[...], other_ref[...]], axis=0)
    nt = (((1,), (1,)), ((), ()))
    tn = (((0,), (0,)), ((), ()))
    gate_pre = jnp.dot(rows, gate_ref[...], preferred_element_type=F32)
    up_pre = jnp.dot(rows, up_ref[...], preferred_element_type=F32)
    sigmoid = 1.0 / (1.0 + jnp.exp(-gate_pre))
    silu = gate_pre * sigmoid
    hidden = (silu * up_pre).astype(BF)
    hidden_ref[...] = hidden
    result = jnp.dot(hidden, down_ref[...], preferred_element_type=F32).astype(BF).astype(F32)
    slot_iota = lax.broadcasted_iota(jnp.int32, (slots, tokens), 0)
    expert_iota = lax.broadcasted_iota(jnp.int32, (experts, tokens), 0)
    masks = []
    for side in range(2):
        pick = one_hot(slot_iota == target_ref[side : side + 1, :])
        chosen = expert_iota == route_ref[side, 0:1, :]
        for k in range(1, route_ref.shape[1]):
            chosen = chosen | (expert_iota == route_ref[side, k : k + 1, :])
        masks.append(lax.dot_general(pick, one_hot(chosen), nt, preferred_element_type=F32))
    chosen = jnp.concatenate(masks, axis=0) > 0.5
    logits = lax.dot_general(rows, router_ref[...], nt, preferred_element_type=F32)
    top = jnp.max(jnp.where(chosen, logits, MASKED), axis=1, keepdims=True)
    weights = jnp.where(chosen, jnp.exp(logits - top), 0.0)
    total = jnp.sum(weights, axis=1, keepdims=True)
    gates = weights / jnp.where(total > 0.0, total, 1.0)
    mine = lax.broadcasted_iota(jnp.int32, gates.shape, 1) == expert_ref[0]
    gate = jnp.sum(jnp.where(mine, gates, 0.0), axis=1, keepdims=True)
    gated = (result * gate).astype(BF)
    back_mine_ref[slots:] = gated[:slots]
    back_other_ref[slots:] = gated[slots:]
    grad = jnp.concatenate([grad_mine_ref[...], grad_other_ref[...]], axis=0).astype(F32)
    gate_value_grad = jnp.sum(grad * result, axis=1, keepdims=True)
    routed = (grad * gate).astype(BF)
    routed_ref[...] = routed
    hidden_grad = lax.dot_general(routed, down_ref[...], nt, preferred_element_type=F32)
    gate_low = (hidden_grad * up_pre * sigmoid * (1.0 + gate_pre * (1.0 - sigmoid))).astype(BF)
    up_low = (hidden_grad * silu).astype(BF)
    gate_grad_ref[...] = gate_low
    up_grad_ref[...] = up_low
    logit_grad = (gate_value_grad * gate) * (jnp.where(mine, 1.0, 0.0) - gates)
    high = logit_grad.astype(BF)
    low = (logit_grad - high.astype(F32)).astype(BF)
    both = jnp.concatenate([high, low], axis=1)
    router = router_ref[...]
    slot_grad = lax.dot_general(gate_low, gate_ref[...], nt, preferred_element_type=F32)
    slot_grad = slot_grad + lax.dot_general(up_low, up_ref[...], nt, preferred_element_type=F32)
    slot_grad = slot_grad + jnp.dot(
        both, jnp.concatenate([router, router], axis=0), preferred_element_type=F32
    )
    slot_grad = slot_grad.astype(BF)
    back_mine_ref[:slots] = slot_grad[:slots]
    back_other_ref[:slots] = slot_grad[slots:]
    router_grad = lax.dot_general(both, rows, tn, preferred_element_type=F32)
    router_grad_ref[...] = router_grad[:experts] + router_grad[experts:]


def expert_rows(expert, mine, other, target, route, *weights):
    count, width = mine.shape
    ff = weights[0].shape[1]
    experts = weights[3].shape[0]
    low = lambda cols: jax.ShapeDtypeStruct((count, cols), BF)
    return pl.pallas_call(
        expert_kernel,
        out_shape=(
            low(width),
            low(width),
            low(ff),
            low(ff),
            low(ff),
            low(width),
            jax.ShapeDtypeStruct((experts, width), F32),
        ),
        in_specs=[SMEM_SPEC] + [VMEM_SPEC] * 8,
        out_specs=[VMEM_SPEC] * 7,
        compiler_params=pltpu.CompilerParams(vmem_limit_bytes=40 << 20),
        cost_estimate=COST,
    )(expert, mine, other, target, route, *weights)


def place_kernel(share, order_ref, owner_ref, part_ref, query_ref, key_ref, value_ref):
    cols = query_ref.shape[1]
    dim = key_ref.shape[1]
    part = part_ref[0]
    query_ref[...] = part[:, :cols].astype(F32)
    key = part[:, cols : cols + dim].astype(F32)
    value = part[:, cols + dim :].astype(F32)
    first = pl.program_id(0) % share == 0

    @pl.when(first)
    def _():
        key_ref[...] = key
        value_ref[...] = value

    @pl.when(jnp.logical_not(first))
    def _():
        key_ref[...] += key
        value_ref[...] += value


def place_weight_grads(parts, owner, share, dim):
    count, rows, width = parts.shape
    cols = width - 2 * dim
    if count == 8 and share == 2:
        order = jnp.asarray([0, 4, 1, 5, 2, 6, 3, 7], jnp.int32)
    else:
        order = jnp.arange(count, dtype=jnp.int32)
    owner = owner[order]
    group = lambda g, order, owner: (0, owner[g] // share)
    return pl.pallas_call(
        functools.partial(place_kernel, share),
        grid_spec=pltpu.PrefetchScalarGridSpec(
            num_scalar_prefetch=2,
            grid=(count,),
            in_specs=[pl.BlockSpec((1, rows, width), lambda g, order, owner: (order[g], 0, 0))],
            out_specs=[
                pl.BlockSpec((rows, cols), lambda g, order, owner: (0, owner[g])),
                pl.BlockSpec((rows, dim), group),
                pl.BlockSpec((rows, dim), group),
            ],
        ),
        out_shape=(
            jax.ShapeDtypeStruct((rows, cols * count), F32),
            jax.ShapeDtypeStruct((rows, dim * count // share), F32),
            jax.ShapeDtypeStruct((rows, dim * count // share), F32),
        ),
        compiler_params=pltpu.CompilerParams(vmem_limit_bytes=ATTEND_LIMIT),
        cost_estimate=COST,
    )(order, owner, parts)


def rows_kernel(owner_ref, part_ref, out_ref):
    out_ref[:, 0] = part_ref[0].astype(F32)


def place_rows(parts, owner):
    count, chunks, rows, width = parts.shape
    return pl.pallas_call(
        rows_kernel,
        grid_spec=pltpu.PrefetchScalarGridSpec(
            num_scalar_prefetch=1,
            grid=(count,),
            in_specs=[pl.BlockSpec((1, chunks, rows, width), lambda g, owner: (g, 0, 0, 0))],
            out_specs=pl.BlockSpec(
                (chunks, 1, rows, width), lambda g, owner: (0, owner[g], 0, 0)
            ),
        ),
        out_shape=jax.ShapeDtypeStruct((chunks, count, rows, width), F32),
        compiler_params=pltpu.CompilerParams(vmem_limit_bytes=ATTEND_LIMIT),
        cost_estimate=COST,
    )(owner, parts)


def place_pieces_kernel(share, owner_ref, *refs):
    pieces, (query_ref, key_ref, value_ref) = refs[:-3], refs[-3:]
    rows, dim = query_ref.shape[0], key_ref.shape[1] * share // 8
    cols = query_ref.shape[1] // 8
    for k in range(4):
        both = [
            [ref[...].astype(F32) for ref in refs_of]
            for refs_of in (block_refs(pieces, k), block_refs(pieces, k + 4))
        ]
        both = [p[0] if len(p) == 1 else jnp.concatenate(p, axis=0) for p in both]
        for side in range(2):
            start = pl.multiple_of(owner_ref[k + 4 * side] * cols, cols)
            query_ref[:, pl.ds(start, cols)] = both[side][:, :cols]
        start = pl.multiple_of(owner_ref[k] // share * dim, dim)
        key_ref[:, pl.ds(start, dim)] = both[0][:, cols : cols + dim] + both[1][:, cols : cols + dim]
        value_ref[:, pl.ds(start, dim)] = both[0][:, cols + dim :] + both[1][:, cols + dim :]


def block_refs(pieces, k):
    first = k // 4 * 5 + k % 4
    return pieces[first : first + 2] if k % 4 == 3 else pieces[first : first + 1]


def place_weight_pieces(pieces, owner, share, dim):
    rows, width = pieces[0].shape
    cols = width - 2 * dim
    return pl.pallas_call(
        functools.partial(place_pieces_kernel, share),
        out_shape=(
            jax.ShapeDtypeStruct((rows, cols * 8), F32),
            jax.ShapeDtypeStruct((rows, dim * 8 // share), F32),
            jax.ShapeDtypeStruct((rows, dim * 8 // share), F32),
        ),
        in_specs=[SMEM_SPEC] + [VMEM_SPEC] * len(pieces),
        out_specs=[VMEM_SPEC] * 3,
        compiler_params=pltpu.CompilerParams(vmem_limit_bytes=ATTEND_LIMIT),
        cost_estimate=COST,
    )(owner, *pieces)


def row_pieces_kernel(owner_ref, *refs):
    pieces, out_ref = refs[:-1], refs[-1]
    chunks, _, rows, _ = out_ref.shape
    for k in range(8):
        parts = [ref[...] for ref in block_refs(pieces, k)]
        part = parts[0] if len(parts) == 1 else jnp.concatenate(parts, axis=0)
        for chunk in range(chunks):
            out_ref[chunk, owner_ref[k]] = part[chunk * rows : (chunk + 1) * rows].astype(F32)


def place_row_pieces(pieces, owner, chunks):
    rows, width = pieces[0].shape
    return pl.pallas_call(
        row_pieces_kernel,
        out_shape=jax.ShapeDtypeStruct((chunks, 8, rows // chunks, width), F32),
        in_specs=[SMEM_SPEC] + [VMEM_SPEC] * len(pieces),
        out_specs=VMEM_SPEC,
        compiler_params=pltpu.CompilerParams(vmem_limit_bytes=ATTEND_LIMIT),
        cost_estimate=COST,
    )(owner, *pieces)


def product_kernel(dims, rows, left_count, right_count, starts, start_ref, *refs):
    lefts, rights = refs[:left_count], refs[left_count : left_count + right_count]
    outs = refs[left_count + right_count :]
    join = lambda parts: parts[0] if len(parts) == 1 else jnp.concatenate(parts, axis=0)
    right = join([ref[...] for ref in rights])
    for k, out_ref in enumerate(outs):
        if starts:
            width = out_ref.shape[0]
            cols = pl.ds(pl.multiple_of(start_ref[k] * width, width), width)
            left = join([ref[:, cols] for ref in lefts])
        else:
            left = join([ref[...] if rows is None else ref[:rows] for ref in lefts])
        out = lax.dot_general(left, right, (dims, ((), ())), preferred_element_type=F32)
        out_ref[...] = out.astype(out_ref.dtype)


def product(lefts, rights, dims, out_shape, kind=F32, rows=None, starts=None, limit=60, tile=None):
    count = 1 if starts is None else starts.shape[0]
    start_arg = jnp.zeros((1,), jnp.int32) if starts is None else starts
    if tile is None:
        left_specs, right_specs = [VMEM_SPEC] * len(lefts), [VMEM_SPEC] * len(rights)
        out_spec = VMEM_SPEC
    else:
        left_specs = [
            pl.BlockSpec((rows or left.shape[0], tile), lambda i: (0, i)) for left in lefts
        ]
        right_specs = [pl.BlockSpec(right.shape, lambda i: (0, 0)) for right in rights]
        out_spec = pl.BlockSpec((tile, out_shape[1]), lambda i: (i, 0))
    outs = pl.pallas_call(
        functools.partial(
            product_kernel, dims, None, len(lefts), len(rights), starts is not None
        ),
        grid=() if tile is None else (out_shape[0] // tile,),
        out_shape=(jax.ShapeDtypeStruct(out_shape, kind),) * count,
        in_specs=[SMEM_SPEC] + left_specs + right_specs,
        out_specs=[out_spec] * count,
        compiler_params=pltpu.CompilerParams(vmem_limit_bytes=limit << 20),
        cost_estimate=COST,
    )(start_arg, *lefts, *rights)
    return outs[0] if starts is None else outs


def move_slots(slot_array):
    return lax.all_to_all(slot_array, ("ctx", "wt"), split_axis=0, concat_axis=0, tiled=True)


def local(
    tokens,
    cotangent,
    segments,
    routes,
    pair_order,
    attn_gain,
    ffn_gain,
    query_gain,
    key_gain,
    w_query,
    key_weight,
    value_weight,
    w_output,
    w_router,
    w_gate,
    w_up,
    w_down,
):
    ctx_count = lax.axis_size("ctx")
    wt_count = lax.axis_size("wt")
    me = lax.axis_index("ctx")
    plane = lax.axis_index("wt")
    inputs = tokens[0].astype(F32)
    tok_rows, model_width = inputs.shape
    half_rows = tok_rows // 2
    head_dim = query_gain.shape[0]
    experts = w_router.shape[1]
    top_count = routes.shape[2]
    seq_len = segments.shape[1]
    total_tokens = tok_rows * ctx_count * wt_count
    heads = w_query.shape[1] // head_dim // ctx_count
    kv_heads = key_weight.shape[1] // head_dim
    share = ctx_count // kv_heads
    head_cols = heads * head_dim
    group = me // share
    shard_width = model_width // wt_count
    capacity = max(2, half_rows * top_count * 5 // (4 * experts))
    dense = ctx_count == 8 and wt_count == 4 and w_gate.shape[0] == 1
    nt = (((1,), (1,)), ((), ()))
    tn = (((0,), (0,)), ((), ()))
    owners = block_owner(ctx_count, me)
    planes = (plane - jnp.arange(wt_count, dtype=jnp.int32)) % wt_count

    normed_one, attn_back = jax.vjp(rms_norm, inputs, attn_gain)
    normed_low = normed_one.astype(BF)
    kv_start = group * head_dim
    own_weight = jnp.concatenate(
        [
            lax.dynamic_slice_in_dim(w_query, me * head_cols, head_cols, 1),
            lax.dynamic_slice_in_dim(key_weight, kv_start, head_dim, 1),
            lax.dynamic_slice_in_dim(value_weight, kv_start, head_dim, 1),
        ],
        axis=1,
    )
    own_chunks = ctx_count // wt_count
    piece_rows = head_cols // ctx_count
    out_piece = lax.dynamic_index_in_dim(
        w_output.reshape(own_chunks, ctx_count, piece_rows, model_width), me, 1, keepdims=False
    )
    cot = cotangent[0]
    if dense:
        cap_rows = 2 * capacity
        slots = 4 * cap_rows
        expert = me * wt_count + plane
        triangle = jnp.triu(jnp.ones((tok_rows, tok_rows), F32)).astype(BF)
        offsets = (jnp.arange(ctx_count, dtype=jnp.int32) % 4) * cap_rows

        def tables(near):
            near = near.astype(jnp.int32).reshape(-1, ctx_count, top_count, tok_rows)

            def slot_of(routed_to):
                hits = jnp.any(near == routed_to, axis=2)
                ranks = jnp.dot(hits.astype(BF), triangle, preferred_element_type=F32)
                place = ranks.astype(jnp.int32) - 1 + offsets[None, :, None]
                return jnp.where(hits, place, -1).reshape(-1, 2, 4 * tok_rows)

            own_slot = slot_of(expert)
            other_slot = slot_of((me ^ 1) * wt_count + plane)[:, 0]
            target = jnp.stack(
                [own_slot[:, 0], jnp.where(other_slot < 0, -1, other_slot + slots)], axis=1
            )
            near_routes = (
                near.reshape(-1, 2, 4, top_count, tok_rows)
                .transpose(0, 1, 3, 2, 4)
                .reshape(-1, 2, top_count, 4 * tok_rows)
            )
            indices = jnp.arange(experts, dtype=jnp.int32)[:, None, None, None, None]
            counts = jnp.sum((near[None] == indices).astype(F32), axis=(1, 2, 3, 4))
            return own_slot, target, target.transpose(0, 2, 1), near_routes, counts

        block_rows = own_chunks * piece_rows
        out_piece = out_piece.reshape(block_rows, model_width)
        ticks = [(out_piece, own_weight), (ring(out_piece), ring(own_weight))]
        own = after(normed_low, out_piece, own_weight)
        via_x, via_y = swap(own, 2), swap(own, 4)
        near = after(routes[0].T.astype(BF), own)
        near_x, near_y = swap(near, 2), swap(near, 4)
        sent = via_x[:half_rows], via_y[half_rows:]
        diag_a, diag_b = swap(sent[0], 4), swap(sent[1], 2)
        near_x, near_y = after((near_x, near_y), sent)
        near = jnp.concatenate([near, near_x, near_y, swap(near_x, 4)], axis=0)
        near = jnp.concatenate([near, swap(near, 1)], axis=0)
        hidden_pieces = [own, via_x, via_y, diag_a, diag_b]
        hidden_pieces = hidden_pieces + [swap(piece, 1) for piece in hidden_pieces]
        ticks[1], near, cot_block = after((ticks[1], near, cot), ticks[1], hidden_pieces, near)
        near_rows = near.shape[0]
        tiny = jnp.concatenate([near, w_router.T.reshape(-1, tok_rows)], axis=0)
        tinies = [tiny, ring(tiny)]
        cot_x, cot_y = swap(cot_block, 2), swap(cot_block, 4)
        ticks.append((ring(ticks[1][0]), ring(ticks[1][1])))
        first_tables = tables(near)
        zero = ticks[1][0][0, 0].astype(F32) * 0.0
        tables_done = cosine, sine = rope_tables(seq_len, head_dim, zero)
        def keep(j, buffers, shards):
            put = lax.dynamic_update_slice_in_dim
            return (
                put(buffers[0], shards[0], planes[j] * block_rows, 0),
                put(buffers[1], shards[1], planes[j] * shard_width, 0),
            )

        cot_sent = cot_x[:half_rows], cot_y[half_rows:]
        ticks[2], cot_sent, tinies[1] = after(
            (ticks[2], cot_sent, tinies[1]), ticks[2], cot_sent, tinies[1], first_tables, tables_done
        )
        ticks.append((ring(ticks[2][0]), ring(ticks[2][1])))
        tinies.append(ring(tinies[1]))
        diag_a, diag_b = swap(cot_sent[0], 4), swap(cot_sent[1], 2)
        seed = ticks[2][0][:1, :1] * 0
        buffers = (
            jnp.broadcast_to(seed, (ctx_count * piece_rows, model_width)),
            jnp.broadcast_to(seed, (model_width, own_weight.shape[1])),
        )

        for j in range(3):
            buffers = keep(j, buffers, ticks[j])
        cot_pieces = [cot, cot_x, cot_y, diag_a, diag_b]
        cot_diag = jnp.concatenate([diag_a, diag_b], axis=0)
        ticks[3] = after(ticks[3], cot_diag, tinies[2], buffers)
        out_pieces, weight = keep(3, buffers, ticks[3])
        tinies.append(ring(after(tinies[2], weight)))
        cot_next = [ring(after(p, weight)) for p in (cot, cot_x, cot_y, cot_diag)]
        tinies_later = tinies[1:]
        router = jnp.stack([tiny[near_rows:].reshape(experts, shard_width) for tiny in tinies])
        router = router[planes].transpose(1, 0, 2).reshape(experts, model_width)
    else:
        hidden_pieces = plane_gather(normed_low)
        out_pieces = lax.all_gather(out_piece, "wt", axis=0, tiled=True)
        weight = lax.all_gather(own_weight, "wt", axis=0, tiled=True)
        router = lax.all_gather(w_router, "wt", axis=0, tiled=True).T
        cosine, sine = rope_tables(seq_len, head_dim, 0.0)
    out_weight = lax.all_to_all(
        out_pieces.reshape(ctx_count, piece_rows, model_width), "ctx", 0, 0, tiled=True
    ).reshape(head_cols, model_width)

    owner_pair = pair_order[owners]
    blocks = jnp.stack([owner_pair, 2 * ctx_count - 1 - owner_pair], 1).reshape(-1)
    order = jnp.arange(2 * ctx_count, dtype=jnp.int32)
    places = jnp.sum(jnp.where(blocks[:, None] == order[None, :], order[:, None], 0), axis=0)
    places = places.astype(jnp.int32)
    seg = segments[0]
    first = jnp.sum(
        (seg[None, :] < seg[::QUERY_ROWS][:, None]).astype(jnp.int32), axis=1
    ).astype(jnp.int32)
    seg_row, seg_col = seg.reshape(1, seq_len), seg.reshape(seq_len, 1)
    query_gain_row, key_gain_row = query_gain.reshape(1, -1), key_gain.reshape(1, -1)

    width = head_cols + 2 * head_dim
    stacked = heads * QUERY_ROWS
    piece_count = len(hidden_pieces)
    query, key, value, raw, attn_low = pl.pallas_call(
        functools.partial(attend_kernel, heads, piece_count),
        out_shape=(
            jax.ShapeDtypeStruct((seq_len, head_cols), BF),
            jax.ShapeDtypeStruct((seq_len, head_dim), BF),
            jax.ShapeDtypeStruct((seq_len, head_dim), BF),
            jax.ShapeDtypeStruct((seq_len, head_cols + head_dim), F32),
            jax.ShapeDtypeStruct((2 * ctx_count, half_rows, head_cols), BF),
        ),
        in_specs=[SMEM_SPEC] * 3 + [VMEM_SPEC] * (7 + piece_count),
        out_specs=[VMEM_SPEC] * 5,
        scratch_shapes=[pltpu.VMEM((stacked, seq_len), F32)],
        compiler_params=pltpu.CompilerParams(vmem_limit_bytes=ATTEND_LIMIT),
        cost_estimate=COST,
    )(
        blocks,
        places,
        first,
        *hidden_pieces,
        weight,
        query_gain_row,
        key_gain_row,
        cosine,
        sine,
        seg_row,
        seg_col,
    )
    attn_rows = attn_low.reshape(seq_len, head_cols)
    later_tables = []
    out_project = lambda rows, kind: low_matmul(rows, out_weight).astype(kind)
    if dense:
        attn_rows = after(attn_rows, cot_next[:2])
        out_project = lambda rows, kind: product(
            [rows], [out_weight], ((1,), (0,)), (rows.shape[0], model_width), kind
        )

        def fill(sends):
            rows = after(tinies_later, sends)
            rows = jnp.concatenate([t[:near_rows] for t in rows], axis=0)
            later_tables.extend(tables(rows))
            return tuple(later_tables) + (cot_next[2],)

        attn = plane_scatter(out_project, attn_rows, fill, (), (cot_next[3],))
    else:
        attn = plane_scatter(out_project, attn_rows)
    residual = inputs + attn
    normed_two, ffn_back = jax.vjp(rms_norm, residual, ffn_gain)
    normed_two_low = normed_two.astype(BF)
    grad_out = cotangent[0].astype(F32)
    if dense:
        own_slot, target_rows, target_cols, near_routes = (
            jnp.concatenate([f, r], axis=0) for f, r in zip(first_tables[:4], later_tables[:4])
        )
        counts = first_tables[4] + later_tables[4]
        logits = lax.dot_general(normed_two_low, router, nt, preferred_element_type=F32)
        router_probs = jax.nn.softmax(logits, axis=-1)
        shares = counts / (total_tokens * top_count)
        prob_grad = (experts * shares / total_tokens)[None, :]
        logits_grad = router_probs * (
            prob_grad - jnp.sum(router_probs * prob_grad, axis=1, keepdims=True)
        )
        logits_grad_low = logits_grad.astype(BF)
        last = wt_count - 1
        mine_backs, other_backs, results = [], [], []

        def compute(j, pieces, others, gates, second=()):
            pieces = after(pieces, *gates)
            mine, other = select_rows(pieces, others, target_rows[j], slots)
            received = after(swap(other, 1), second)
            result = expert_rows(
                expert.reshape(1),
                mine,
                received,
                own_slot[j],
                near_routes[j],
                w_gate[0],
                w_up[0],
                w_down[0],
                router,
            )
            mine_backs.append(result[0])
            other_backs.append(swap(result[1], 1))
            results.append((mine, received) + tuple(result[2:]))
            return result[0]

        payload, before, done = normed_two_low, None, None
        for j in range(wt_count):
            if j == 2:
                cot_own = cot_next[0]
                halves = payload[:half_rows], cot_own[:half_rows], payload[half_rows:], cot_own[half_rows:]
                payload = jnp.concatenate(halves, axis=0)
            if j > 0:
                payload = ring(payload)
            block = payload if j == 0 else after(payload, before[3:])
            via_x, via_y = swap(block, 2), swap(block, 4)
            if done is not None:
                via_x, via_y = after((via_x, via_y), done)
            middle = via_x.shape[0] // 2
            sent = via_x[:middle], via_y[middle:]
            pieces = [block, via_x, via_y, swap(sent[0], 4), swap(sent[1], 2)]
            if before is not None:
                done = compute(j - 1, before, [cot_pieces, cot_next, []][j - 1], (sent,), pieces[3:])
            before = pieces
        group_sent, blocks = spread_rows(
            mine_backs, other_backs, target_cols[:last], tok_rows, 0, False
        )
        group_sent = after(group_sent, sent)
        group_diag = swap(group_sent[0], 4), swap(group_sent[1], 2)
        done = compute(last, pieces, [], (done,), group_sent)
        step = Order(done)

        def add_chunk(own, part_x, part_y, from_y, from_x):
            part_x, part_y, from_y, from_x = step.take((part_x, part_y, from_y, from_x))
            part_x, part_y = add_diag(part_x, part_y, from_y, from_x)
            step.give(part_x, part_y)
            return own, swap(part_x, 2), swap(part_y, 4)

        def chunk_sum(own, got_x, got_y):
            return [own] + list(step.take((got_x, got_y)))

        def chunk_diag(j):
            return [part[j * half_rows : (j + 1) * half_rows] for part in group_diag]

        partial = {j: add_chunk(*blocks[3 * j : 3 * j + 3], *chunk_diag(j)) for j in range(1, last)}
        tail_sent, tail = spread_rows(
            step.take(mine_backs[last:]), other_backs[last:], target_cols[last:], tok_rows, 0, False
        )
        step.give(tail_sent)
        tail_diag = swap(tail_sent[0], 4), swap(tail_sent[1], 2)
        rows_all = [r for res in results for r in res[:2]]
        hidden_low, gate_low, up_low, routed = ([res[k] for res in results] for k in range(2, 6))
        ff = w_gate.shape[2]
        grad_w_gate = product(step.take(rows_all), gate_low, ((0,), (0,)), (model_width, ff), F32, slots, tile=512, limit=40)
        step.give(grad_w_gate)
        total = sum_of(chunk_sum(*partial[1]), BF)
        step.give(total)
        total = ring(total)
        grad_w_up = product(step.take(rows_all), up_low, ((0,), (0,)), (model_width, ff), F32, slots, tile=512, limit=40)
        step.give(grad_w_up)
        for j in range(2, last):
            total = sum_of([step.take(total)] + chunk_sum(*partial[j]), BF)
            step.give(total)
            total = ring(total)
        partial[last] = add_chunk(*tail, *tail_diag)
        partial[0] = add_chunk(*blocks[:3], *chunk_diag(0))
        grad_w_down = product(
            step.take(hidden_low), routed, ((0,), (0,)), (ff, model_width), F32, tile=256, limit=40
        )
        step.give(grad_w_down)
        total = sum_of([step.take(total)] + chunk_sum(*partial[last]), BF)
        step.give(total)
        total = ring(total)
        out_sent, out_blocks = spread_rows(
            step.take(mine_backs), other_backs, target_cols, tok_rows, 1, True
        )
        step.give(out_sent)
        total = sum_of([step.take(total)] + chunk_sum(*partial[0]), F32)
        grad_normed_two = total + jnp.dot(logits_grad_low, router, preferred_element_type=F32)
        grad_w_gate, grad_w_up, grad_w_down = grad_w_gate[None], grad_w_up[None], grad_w_down[None]
        router_grad = sum(res[6] for res in results) + lax.dot_general(
            logits_grad_low, normed_two_low, tn, preferred_element_type=F32
        )
    else:
        w_router_all = router.T
        slot_rows = 2 * capacity
        local_experts = w_gate.shape[0]
        logits = low_matmul(normed_two_low, w_router_all)
        local_routes = routes[0]

        def router_fn(logit_values):
            router_probs = jax.nn.softmax(logit_values, axis=-1)
            chosen = jnp.take_along_axis(router_probs, local_routes, axis=1)
            return (chosen / jnp.sum(chosen, axis=1, keepdims=True), router_probs)

        (gate_values, router_probs), router_back = jax.vjp(router_fn, logits)
        route_flat = local_routes.reshape(-1)
        route_hits = (route_flat[:, None] == jnp.arange(experts, dtype=jnp.int32)[None, :]).astype(
            jnp.int32
        )
        counts = lax.psum(jnp.sum(route_hits, axis=0).astype(jnp.float32), ("ctx", "wt"))
        shares = counts / (total_tokens * top_count)
        halves = route_hits.reshape(2, half_rows * top_count, experts)
        ranks = jnp.sum((jnp.cumsum(halves, axis=1) - halves) * halves, axis=2).reshape(-1)
        half_index = jnp.arange(tok_rows * top_count, dtype=jnp.int32) // (half_rows * top_count)
        slot_index = route_flat * slot_rows + half_index * capacity + ranks
        slot_owner = (
            jnp.full((experts * slot_rows,), tok_rows * top_count, jnp.int32)
            .at[slot_index]
            .set(jnp.arange(tok_rows * top_count, dtype=jnp.int32))
        )
        slot_shape = (experts // local_experts, local_experts, slot_rows, model_width)
        padded = jnp.concatenate([normed_two_low, jnp.zeros((1, model_width), jnp.bfloat16)], axis=0)
        outgoing = padded[slot_owner // top_count].reshape(slot_shape)
        arrived = move_slots(outgoing)
        gate_pre = jnp.einsum("nesd,edf->nesf", arrived, w_gate, preferred_element_type=jnp.float32)
        up_pre = jnp.einsum("nesd,edf->nesf", arrived, w_up, preferred_element_type=jnp.float32)
        hidden_low, swiglu_back = jax.vjp(swiglu, gate_pre, up_pre)
        hidden_low = hidden_low.astype(jnp.bfloat16)
        expert_out = jnp.einsum(
            "nesf,efd->nesd", hidden_low, w_down, preferred_element_type=jnp.float32
        ).astype(jnp.bfloat16)
        returned = move_slots(expert_out).reshape(experts * slot_rows, model_width)
        picked = returned[slot_index].reshape(tok_rows, top_count, model_width)
        mixture = jnp.einsum("tk,tkd->td", gate_values, picked, preferred_element_type=jnp.float32)
        output = (residual + mixture).astype(jnp.bfloat16)
        grad_gates = jnp.einsum("td,tkd->tk", grad_out, picked, preferred_element_type=jnp.float32)
        grad_routed = (
            (gate_values[:, :, None] * grad_out[:, None, :])
            .astype(jnp.bfloat16)
            .reshape(-1, model_width)
        )
        grad_routed = jnp.concatenate([grad_routed, jnp.zeros((1, model_width), jnp.bfloat16)], axis=0)
        grad_arrived = move_slots(grad_routed[slot_owner].reshape(slot_shape))
        grad_hidden = jnp.einsum(
            "nesd,efd->nesf", grad_arrived, w_down, preferred_element_type=jnp.float32
        )
        grad_w_down = jnp.einsum(
            "nesf,nesd->efd", hidden_low, grad_arrived, preferred_element_type=jnp.float32
        )
        grad_gate_pre, grad_up_pre = swiglu_back(grad_hidden)
        gate_grad_low = grad_gate_pre.astype(jnp.bfloat16)
        up_grad_low = grad_up_pre.astype(jnp.bfloat16)
        grad_w_gate = jnp.einsum(
            "nesd,nesf->edf", arrived, gate_grad_low, preferred_element_type=jnp.float32
        )
        grad_w_up = jnp.einsum(
            "nesd,nesf->edf", arrived, up_grad_low, preferred_element_type=jnp.float32
        )
        grad_slots = (
            jnp.einsum("nesf,edf->nesd", gate_grad_low, w_gate, preferred_element_type=jnp.float32)
            + jnp.einsum("nesf,edf->nesd", up_grad_low, w_up, preferred_element_type=jnp.float32)
        ).astype(jnp.bfloat16)
        grad_back = move_slots(grad_slots).reshape(experts * slot_rows, model_width)
        grad_normed_two = jnp.sum(
            grad_back[slot_index].reshape(tok_rows, top_count, model_width).astype(jnp.float32), axis=1
        )
        prob_grad = jnp.broadcast_to(experts * shares / total_tokens, router_probs.shape)
        (grad_logits,) = router_back((grad_gates, prob_grad))
        logits_low = grad_logits.astype(jnp.bfloat16)
        grad_normed_two = grad_normed_two + jnp.einsum(
            "te,de->td", logits_low, w_router_all, preferred_element_type=jnp.float32
        )
        grad_w_router = jnp.einsum(
            "td,te->de", normed_two_low, logits_low, preferred_element_type=jnp.float32
        )
        router_grad = grad_w_router.T
    grad_residual_part, grad_ffn_gain = ffn_back(grad_normed_two)
    grad_residual = grad_out + grad_residual_part
    grad_pieces = plane_gather(grad_residual.astype(BF))
    if dense:
        out_grad = product(
            [attn_rows], grad_pieces, ((0,), (0,)), (head_cols, model_width), BF
        )
    else:
        out_grad = lax.dot_general(
            attn_rows, jnp.concatenate(grad_pieces, axis=0), tn, preferred_element_type=F32
        ).astype(BF)
    if dense:
        out_sent = after(out_sent, grad_pieces)
        out_diag = swap(out_sent[0], 4), swap(out_sent[1], 2)
        query = after(query, out_sent, out_grad)
    out_grad = lax.all_to_all(
        out_grad.reshape(ctx_count, piece_rows, model_width), "ctx", 0, 0, tiled=True
    )
    head_grads, grad_query_gain, grad_key_gain = pl.pallas_call(
        functools.partial(attend_back_kernel, heads, piece_count),
        out_shape=(
            jax.ShapeDtypeStruct((2 * ctx_count, half_rows, width), BF),
            jax.ShapeDtypeStruct((1, head_dim), F32),
            jax.ShapeDtypeStruct((1, head_dim), F32),
        ),
        in_specs=[SMEM_SPEC] * 2 + [VMEM_SPEC] * (11 + piece_count),
        out_specs=[VMEM_SPEC] * 3,
        scratch_shapes=[
            pltpu.VMEM((stacked, seq_len), F32),
            pltpu.VMEM((stacked, seq_len), F32),
            pltpu.VMEM((seq_len, head_dim), F32),
            pltpu.VMEM((seq_len, head_dim), F32),
            pltpu.VMEM((2 * ctx_count, half_rows, head_cols), BF),
        ],
        compiler_params=pltpu.CompilerParams(vmem_limit_bytes=ATTEND_LIMIT),
        cost_estimate=COST,
    )(
        places,
        first,
        *grad_pieces,
        out_weight,
        query,
        key,
        value,
        raw,
        query_gain_row,
        key_gain_row,
        cosine,
        sine,
        seg_row,
        seg_col,
    )
    head_grads = head_grads.reshape(seq_len, width)
    heads_back = lambda rows, kind: lax.dot_general(
        rows, weight, nt, preferred_element_type=F32
    ).astype(kind)
    if dense:
        step = Order(out_grad)

        def weight_parts(places, kind):
            return product(
                hidden_pieces,
                [step.take(head_grads)],
                ((0,), (0,)),
                (shard_width, width),
                kind,
                starts=places,
            )

        def add_send(got, part, kind=BF):
            total = sum_of([step.take(got), part], kind)
            step.give(total)
            return ring(total)

        (first,) = weight_parts(planes[1:2], BF)
        step.give(first)
        total = ring(first)
        out_x, out_y = add_diag(*step.take((out_blocks[1], out_blocks[2])), *step.take(out_diag))
        step.give(out_x, out_y)
        out_got = swap(out_x, 2), swap(out_y, 4)
        more = weight_parts(planes[jnp.asarray([2, 3, 0])], F32)
        step.give(more)
        total = add_send(total, more[0])
        side = seq_len // 2
        give = product(
            [step.take(head_grads[side:])], [weight], ((1,), (1,)), (side, model_width), BF
        )
        step.give(give)
        got = swap(give, 1)
        keep_part = product(
            [step.take(head_grads[:side])], [weight], ((1,), (1,)), (side, model_width), BF
        )
        step.give(keep_part)
        total = add_send(total, more[1])
        out_parts = step.take(out_grad).reshape(wt_count, block_rows, model_width)
        out_parts = [
            lax.dynamic_index_in_dim(out_parts, planes[j], 0, keepdims=False)
            for j in range(wt_count)
        ]
        step.give(out_parts[1])
        out_total = ring(out_parts[1])
        sums = sum_of([out_blocks[0]] + list(step.take(out_got)), F32)
        step.give(sums)
        sums = sums.reshape(wt_count, tok_rows, model_width)
        kept = sum_of([keep_part, step.take(got)], BF)
        kept_sent = kept[3 * tok_rows : -half_rows], kept[-half_rows:]
        step.give(kept_sent)
        kept_diag = swap(kept_sent[0], 4), swap(kept_sent[1], 2)
        mixed_low = step.take(sums[1]).astype(BF)
        step.give(mixed_low)
        mixed_total = ring(mixed_low)
        weight_grad = sum_of([step.take(total), more[2]], BF)
        step.give(weight_grad)
        weight_x, weight_y = swap(weight_grad, 2), swap(weight_grad, 4)
        half = weight_grad.shape[0] // 2
        weight_x, weight_y = step.take((weight_x, weight_y))
        weight_sent = weight_x[:half], weight_y[half:]
        step.give(weight_sent)
        weight_pieces = [
            weight_grad,
            weight_x,
            weight_y,
            swap(weight_sent[0], 4),
            swap(weight_sent[1], 2),
        ]
        weight_pieces = weight_pieces + [swap(piece, 1) for piece in weight_pieces]
        kept_x, kept_y = add_diag(
            kept[tok_rows : 2 * tok_rows], kept[2 * tok_rows : 3 * tok_rows], *step.take(kept_diag)
        )
        step.give(kept_x, kept_y)
        kept_got = swap(kept_x, 2), swap(kept_y, 4)
        out_total = add_send(out_total, out_parts[2])
        mixed_total = add_send(mixed_total, sums[2])
        kept_got = step.take(kept_got)
        grad_normed_one = sum_of([kept[:tok_rows]] + list(kept_got), F32)
    else:
        hidden_rows = jnp.concatenate(hidden_pieces, axis=0)
        weight_grad = lax.dot_general(hidden_rows, head_grads, tn, preferred_element_type=F32)
        weight_grad = lax.psum_scatter(
            weight_grad.astype(BF), "wt", scatter_dimension=0, tiled=True
        )
        weight_grads = jnp.concatenate(plane_gather(weight_grad), axis=0)
        grad_w_query, grad_w_key, grad_w_value = place_weight_grads(
            weight_grads.reshape(ctx_count, -1, width), owners, share, head_dim
        )
        out_grad = lax.psum_scatter(out_grad, "wt", scatter_dimension=0, tiled=True)
        out_grads = jnp.concatenate(plane_gather(out_grad.reshape(-1, model_width)), axis=0)
        grad_w_output = place_rows(
            out_grads.reshape(ctx_count, own_chunks, piece_rows, model_width), owners
        ).reshape(w_output.shape)
        grad_normed_one = plane_scatter(heads_back, head_grads)
    grad_inputs_part, grad_attn_gain = attn_back(grad_normed_one)
    grad_inputs = grad_residual + grad_inputs_part

    part = head_dim // wt_count
    prob_sums = jnp.sum(router_probs, axis=0)
    prob_row = jnp.zeros((shard_width - 2 * part,), F32)
    if dense:
        prob_row = lax.dynamic_update_slice_in_dim(prob_row, prob_sums, plane * experts, 0)
    gains = jnp.concatenate(
        [
            grad_query_gain.reshape(wt_count, part),
            grad_key_gain.reshape(wt_count, part),
            jnp.broadcast_to(prob_row[None], (wt_count, shard_width - 2 * part)),
        ],
        axis=1,
    )
    small = jnp.concatenate([router_grad, grad_ffn_gain[None], grad_attn_gain[None]], axis=0)
    small = small.reshape(experts + 2, wt_count, shard_width).transpose(1, 0, 2)
    small = jnp.concatenate([small, gains[:, None]], axis=1)[planes]
    if dense:
        out_total = add_send(out_total, out_parts[3])
        mixed_total = add_send(mixed_total, sums[3])
        small_low = step.take(small[1])
        small_total = ring(small_low)
        out_total = sum_of([step.take(out_total), out_parts[0]], BF)
        step.give(out_total)
        out_x, out_y = swap(out_total, 2), swap(out_total, 4)
        small_total = add_send(small_total, small[2], F32)
        grad_w_query, grad_w_key, grad_w_value = place_weight_pieces(
            step.take(weight_pieces), owners, share, head_dim
        )
        step.give(grad_w_value)
        out_x, out_y = step.take((out_x, out_y))
        half = out_total.shape[0] // 2
        out_sent = out_x[:half], out_y[half:]
        step.give(out_sent)
        out_pieces = [out_total, out_x, out_y, swap(out_sent[0], 4), swap(out_sent[1], 2)]
        out_pieces = out_pieces + [swap(piece, 1) for piece in out_pieces]
        small_total = add_send(small_total, small[3], F32)
        output = step.take(mixed_total).astype(F32) + sums[0]
        output = (residual + output).astype(BF)
        step.give(output)
        small = step.take(small_total) + small[0]
        step.give(small)
        grad_w_output = place_row_pieces(step.take(out_pieces), owners, own_chunks)
        grad_w_output = grad_w_output.reshape(w_output.shape)
        small = axis_sum(small, "ctx")
    else:
        small = ring_sum([small[j] for j in range(wt_count)], F32)
        small = axis_sum(small, "ctx")
    if dense:
        prob_sums = small[experts + 2, 2 * part : 2 * part + wt_count * experts]
        prob_sums = jnp.sum(prob_sums.reshape(wt_count, experts), axis=0)
    else:
        prob_sums = axis_sum(axis_sum(prob_sums[None], "ctx"), "wt")[0]
    balance = experts * experts * shares * (prob_sums / total_tokens)
    loss_value = jnp.mean(balance)
    return (
        output[None],
        loss_value,
        balance,
        grad_inputs[None],
        small[experts + 1],
        small[experts],
        small[experts + 2, :part],
        small[experts + 2, part : 2 * part],
        grad_w_query,
        grad_w_key,
        grad_w_value,
        grad_w_output,
        small[:experts].T,
        grad_w_gate,
        grad_w_up,
        grad_w_down,
    )


def solution(mesh):
    in_specs = (
        P("wt", "ctx", None),
        P("wt", "ctx", None),
        P("wt", None),
        P("wt", "ctx", None),
        P(),
        P(),
        P(),
        P(),
        P(),
        P("wt", None),
        P("wt", None),
        P("wt", None),
        P("wt", None),
        P("wt", None),
        P(("ctx", "wt"), None, None),
        P(("ctx", "wt"), None, None),
        P(("ctx", "wt"), None, None),
    )
    out_specs = (
        P("wt", "ctx", None),
        P(),
        P(),
        P("wt", "ctx", None),
        P("wt"),
        P("wt"),
        P("wt"),
        P("wt"),
        P("wt", None),
        P("wt", None),
        P("wt", None),
        P("wt", None),
        P("wt", None),
        P(("ctx", "wt"), None, None),
        P(("ctx", "wt"), None, None),
        P(("ctx", "wt"), None, None),
    )
    return jax.shard_map(local, mesh=mesh, in_specs=in_specs, out_specs=out_specs, check_vma=False)
```

```python
import functools

import jax
import jax.numpy as jnp
from jax import lax
from jax.experimental import pallas as pl
from jax.experimental.pallas import tpu as pltpu
from jax.sharding import PartitionSpec as P

EPSILON = 1e-06
ROPE_BASE = 1000000.0
MASKED = -1e30
BF = jnp.bfloat16
F32 = jnp.float32
VMEM_SPEC = pl.BlockSpec(memory_space=pltpu.VMEM)
SMEM_SPEC = pl.BlockSpec(memory_space=pltpu.SMEM)
QUERY_ROWS = 128
KEY_ROWS = 256
ATTEND_LIMIT = 60 << 20
COST = pl.CostEstimate(flops=1, bytes_accessed=1, transcendentals=0)


def rms_norm(value_vectors, gain_vector):
    return (
        value_vectors
        * lax.rsqrt(jnp.mean(value_vectors * value_vectors, axis=-1, keepdims=True) + EPSILON)
        * gain_vector
    )


def low_matmul(left, right):
    return jnp.dot(left, right, preferred_element_type=F32)


def swiglu(gate_pre, up_pre):
    return jax.nn.silu(gate_pre) * up_pre


def rope_tables(length, head_width, zero):
    inv_freq = ROPE_BASE ** (-jnp.arange(0, head_width // 2, dtype=F32) * 2.0 / head_width)
    angle_table = (jnp.arange(length, dtype=F32) + zero)[:, None] * inv_freq[None, :]
    cosine, sine = jnp.cos(angle_table), jnp.sin(angle_table)
    return jnp.concatenate([cosine, cosine], 1), jnp.concatenate([-sine, sine], 1)


RELATIVE = (0, 2, 4, 6, 1, 3, 5, 7)


def swap(value, bit):
    count = lax.axis_size("ctx")
    return lax.ppermute(value, "ctx", [(i, i ^ bit) for i in range(count)])


def block_owner(count, me):
    if count == 8:
        return jnp.asarray(RELATIVE, jnp.int32) ^ me
    return jnp.arange(count, dtype=jnp.int32)


def after(value, *others):
    return lax.optimization_barrier((value,) + others)[0]


def plane_pieces(block):
    half = block.shape[0] // 2
    via_x = swap(block, 2)
    via_y = swap(block, 4)
    return [block, via_x, via_y, swap(via_x[:half], 4), swap(via_y[half:], 2)]


def plane_sends(block):
    half = block.shape[0] // 2
    via_x = swap(block, 2)
    via_y = swap(block, 4)
    from_x, from_y = via_x[:half], via_y[half:]
    return [block, via_x, via_y, swap(from_x, 4), swap(from_y, 2)], (from_x, from_y)


def plane_gather(block):
    count = lax.axis_size("ctx")
    if count != 8:
        return [lax.all_gather(block, "ctx", axis=0, tiled=True)]
    mine = plane_pieces(block)
    return mine + [swap(piece, 1) for piece in mine]


def sum_kernel(*refs):
    total = refs[0][...].astype(F32)
    for ref in refs[1:-1]:
        total = total + ref[...].astype(F32)
    refs[-1][...] = total.astype(refs[-1].dtype)


def sum_of(values, kind, limit=24):
    return pl.pallas_call(
        sum_kernel,
        out_shape=jax.ShapeDtypeStruct(values[0].shape, kind),
        in_specs=[VMEM_SPEC] * len(values),
        out_specs=VMEM_SPEC,
        compiler_params=pltpu.CompilerParams(vmem_limit_bytes=limit << 20),
        cost_estimate=COST,
    )(*values)


def add_diag_kernel(part_x_ref, part_y_ref, from_y_ref, from_x_ref, out_x_ref, out_y_ref):
    half = from_y_ref.shape[0]
    low = lambda a, b: (a.astype(F32) + b.astype(F32)).astype(BF)
    out_x_ref[:half] = low(part_x_ref[:half], from_y_ref[...])
    out_x_ref[half:] = part_x_ref[half:].astype(BF)
    out_y_ref[:half] = part_y_ref[:half].astype(BF)
    out_y_ref[half:] = low(part_y_ref[half:], from_x_ref[...])


def add_diag(part_x, part_y, from_y, from_x):
    return pl.pallas_call(
        add_diag_kernel,
        out_shape=(jax.ShapeDtypeStruct(part_x.shape, BF),) * 2,
        in_specs=[VMEM_SPEC] * 4,
        out_specs=[VMEM_SPEC] * 2,
        compiler_params=pltpu.CompilerParams(vmem_limit_bytes=24 << 20),
        cost_estimate=COST,
    )(part_x, part_y, from_y, from_x)


def plane_scatter(multiply, left, fill=None, others=(), last=()):
    count = lax.axis_size("ctx")
    if count != 8:
        parts = multiply(left, BF)
        return lax.psum_scatter(parts, "ctx", scatter_dimension=0, tiled=True).astype(F32)
    side = left.shape[0] // 2
    rows = side // 4
    half = rows // 2
    give = multiply(left[side:], BF)
    got = swap(give, 1)
    keep = multiply(after(left[:side], give), BF)
    kept = sum_of(after([keep, got], others), BF)
    sends = kept[3 * rows : -half], kept[-half:]
    from_y, from_x = swap(sends[0], 4), swap(sends[1], 2)
    from_y, from_x = after((from_y, from_x), fill(sends))
    part_x, part_y = add_diag(kept[rows : 2 * rows], kept[2 * rows : 3 * rows], from_y, from_x)
    got = after((swap(part_x, 2), swap(part_y, 4)), last)
    return kept[:rows].astype(F32) + got[0].astype(F32) + got[1].astype(F32)


class Order:
    def __init__(self, *values):
        self.last = values

    def take(self, value):
        return after(value, *self.last)

    def give(self, *values):
        self.last = values


def ring(value):
    count = lax.axis_size("wt")
    return lax.ppermute(value, "wt", [(i, (i + 1) % count) for i in range(count)])


def ring_chunks(block):
    chunks = [block]
    for _ in range(lax.axis_size("wt") - 1):
        chunks.append(ring(chunks[-1]))
    return chunks


def ring_sum(parts, kind):
    total = parts[1]
    for part in parts[2:] + parts[:1]:
        total = ring(total.astype(kind)).astype(F32) + part
    return total


def axis_sum(value, name):
    count = lax.axis_size(name)
    bit = 1
    while bit < count:
        value = value + lax.ppermute(value, name, [(i, i ^ bit) for i in range(count)])
        bit *= 2
    return value


def head_norm(raw, gain):
    scale = lax.rsqrt(jnp.mean(raw * raw, axis=-1, keepdims=True) + EPSILON)
    return raw * scale * gain


def turn(value):
    return pltpu.roll(value, value.shape[-1] // 2, 1)


def tile_mask(seg_col, seg_row, row_start, col_start):
    shape = (seg_col.shape[0], seg_row.shape[1])
    rows = lax.broadcasted_iota(jnp.int32, shape, 0) + row_start
    cols = lax.broadcasted_iota(jnp.int32, shape, 1) + col_start
    return (seg_col == seg_row) & (cols <= rows)


def attend_kernel(
    heads,
    pieces,
    block_ref,
    place_ref,
    first_ref,
    *refs,
):
    attend_body(heads, block_ref, place_ref, first_ref, refs[:pieces], *refs[pieces:])


def joined(refs, rows):
    group, have = [], 0
    for ref in refs:
        for start in range(0, ref.shape[0], rows):
            stop = min(start + rows, ref.shape[0])
            group.append(ref[start:stop])
            have += stop - start
            if have == rows:
                yield group[0] if len(group) == 1 else jnp.concatenate(group, axis=0)
                group, have = [], 0


def attend_body(
    heads,
    block_ref,
    place_ref,
    first_ref,
    hidden_refs,
    weight_ref,
    query_gain_ref,
    key_gain_ref,
    cosine_ref,
    sine_ref,
    seg_row_ref,
    seg_col_ref,
    query_ref,
    key_ref,
    value_ref,
    raw_ref,
    out_ref,
    score_ref,
):
    half = out_ref.shape[1]
    dim = query_gain_ref.shape[1]
    scale = dim ** (-0.5)

    for pair, lhs in enumerate(joined(hidden_refs, 4 * half)):
        raw = jnp.dot(lhs, weight_ref[...], preferred_element_type=F32)
        for piece in range(4):
            start = pl.multiple_of(block_ref[pair * 4 + piece] * half, half)
            spot = pl.ds(start, half)
            cosine, sine = cosine_ref[spot, :], sine_ref[spot, :]
            part = raw[piece * half : (piece + 1) * half]
            for head in range(heads + 1):
                cols = slice(head * dim, (head + 1) * dim)
                gain = query_gain_ref[...] if head < heads else key_gain_ref[...]
                normed = head_norm(part[:, cols], gain)
                roped = (normed * cosine + turn(normed) * sine).astype(BF)
                if head < heads:
                    query_ref[spot, cols] = roped
                else:
                    key_ref[spot, :] = roped
            raw_ref[spot, :] = part[:, : (heads + 1) * dim]
            value_ref[spot, :] = part[:, (heads + 1) * dim :].astype(BF)

    seq = key_ref.shape[0]
    stacked = heads * QUERY_ROWS

    def attend(index, carry):
        row_start = pl.multiple_of(index * QUERY_ROWS, QUERY_ROWS)
        row_spot = pl.ds(row_start, QUERY_ROWS)
        query = jnp.concatenate(
            [query_ref[row_spot, h * dim : (h + 1) * dim] for h in range(heads)], axis=0
        )
        seg_col = seg_col_ref[row_spot, :]
        low = first_ref[index] // KEY_ROWS
        high = (row_start + QUERY_ROWS + KEY_ROWS - 1) // KEY_ROWS

        def scores(tile, top):
            start = pl.multiple_of(tile * KEY_ROWS, KEY_ROWS)
            spot = pl.ds(start, KEY_ROWS)
            raw = lax.dot_general(
                query, key_ref[spot, :], (((1,), (1,)), ((), ())), preferred_element_type=F32
            )
            allowed = tile_mask(seg_col, seg_row_ref[:, spot], row_start, start)
            raw = raw.reshape(heads, QUERY_ROWS, KEY_ROWS) * scale
            masked = jnp.where(allowed[None], raw, MASKED).reshape(stacked, KEY_ROWS)
            score_ref[:, spot] = masked
            return jnp.maximum(top, jnp.max(masked, axis=1, keepdims=True))

        top = lax.fori_loop(low, high, scores, jnp.full((stacked, 1), MASKED, F32))

        def gather(tile, state):
            total, acc = state
            start = pl.multiple_of(tile * KEY_ROWS, KEY_ROWS)
            spot = pl.ds(start, KEY_ROWS)
            probs = jnp.exp(score_ref[:, spot] - top)
            total = total + jnp.sum(probs, axis=1, keepdims=True)
            acc = acc + jnp.dot(
                probs.astype(BF), value_ref[spot, :], preferred_element_type=F32
            )
            return total, acc

        total, acc = lax.fori_loop(
            low, high, gather, (jnp.zeros((stacked, 1), F32), jnp.zeros((stacked, dim), F32))
        )
        result = (acc / total).astype(BF)
        for head in range(heads):
            for piece in range(QUERY_ROWS // half):
                spot = place_ref[index * (QUERY_ROWS // half) + piece]
                begin = head * QUERY_ROWS + piece * half
                out_ref[spot, :, head * dim : (head + 1) * dim] = result[begin : begin + half]
        return carry

    lax.fori_loop(0, seq // QUERY_ROWS, attend, 0)


def attend_back_kernel(heads, pieces, place_ref, first_ref, *refs):
    attend_back_body(heads, place_ref, first_ref, refs[:pieces], *refs[pieces:])


def attend_back_body(
    heads,
    place_ref,
    first_ref,
    piece_refs,
    out_weight_ref,
    query_ref,
    key_ref,
    value_ref,
    raw_ref,
    query_gain_ref,
    key_gain_ref,
    cosine_ref,
    sine_ref,
    seg_row_ref,
    seg_col_ref,
    out_ref,
    query_gain_grad_ref,
    key_gain_grad_ref,
    score_ref,
    prob_grad_ref,
    key_grad_ref,
    value_grad_ref,
    grad_ref,
):
    half = grad_ref.shape[1]
    spot = 0
    for part in joined(piece_refs, 4 * half):
        part = lax.dot_general(
            part, out_weight_ref[...], (((1,), (1,)), ((), ())), preferred_element_type=F32
        ).astype(BF)
        for piece in range(4):
            grad_ref[spot] = part[piece * half : (piece + 1) * half]
            spot += 1
    dim = query_gain_ref.shape[1]
    scale = dim ** (-0.5)
    seq = key_ref.shape[0]
    stacked = heads * QUERY_ROWS
    pieces = QUERY_ROWS // half
    key_grad_ref[...] = jnp.zeros_like(key_grad_ref)
    value_grad_ref[...] = jnp.zeros_like(value_grad_ref)
    query_gain_grad_ref[...] = jnp.zeros_like(query_gain_grad_ref)
    key_gain_grad_ref[...] = jnp.zeros_like(key_gain_grad_ref)

    def unrope(grad, raw, gain, cosine, sine):
        norm_scale = lax.rsqrt(jnp.mean(raw * raw, axis=-1, keepdims=True) + EPSILON)
        unit = raw * norm_scale
        grad = grad * cosine + turn(grad * sine)
        gain_grad = jnp.sum(grad * unit, axis=0, keepdims=True)
        grad = grad * gain
        grad = norm_scale * (grad - unit * jnp.mean(grad * unit, axis=-1, keepdims=True))
        return grad, gain_grad

    def back(index, carry):
        row_start = pl.multiple_of(index * QUERY_ROWS, QUERY_ROWS)
        row_spot = pl.ds(row_start, QUERY_ROWS)
        places = [place_ref[index * pieces + piece] for piece in range(pieces)]
        query = jnp.concatenate(
            [query_ref[row_spot, h * dim : (h + 1) * dim] for h in range(heads)], axis=0
        )
        grad = jnp.concatenate(
            [
                grad_ref[place, :, h * dim : (h + 1) * dim]
                for h in range(heads)
                for place in places
            ],
            axis=0,
        )
        seg_col = seg_col_ref[row_spot, :]
        low = first_ref[index] // KEY_ROWS
        high = (row_start + QUERY_ROWS + KEY_ROWS - 1) // KEY_ROWS

        def scores(tile, top):
            start = pl.multiple_of(tile * KEY_ROWS, KEY_ROWS)
            spot = pl.ds(start, KEY_ROWS)
            raw = lax.dot_general(
                query, key_ref[spot, :], (((1,), (1,)), ((), ())), preferred_element_type=F32
            )
            allowed = tile_mask(seg_col, seg_row_ref[:, spot], row_start, start)
            raw = raw.reshape(heads, QUERY_ROWS, KEY_ROWS) * scale
            masked = jnp.where(allowed[None], raw, MASKED).reshape(stacked, KEY_ROWS)
            score_ref[:, spot] = masked
            return jnp.maximum(top, jnp.max(masked, axis=1, keepdims=True))

        top = lax.fori_loop(low, high, scores, jnp.full((stacked, 1), MASKED, F32))

        def probabilities(tile, state):
            total, inner = state
            start = pl.multiple_of(tile * KEY_ROWS, KEY_ROWS)
            spot = pl.ds(start, KEY_ROWS)
            probs = jnp.exp(score_ref[:, spot] - top)
            prob_grad = lax.dot_general(
                grad, value_ref[spot, :], (((1,), (1,)), ((), ())), preferred_element_type=F32
            )
            score_ref[:, spot] = probs
            prob_grad_ref[:, spot] = prob_grad
            total = total + jnp.sum(probs, axis=1, keepdims=True)
            inner = inner + jnp.sum(probs * prob_grad, axis=1, keepdims=True)
            return total, inner

        zero = jnp.zeros((stacked, 1), F32)
        total, inner = lax.fori_loop(low, high, probabilities, (zero, zero))
        share = 1.0 / total
        inner = inner * share

        def gradients(tile, acc):
            start = pl.multiple_of(tile * KEY_ROWS, KEY_ROWS)
            spot = pl.ds(start, KEY_ROWS)
            probs = score_ref[:, spot] * share
            score_grad = (probs * (prob_grad_ref[:, spot] - inner) * scale).astype(BF)
            acc = acc + jnp.dot(score_grad, key_ref[spot, :], preferred_element_type=F32)
            key_grad_ref[spot, :] += lax.dot_general(
                score_grad, query, (((0,), (0,)), ((), ())), preferred_element_type=F32
            )
            value_grad_ref[spot, :] += lax.dot_general(
                probs.astype(BF), grad, (((0,), (0,)), ((), ())), preferred_element_type=F32
            )
            return acc

        acc = lax.fori_loop(low, high, gradients, jnp.zeros((stacked, dim), F32))
        cosine, sine = cosine_ref[row_spot, :], sine_ref[row_spot, :]
        for head in range(heads):
            cols = slice(head * dim, (head + 1) * dim)
            part = acc[head * QUERY_ROWS : (head + 1) * QUERY_ROWS]
            part, gain_grad = unrope(
                part, raw_ref[row_spot, cols], query_gain_ref[...], cosine, sine
            )
            query_gain_grad_ref[...] += gain_grad
            part = part.astype(BF)
            for piece in range(pieces):
                out_ref[places[piece], :, cols] = part[piece * half : (piece + 1) * half]
        return carry

    lax.fori_loop(0, seq // QUERY_ROWS, back, 0)

    def finish(index, carry):
        row_start = pl.multiple_of(index * QUERY_ROWS, QUERY_ROWS)
        row_spot = pl.ds(row_start, QUERY_ROWS)
        key_cols = slice(heads * dim, (heads + 1) * dim)
        value_cols = slice((heads + 1) * dim, (heads + 2) * dim)
        part, gain_grad = unrope(
            key_grad_ref[row_spot, :],
            raw_ref[row_spot, key_cols],
            key_gain_ref[...],
            cosine_ref[row_spot, :],
            sine_ref[row_spot, :],
        )
        key_gain_grad_ref[...] += gain_grad
        part = part.astype(BF)
        value = value_grad_ref[row_spot, :].astype(BF)
        for piece in range(pieces):
            place = place_ref[index * pieces + piece]
            out_ref[place, :, key_cols] = part[piece * half : (piece + 1) * half]
            out_ref[place, :, value_cols] = value[piece * half : (piece + 1) * half]
        return carry

    lax.fori_loop(0, seq // QUERY_ROWS, finish, 0)


def one_hot(hit):
    return hit.astype(F32).astype(BF)


def select_kernel(groups, joint, *refs):
    target_ref, mine_ref, other_ref = refs[sum(groups) :]
    slots = mine_ref.shape[0] // 2
    target = target_ref[...]
    half = target.shape[1] // 8
    index = lax.broadcasted_iota(jnp.int32, (2 * slots, target.shape[1]), 0)
    pick = one_hot((index == target[0:1]) | (index == target[1:2]))
    for k in range(2):
        rows = []
        if joint:
            for ref in refs[: groups[0]]:
                for start in range(k * half, ref.shape[0], 2 * half):
                    rows.append(ref[start : start + half])
        else:
            first = k * groups[0]
            rows = [ref[...] for ref in refs[first : first + groups[k]]]
        picked = jnp.dot(pick, jnp.concatenate(rows, axis=0), preferred_element_type=F32)
        picked = picked.astype(BF)
        mine_ref[k * slots : (k + 1) * slots] = picked[:slots]
        other_ref[k * slots : (k + 1) * slots] = picked[slots:]


def select_rows(pieces, others, target, slots):
    width = pieces[0].shape[1]
    return pl.pallas_call(
        functools.partial(select_kernel, (len(pieces), len(others)), not others),
        out_shape=(jax.ShapeDtypeStruct((2 * slots, width), BF),) * 2,
        in_specs=[VMEM_SPEC] * (len(pieces) + len(others) + 1),
        out_specs=[VMEM_SPEC] * 2,
        compiler_params=pltpu.CompilerParams(vmem_limit_bytes=24 << 20),
        cost_estimate=COST,
    )(*pieces, *others, target)


def spread_kernel(chunks, part, grouped, *refs):
    mine_refs, other_refs = refs[:chunks], refs[chunks : 2 * chunks]
    target_ref, first_ref, second_ref = refs[2 * chunks : 2 * chunks + 3]
    outs = refs[2 * chunks + 3 :]
    slots = mine_refs[0].shape[0] // 2
    half = first_ref.shape[0] // chunks
    rows = 2 * half
    spot = slice(part * slots, (part + 1) * slots)
    for j in range(chunks):
        values = jnp.concatenate([mine_refs[j][spot], other_refs[j][spot]], axis=0)
        target = target_ref[j]
        index = lax.broadcasted_iota(jnp.int32, (4 * rows, 2 * slots), 1)
        pick = one_hot((index == target[:, 0:1]) | (index == target[:, 1:2]))
        spread = jnp.dot(pick, values, preferred_element_type=F32).astype(BF)
        for k in range(3):
            ref, start = (outs[k], j * rows) if grouped else (outs[3 * j + k], 0)
            ref[start : start + rows] = spread[k * rows : (k + 1) * rows]
        if grouped:
            ref = first_ref if 2 * j < chunks else second_ref
            start = j % (chunks // 2) * rows
            ref[start : start + rows] = spread[3 * rows :]
        else:
            first_ref[j * half : (j + 1) * half] = spread[3 * rows : 3 * rows + half]
            second_ref[j * half : (j + 1) * half] = spread[3 * rows + half :]


def spread_rows(mine, other, target, rows, part, grouped):
    chunks = len(mine)
    slots, width = mine[0].shape
    low = lambda count: jax.ShapeDtypeStruct((count, width), BF)
    blocks = (low(chunks * rows),) * 3 if grouped else (low(rows),) * (3 * chunks)
    outs = pl.pallas_call(
        functools.partial(spread_kernel, chunks, part, grouped),
        out_shape=(low(chunks * rows // 2),) * 2 + blocks,
        in_specs=[VMEM_SPEC] * (2 * chunks + 1),
        out_specs=[VMEM_SPEC] * (2 + len(blocks)),
        compiler_params=pltpu.CompilerParams(
            vmem_limit_bytes=(16 << 20) if chunks == 1 else (36 << 20)
        ),
        cost_estimate=COST,
    )(*mine, *other, target)
    return outs[:2], outs[2:]


def expert_kernel(expert_ref, mine_ref, other_ref, *refs):
    slots = mine_ref.shape[0] // 2
    rows, grads = slice(0, slots), slice(slots, 2 * slots)
    expert_body(
        expert_ref, mine_ref.at[rows], other_ref.at[rows], mine_ref.at[grads], other_ref.at[grads], *refs
    )


def expert_body(
    expert_ref,
    mine_ref,
    other_ref,
    grad_mine_ref,
    grad_other_ref,
    target_ref,
    route_ref,
    gate_ref,
    up_ref,
    down_ref,
    router_ref,
    back_mine_ref,
    back_other_ref,
    hidden_ref,
    gate_grad_ref,
    up_grad_ref,
    routed_ref,
    router_grad_ref,
):
    slots = mine_ref.shape[0]
    experts = router_ref.shape[0]
    tokens = target_ref.shape[1]
    rows = jnp.concatenate([mine_ref[...], other_ref[...]], axis=0)
    nt = (((1,), (1,)), ((), ()))
    tn = (((0,), (0,)), ((), ()))
    gate_pre = jnp.dot(rows, gate_ref[...], preferred_element_type=F32)
    up_pre = jnp.dot(rows, up_ref[...], preferred_element_type=F32)
    sigmoid = 1.0 / (1.0 + jnp.exp(-gate_pre))
    silu = gate_pre * sigmoid
    hidden = (silu * up_pre).astype(BF)
    hidden_ref[...] = hidden
    result = jnp.dot(hidden, down_ref[...], preferred_element_type=F32).astype(BF).astype(F32)
    slot_iota = lax.broadcasted_iota(jnp.int32, (slots, tokens), 0)
    expert_iota = lax.broadcasted_iota(jnp.int32, (experts, tokens), 0)
    masks = []
    for side in range(2):
        pick = one_hot(slot_iota == target_ref[side : side + 1, :])
        chosen = expert_iota == route_ref[side, 0:1, :]
        for k in range(1, route_ref.shape[1]):
            chosen = chosen | (expert_iota == route_ref[side, k : k + 1, :])
        masks.append(lax.dot_general(pick, one_hot(chosen), nt, preferred_element_type=F32))
    chosen = jnp.concatenate(masks, axis=0) > 0.5
    logits = lax.dot_general(rows, router_ref[...], nt, preferred_element_type=F32)
    top = jnp.max(jnp.where(chosen, logits, MASKED), axis=1, keepdims=True)
    weights = jnp.where(chosen, jnp.exp(logits - top), 0.0)
    total = jnp.sum(weights, axis=1, keepdims=True)
    gates = weights / jnp.where(total > 0.0, total, 1.0)
    mine = lax.broadcasted_iota(jnp.int32, gates.shape, 1) == expert_ref[0]
    gate = jnp.sum(jnp.where(mine, gates, 0.0), axis=1, keepdims=True)
    gated = (result * gate).astype(BF)
    back_mine_ref[slots:] = gated[:slots]
    back_other_ref[slots:] = gated[slots:]
    grad = jnp.concatenate([grad_mine_ref[...], grad_other_ref[...]], axis=0).astype(F32)
    gate_value_grad = jnp.sum(grad * result, axis=1, keepdims=True)
    routed = (grad * gate).astype(BF)
    routed_ref[...] = routed
    hidden_grad = lax.dot_general(routed, down_ref[...], nt, preferred_element_type=F32)
    gate_low = (hidden_grad * up_pre * sigmoid * (1.0 + gate_pre * (1.0 - sigmoid))).astype(BF)
    up_low = (hidden_grad * silu).astype(BF)
    gate_grad_ref[...] = gate_low
    up_grad_ref[...] = up_low
    logit_grad = (gate_value_grad * gate) * (jnp.where(mine, 1.0, 0.0) - gates)
    high = logit_grad.astype(BF)
    low = (logit_grad - high.astype(F32)).astype(BF)
    both = jnp.concatenate([high, low], axis=1)
    router = router_ref[...]
    slot_grad = lax.dot_general(gate_low, gate_ref[...], nt, preferred_element_type=F32)
    slot_grad = slot_grad + lax.dot_general(up_low, up_ref[...], nt, preferred_element_type=F32)
    slot_grad = slot_grad + jnp.dot(
        both, jnp.concatenate([router, router], axis=0), preferred_element_type=F32
    )
    slot_grad = slot_grad.astype(BF)
    back_mine_ref[:slots] = slot_grad[:slots]
    back_other_ref[:slots] = slot_grad[slots:]
    router_grad = lax.dot_general(both, rows, tn, preferred_element_type=F32)
    router_grad_ref[...] = router_grad[:experts] + router_grad[experts:]


def expert_rows(expert, mine, other, target, route, *weights):
    count, width = mine.shape
    ff = weights[0].shape[1]
    experts = weights[3].shape[0]
    low = lambda cols: jax.ShapeDtypeStruct((count, cols), BF)
    return pl.pallas_call(
        expert_kernel,
        out_shape=(
            low(width),
            low(width),
            low(ff),
            low(ff),
            low(ff),
            low(width),
            jax.ShapeDtypeStruct((experts, width), F32),
        ),
        in_specs=[SMEM_SPEC] + [VMEM_SPEC] * 8,
        out_specs=[VMEM_SPEC] * 7,
        compiler_params=pltpu.CompilerParams(vmem_limit_bytes=40 << 20),
        cost_estimate=COST,
    )(expert, mine, other, target, route, *weights)


def place_kernel(share, order_ref, owner_ref, part_ref, query_ref, key_ref, value_ref):
    cols = query_ref.shape[1]
    dim = key_ref.shape[1]
    part = part_ref[0]
    query_ref[...] = part[:, :cols].astype(F32)
    key = part[:, cols : cols + dim].astype(F32)
    value = part[:, cols + dim :].astype(F32)
    first = pl.program_id(0) % share == 0

    @pl.when(first)
    def _():
        key_ref[...] = key
        value_ref[...] = value

    @pl.when(jnp.logical_not(first))
    def _():
        key_ref[...] += key
        value_ref[...] += value


def place_weight_grads(parts, owner, share, dim):
    count, rows, width = parts.shape
    cols = width - 2 * dim
    if count == 8 and share == 2:
        order = jnp.asarray([0, 4, 1, 5, 2, 6, 3, 7], jnp.int32)
    else:
        order = jnp.arange(count, dtype=jnp.int32)
    owner = owner[order]
    group = lambda g, order, owner: (0, owner[g] // share)
    return pl.pallas_call(
        functools.partial(place_kernel, share),
        grid_spec=pltpu.PrefetchScalarGridSpec(
            num_scalar_prefetch=2,
            grid=(count,),
            in_specs=[pl.BlockSpec((1, rows, width), lambda g, order, owner: (order[g], 0, 0))],
            out_specs=[
                pl.BlockSpec((rows, cols), lambda g, order, owner: (0, owner[g])),
                pl.BlockSpec((rows, dim), group),
                pl.BlockSpec((rows, dim), group),
            ],
        ),
        out_shape=(
            jax.ShapeDtypeStruct((rows, cols * count), F32),
            jax.ShapeDtypeStruct((rows, dim * count // share), F32),
            jax.ShapeDtypeStruct((rows, dim * count // share), F32),
        ),
        compiler_params=pltpu.CompilerParams(vmem_limit_bytes=ATTEND_LIMIT),
        cost_estimate=COST,
    )(order, owner, parts)


def rows_kernel(owner_ref, part_ref, out_ref):
    out_ref[:, 0] = part_ref[0].astype(F32)


def place_rows(parts, owner):
    count, chunks, rows, width = parts.shape
    return pl.pallas_call(
        rows_kernel,
        grid_spec=pltpu.PrefetchScalarGridSpec(
            num_scalar_prefetch=1,
            grid=(count,),
            in_specs=[pl.BlockSpec((1, chunks, rows, width), lambda g, owner: (g, 0, 0, 0))],
            out_specs=pl.BlockSpec(
                (chunks, 1, rows, width), lambda g, owner: (0, owner[g], 0, 0)
            ),
        ),
        out_shape=jax.ShapeDtypeStruct((chunks, count, rows, width), F32),
        compiler_params=pltpu.CompilerParams(vmem_limit_bytes=ATTEND_LIMIT),
        cost_estimate=COST,
    )(owner, parts)


def place_pieces_kernel(share, owner_ref, *refs):
    pieces, (query_ref, key_ref, value_ref) = refs[:-3], refs[-3:]
    rows, dim = query_ref.shape[0], key_ref.shape[1] * share // 8
    cols = query_ref.shape[1] // 8
    for k in range(4):
        both = [
            [ref[...].astype(F32) for ref in refs_of]
            for refs_of in (block_refs(pieces, k), block_refs(pieces, k + 4))
        ]
        both = [p[0] if len(p) == 1 else jnp.concatenate(p, axis=0) for p in both]
        for side in range(2):
            start = pl.multiple_of(owner_ref[k + 4 * side] * cols, cols)
            query_ref[:, pl.ds(start, cols)] = both[side][:, :cols]
        start = pl.multiple_of(owner_ref[k] // share * dim, dim)
        key_ref[:, pl.ds(start, dim)] = both[0][:, cols : cols + dim] + both[1][:, cols : cols + dim]
        value_ref[:, pl.ds(start, dim)] = both[0][:, cols + dim :] + both[1][:, cols + dim :]


def block_refs(pieces, k):
    first = k // 4 * 5 + k % 4
    return pieces[first : first + 2] if k % 4 == 3 else pieces[first : first + 1]


def place_weight_pieces(pieces, owner, share, dim):
    rows, width = pieces[0].shape
    cols = width - 2 * dim
    return pl.pallas_call(
        functools.partial(place_pieces_kernel, share),
        out_shape=(
            jax.ShapeDtypeStruct((rows, cols * 8), F32),
            jax.ShapeDtypeStruct((rows, dim * 8 // share), F32),
            jax.ShapeDtypeStruct((rows, dim * 8 // share), F32),
        ),
        in_specs=[SMEM_SPEC] + [VMEM_SPEC] * len(pieces),
        out_specs=[VMEM_SPEC] * 3,
        compiler_params=pltpu.CompilerParams(vmem_limit_bytes=ATTEND_LIMIT),
        cost_estimate=COST,
    )(owner, *pieces)


def row_pieces_kernel(owner_ref, *refs):
    pieces, out_ref = refs[:-1], refs[-1]
    chunks, _, rows, _ = out_ref.shape
    for k in range(8):
        parts = [ref[...] for ref in block_refs(pieces, k)]
        part = parts[0] if len(parts) == 1 else jnp.concatenate(parts, axis=0)
        for chunk in range(chunks):
            out_ref[chunk, owner_ref[k]] = part[chunk * rows : (chunk + 1) * rows].astype(F32)


def place_row_pieces(pieces, owner, chunks):
    rows, width = pieces[0].shape
    return pl.pallas_call(
        row_pieces_kernel,
        out_shape=jax.ShapeDtypeStruct((chunks, 8, rows // chunks, width), F32),
        in_specs=[SMEM_SPEC] + [VMEM_SPEC] * len(pieces),
        out_specs=VMEM_SPEC,
        compiler_params=pltpu.CompilerParams(vmem_limit_bytes=ATTEND_LIMIT),
        cost_estimate=COST,
    )(owner, *pieces)


def product_kernel(dims, rows, left_count, right_count, starts, start_ref, *refs):
    lefts, rights = refs[:left_count], refs[left_count : left_count + right_count]
    outs = refs[left_count + right_count :]
    join = lambda parts: parts[0] if len(parts) == 1 else jnp.concatenate(parts, axis=0)
    right = join([ref[...] for ref in rights])
    for k, out_ref in enumerate(outs):
        if starts:
            width = out_ref.shape[0]
            cols = pl.ds(pl.multiple_of(start_ref[k] * width, width), width)
            left = join([ref[:, cols] for ref in lefts])
        else:
            left = join([ref[...] if rows is None else ref[:rows] for ref in lefts])
        out = lax.dot_general(left, right, (dims, ((), ())), preferred_element_type=F32)
        out_ref[...] = out.astype(out_ref.dtype)


def product(lefts, rights, dims, out_shape, kind=F32, rows=None, starts=None, limit=60, tile=None):
    count = 1 if starts is None else starts.shape[0]
    start_arg = jnp.zeros((1,), jnp.int32) if starts is None else starts
    if tile is None:
        left_specs, right_specs = [VMEM_SPEC] * len(lefts), [VMEM_SPEC] * len(rights)
        out_spec = VMEM_SPEC
    else:
        left_specs = [
            pl.BlockSpec((rows or left.shape[0], tile), lambda i: (0, i)) for left in lefts
        ]
        right_specs = [pl.BlockSpec(right.shape, lambda i: (0, 0)) for right in rights]
        out_spec = pl.BlockSpec((tile, out_shape[1]), lambda i: (i, 0))
    outs = pl.pallas_call(
        functools.partial(
            product_kernel, dims, None, len(lefts), len(rights), starts is not None
        ),
        grid=() if tile is None else (out_shape[0] // tile,),
        out_shape=(jax.ShapeDtypeStruct(out_shape, kind),) * count,
        in_specs=[SMEM_SPEC] + left_specs + right_specs,
        out_specs=[out_spec] * count,
        compiler_params=pltpu.CompilerParams(vmem_limit_bytes=limit << 20),
        cost_estimate=COST,
    )(start_arg, *lefts, *rights)
    return outs[0] if starts is None else outs


def move_slots(slot_array):
    return lax.all_to_all(slot_array, ("ctx", "wt"), split_axis=0, concat_axis=0, tiled=True)


def local(
    tokens,
    cotangent,
    segments,
    routes,
    pair_order,
    attn_gain,
    ffn_gain,
    query_gain,
    key_gain,
    w_query,
    key_weight,
    value_weight,
    w_output,
    w_router,
    w_gate,
    w_up,
    w_down,
):
    ctx_count = lax.axis_size("ctx")
    wt_count = lax.axis_size("wt")
    me = lax.axis_index("ctx")
    plane = lax.axis_index("wt")
    inputs = tokens[0].astype(F32)
    tok_rows, model_width = inputs.shape
    half_rows = tok_rows // 2
    head_dim = query_gain.shape[0]
    experts = w_router.shape[1]
    top_count = routes.shape[2]
    seq_len = segments.shape[1]
    total_tokens = tok_rows * ctx_count * wt_count
    heads = w_query.shape[1] // head_dim // ctx_count
    kv_heads = key_weight.shape[1] // head_dim
    share = ctx_count // kv_heads
    head_cols = heads * head_dim
    group = me // share
    shard_width = model_width // wt_count
    capacity = max(2, half_rows * top_count * 5 // (4 * experts))
    dense = ctx_count == 8 and wt_count == 4 and w_gate.shape[0] == 1
    nt = (((1,), (1,)), ((), ()))
    tn = (((0,), (0,)), ((), ()))
    owners = block_owner(ctx_count, me)
    planes = (plane - jnp.arange(wt_count, dtype=jnp.int32)) % wt_count

    normed_one, attn_back = jax.vjp(rms_norm, inputs, attn_gain)
    normed_low = normed_one.astype(BF)
    kv_start = group * head_dim
    own_weight = jnp.concatenate(
        [
            lax.dynamic_slice_in_dim(w_query, me * head_cols, head_cols, 1),
            lax.dynamic_slice_in_dim(key_weight, kv_start, head_dim, 1),
            lax.dynamic_slice_in_dim(value_weight, kv_start, head_dim, 1),
        ],
        axis=1,
    )
    own_chunks = ctx_count // wt_count
    piece_rows = head_cols // ctx_count
    out_piece = lax.dynamic_index_in_dim(
        w_output.reshape(own_chunks, ctx_count, piece_rows, model_width), me, 1, keepdims=False
    )
    cot = cotangent[0]
    if dense:
        cap_rows = 2 * capacity
        slots = 4 * cap_rows
        expert = me * wt_count + plane
        triangle = jnp.triu(jnp.ones((tok_rows, tok_rows), F32)).astype(BF)
        offsets = (jnp.arange(ctx_count, dtype=jnp.int32) % 4) * cap_rows

        def tables(near):
            near = near.astype(jnp.int32).reshape(-1, ctx_count, top_count, tok_rows)

            def slot_of(routed_to):
                hits = jnp.any(near == routed_to, axis=2)
                ranks = jnp.dot(hits.astype(BF), triangle, preferred_element_type=F32)
                place = ranks.astype(jnp.int32) - 1 + offsets[None, :, None]
                return jnp.where(hits, place, -1).reshape(-1, 2, 4 * tok_rows)

            own_slot = slot_of(expert)
            other_slot = slot_of((me ^ 1) * wt_count + plane)[:, 0]
            target = jnp.stack(
                [own_slot[:, 0], jnp.where(other_slot < 0, -1, other_slot + slots)], axis=1
            )
            near_routes = (
                near.reshape(-1, 2, 4, top_count, tok_rows)
                .transpose(0, 1, 3, 2, 4)
                .reshape(-1, 2, top_count, 4 * tok_rows)
            )
            indices = jnp.arange(experts, dtype=jnp.int32)[:, None, None, None, None]
            counts = jnp.sum((near[None] == indices).astype(F32), axis=(1, 2, 3, 4))
            return own_slot, target, target.transpose(0, 2, 1), near_routes, counts

        block_rows = own_chunks * piece_rows
        out_piece = out_piece.reshape(block_rows, model_width)
        ticks = [(out_piece, own_weight), (ring(out_piece), ring(own_weight))]
        own = after(normed_low, out_piece, own_weight)
        via_x, via_y = swap(own, 2), swap(own, 4)
        near = after(routes[0].T.astype(BF), own)
        near_x, near_y = swap(near, 2), swap(near, 4)
        sent = via_x[:half_rows], via_y[half_rows:]
        diag_a, diag_b = swap(sent[0], 4), swap(sent[1], 2)
        near_x, near_y = after((near_x, near_y), sent)
        near = jnp.concatenate([near, near_x, near_y, swap(near_x, 4)], axis=0)
        near = jnp.concatenate([near, swap(near, 1)], axis=0)
        hidden_pieces = [own, via_x, via_y, diag_a, diag_b]
        hidden_pieces = hidden_pieces + [swap(piece, 1) for piece in hidden_pieces]
        ticks[1], near, cot_block = after((ticks[1], near, cot), ticks[1], hidden_pieces, near)
        near_rows = near.shape[0]
        tiny = jnp.concatenate([near, w_router.T.reshape(-1, tok_rows)], axis=0)
        tinies = [tiny, ring(tiny)]
        cot_x, cot_y = swap(cot_block, 2), swap(cot_block, 4)
        ticks.append((ring(ticks[1][0]), ring(ticks[1][1])))
        first_tables = tables(near)
        zero = ticks[1][0][0, 0].astype(F32) * 0.0
        tables_done = cosine, sine = rope_tables(seq_len, head_dim, zero)
        def keep(j, buffers, shards):
            put = lax.dynamic_update_slice_in_dim
            return (
                put(buffers[0], shards[0], planes[j] * block_rows, 0),
                put(buffers[1], shards[1], planes[j] * shard_width, 0),
            )

        cot_sent = cot_x[:half_rows], cot_y[half_rows:]
        ticks[2], cot_sent, tinies[1] = after(
            (ticks[2], cot_sent, tinies[1]), ticks[2], cot_sent, tinies[1], first_tables, tables_done
        )
        ticks.append((ring(ticks[2][0]), ring(ticks[2][1])))
        tinies.append(ring(tinies[1]))
        diag_a, diag_b = swap(cot_sent[0], 4), swap(cot_sent[1], 2)
        seed = ticks[2][0][:1, :1] * 0
        buffers = (
            jnp.broadcast_to(seed, (ctx_count * piece_rows, model_width)),
            jnp.broadcast_to(seed, (model_width, own_weight.shape[1])),
        )

        for j in range(3):
            buffers = keep(j, buffers, ticks[j])
        cot_pieces = [cot, cot_x, cot_y, diag_a, diag_b]
        cot_diag = jnp.concatenate([diag_a, diag_b], axis=0)
        ticks[3] = after(ticks[3], cot_diag, tinies[2], buffers)
        out_pieces, weight = keep(3, buffers, ticks[3])
        tinies.append(ring(after(tinies[2], weight)))
        cot_next = [ring(after(p, weight)) for p in (cot, cot_x, cot_y, cot_diag)]
        tinies_later = tinies[1:]
        router = jnp.stack([tiny[near_rows:].reshape(experts, shard_width) for tiny in tinies])
        router = router[planes].transpose(1, 0, 2).reshape(experts, model_width)
    else:
        hidden_pieces = plane_gather(normed_low)
        out_pieces = lax.all_gather(out_piece, "wt", axis=0, tiled=True)
        weight = lax.all_gather(own_weight, "wt", axis=0, tiled=True)
        router = lax.all_gather(w_router, "wt", axis=0, tiled=True).T
        cosine, sine = rope_tables(seq_len, head_dim, 0.0)
    out_weight = lax.all_to_all(
        out_pieces.reshape(ctx_count, piece_rows, model_width), "ctx", 0, 0, tiled=True
    ).reshape(head_cols, model_width)

    owner_pair = pair_order[owners]
    blocks = jnp.stack([owner_pair, 2 * ctx_count - 1 - owner_pair], 1).reshape(-1)
    order = jnp.arange(2 * ctx_count, dtype=jnp.int32)
    places = jnp.sum(jnp.where(blocks[:, None] == order[None, :], order[:, None], 0), axis=0)
    places = places.astype(jnp.int32)
    seg = segments[0]
    first = jnp.sum(
        (seg[None, :] < seg[::QUERY_ROWS][:, None]).astype(jnp.int32), axis=1
    ).astype(jnp.int32)
    seg_row, seg_col = seg.reshape(1, seq_len), seg.reshape(seq_len, 1)
    query_gain_row, key_gain_row = query_gain.reshape(1, -1), key_gain.reshape(1, -1)

    width = head_cols + 2 * head_dim
    stacked = heads * QUERY_ROWS
    piece_count = len(hidden_pieces)
    query, key, value, raw, attn_low = pl.pallas_call(
        functools.partial(attend_kernel, heads, piece_count),
        out_shape=(
            jax.ShapeDtypeStruct((seq_len, head_cols), BF),
            jax.ShapeDtypeStruct((seq_len, head_dim), BF),
            jax.ShapeDtypeStruct((seq_len, head_dim), BF),
            jax.ShapeDtypeStruct((seq_len, head_cols + head_dim), F32),
            jax.ShapeDtypeStruct((2 * ctx_count, half_rows, head_cols), BF),
        ),
        in_specs=[SMEM_SPEC] * 3 + [VMEM_SPEC] * (7 + piece_count),
        out_specs=[VMEM_SPEC] * 5,
        scratch_shapes=[pltpu.VMEM((stacked, seq_len), F32)],
        compiler_params=pltpu.CompilerParams(vmem_limit_bytes=ATTEND_LIMIT),
        cost_estimate=COST,
    )(
        blocks,
        places,
        first,
        *hidden_pieces,
        weight,
        query_gain_row,
        key_gain_row,
        cosine,
        sine,
        seg_row,
        seg_col,
    )
    attn_rows = attn_low.reshape(seq_len, head_cols)
    later_tables = []
    out_project = lambda rows, kind: low_matmul(rows, out_weight).astype(kind)
    if dense:
        attn_rows = after(attn_rows, cot_next[0])
        out_project = lambda rows, kind: product(
            [rows], [out_weight], ((1,), (0,)), (rows.shape[0], model_width), kind
        )

        def fill(sends):
            rows = after(tinies_later, sends)
            rows = jnp.concatenate([t[:near_rows] for t in rows], axis=0)
            later_tables.extend(tables(rows))
            return tuple(later_tables) + (cot_next[2],)

        attn = plane_scatter(out_project, attn_rows, fill, (cot_next[1],), (cot_next[3],))
    else:
        attn = plane_scatter(out_project, attn_rows)
    residual = inputs + attn
    normed_two, ffn_back = jax.vjp(rms_norm, residual, ffn_gain)
    normed_two_low = normed_two.astype(BF)
    grad_out = cotangent[0].astype(F32)
    if dense:
        own_slot, target_rows, target_cols, near_routes = (
            jnp.concatenate([f, r], axis=0) for f, r in zip(first_tables[:4], later_tables[:4])
        )
        counts = first_tables[4] + later_tables[4]
        logits = lax.dot_general(normed_two_low, router, nt, preferred_element_type=F32)
        router_probs = jax.nn.softmax(logits, axis=-1)
        shares = counts / (total_tokens * top_count)
        prob_grad = (experts * shares / total_tokens)[None, :]
        logits_grad = router_probs * (
            prob_grad - jnp.sum(router_probs * prob_grad, axis=1, keepdims=True)
        )
        logits_grad_low = logits_grad.astype(BF)
        last = wt_count - 1
        mine_backs, other_backs, results = [], [], []

        def compute(j, pieces, others, gates, second=()):
            pieces = after(pieces, *gates)
            mine, other = select_rows(pieces, others, target_rows[j], slots)
            received = after(swap(other, 1), second)
            result = expert_rows(
                expert.reshape(1),
                mine,
                received,
                own_slot[j],
                near_routes[j],
                w_gate[0],
                w_up[0],
                w_down[0],
                router,
            )
            mine_backs.append(result[0])
            other_backs.append(swap(result[1], 1))
            results.append((mine, received) + tuple(result[2:]))
            return result[0]

        payload, before, done = normed_two_low, None, None
        for j in range(wt_count):
            if j == 2:
                cot_own = cot_next[0]
                halves = payload[:half_rows], cot_own[:half_rows], payload[half_rows:], cot_own[half_rows:]
                payload = jnp.concatenate(halves, axis=0)
            if j > 0:
                payload = ring(payload)
            block = payload if j == 0 else after(payload, before[3:])
            via_x, via_y = swap(block, 2), swap(block, 4)
            if done is not None:
                via_x, via_y = after((via_x, via_y), done)
            middle = via_x.shape[0] // 2
            sent = via_x[:middle], via_y[middle:]
            pieces = [block, via_x, via_y, swap(sent[0], 4), swap(sent[1], 2)]
            if before is not None:
                done = compute(j - 1, before, [cot_pieces, cot_next, []][j - 1], (sent,), pieces[3:])
            before = pieces
        group_sent, blocks = spread_rows(
            mine_backs, other_backs, target_cols[:last], tok_rows, 0, False
        )
        group_sent = after(group_sent, sent)
        group_diag = swap(group_sent[0], 4), swap(group_sent[1], 2)
        done = compute(last, pieces, [], (done,), group_sent)
        step = Order(done)

        def add_chunk(own, part_x, part_y, from_y, from_x):
            part_x, part_y, from_y, from_x = step.take((part_x, part_y, from_y, from_x))
            part_x, part_y = add_diag(part_x, part_y, from_y, from_x)
            step.give(part_x, part_y)
            return own, swap(part_x, 2), swap(part_y, 4)

        def chunk_sum(own, got_x, got_y):
            return [own] + list(step.take((got_x, got_y)))

        def chunk_diag(j):
            return [part[j * half_rows : (j + 1) * half_rows] for part in group_diag]

        partial = {j: add_chunk(*blocks[3 * j : 3 * j + 3], *chunk_diag(j)) for j in range(1, last)}
        tail_sent, tail = spread_rows(
            step.take(mine_backs[last:]), other_backs[last:], target_cols[last:], tok_rows, 0, False
        )
        step.give(tail_sent)
        tail_diag = swap(tail_sent[0], 4), swap(tail_sent[1], 2)
        rows_all = [r for res in results for r in res[:2]]
        hidden_low, gate_low, up_low, routed = ([res[k] for res in results] for k in range(2, 6))
        ff = w_gate.shape[2]
        grad_w_gate = product(step.take(rows_all), gate_low, ((0,), (0,)), (model_width, ff), F32, slots, tile=512, limit=40)
        step.give(grad_w_gate)
        total = sum_of(chunk_sum(*partial[1]), BF)
        step.give(total)
        total = ring(total)
        grad_w_up = product(step.take(rows_all), up_low, ((0,), (0,)), (model_width, ff), F32, slots, tile=512, limit=40)
        step.give(grad_w_up)
        for j in range(2, last):
            total = sum_of([step.take(total)] + chunk_sum(*partial[j]), BF)
            step.give(total)
            total = ring(total)
        partial[last] = add_chunk(*tail, *tail_diag)
        partial[0] = add_chunk(*blocks[:3], *chunk_diag(0))
        grad_w_down = product(
            step.take(hidden_low), routed, ((0,), (0,)), (ff, model_width), F32, tile=256, limit=40
        )
        step.give(grad_w_down)
        total = sum_of([step.take(total)] + chunk_sum(*partial[last]), BF)
        step.give(total)
        total = ring(total)
        out_sent, out_blocks = spread_rows(
            step.take(mine_backs), other_backs, target_cols, tok_rows, 1, True
        )
        step.give(out_sent)
        total = sum_of([step.take(total)] + chunk_sum(*partial[0]), F32)
        grad_normed_two = total + jnp.dot(logits_grad_low, router, preferred_element_type=F32)
        grad_w_gate, grad_w_up, grad_w_down = grad_w_gate[None], grad_w_up[None], grad_w_down[None]
        router_grad = sum(res[6] for res in results) + lax.dot_general(
            logits_grad_low, normed_two_low, tn, preferred_element_type=F32
        )
    else:
        w_router_all = router.T
        slot_rows = 2 * capacity
        local_experts = w_gate.shape[0]
        logits = low_matmul(normed_two_low, w_router_all)
        local_routes = routes[0]

        def router_fn(logit_values):
            router_probs = jax.nn.softmax(logit_values, axis=-1)
            chosen = jnp.take_along_axis(router_probs, local_routes, axis=1)
            return (chosen / jnp.sum(chosen, axis=1, keepdims=True), router_probs)

        (gate_values, router_probs), router_back = jax.vjp(router_fn, logits)
        route_flat = local_routes.reshape(-1)
        route_hits = (route_flat[:, None] == jnp.arange(experts, dtype=jnp.int32)[None, :]).astype(
            jnp.int32
        )
        counts = lax.psum(jnp.sum(route_hits, axis=0).astype(jnp.float32), ("ctx", "wt"))
        shares = counts / (total_tokens * top_count)
        halves = route_hits.reshape(2, half_rows * top_count, experts)
        ranks = jnp.sum((jnp.cumsum(halves, axis=1) - halves) * halves, axis=2).reshape(-1)
        half_index = jnp.arange(tok_rows * top_count, dtype=jnp.int32) // (half_rows * top_count)
        slot_index = route_flat * slot_rows + half_index * capacity + ranks
        slot_owner = (
            jnp.full((experts * slot_rows,), tok_rows * top_count, jnp.int32)
            .at[slot_index]
            .set(jnp.arange(tok_rows * top_count, dtype=jnp.int32))
        )
        slot_shape = (experts // local_experts, local_experts, slot_rows, model_width)
        padded = jnp.concatenate([normed_two_low, jnp.zeros((1, model_width), jnp.bfloat16)], axis=0)
        outgoing = padded[slot_owner // top_count].reshape(slot_shape)
        arrived = move_slots(outgoing)
        gate_pre = jnp.einsum("nesd,edf->nesf", arrived, w_gate, preferred_element_type=jnp.float32)
        up_pre = jnp.einsum("nesd,edf->nesf", arrived, w_up, preferred_element_type=jnp.float32)
        hidden_low, swiglu_back = jax.vjp(swiglu, gate_pre, up_pre)
        hidden_low = hidden_low.astype(jnp.bfloat16)
        expert_out = jnp.einsum(
            "nesf,efd->nesd", hidden_low, w_down, preferred_element_type=jnp.float32
        ).astype(jnp.bfloat16)
        returned = move_slots(expert_out).reshape(experts * slot_rows, model_width)
        picked = returned[slot_index].reshape(tok_rows, top_count, model_width)
        mixture = jnp.einsum("tk,tkd->td", gate_values, picked, preferred_element_type=jnp.float32)
        output = (residual + mixture).astype(jnp.bfloat16)
        grad_gates = jnp.einsum("td,tkd->tk", grad_out, picked, preferred_element_type=jnp.float32)
        grad_routed = (
            (gate_values[:, :, None] * grad_out[:, None, :])
            .astype(jnp.bfloat16)
            .reshape(-1, model_width)
        )
        grad_routed = jnp.concatenate([grad_routed, jnp.zeros((1, model_width), jnp.bfloat16)], axis=0)
        grad_arrived = move_slots(grad_routed[slot_owner].reshape(slot_shape))
        grad_hidden = jnp.einsum(
            "nesd,efd->nesf", grad_arrived, w_down, preferred_element_type=jnp.float32
        )
        grad_w_down = jnp.einsum(
            "nesf,nesd->efd", hidden_low, grad_arrived, preferred_element_type=jnp.float32
        )
        grad_gate_pre, grad_up_pre = swiglu_back(grad_hidden)
        gate_grad_low = grad_gate_pre.astype(jnp.bfloat16)
        up_grad_low = grad_up_pre.astype(jnp.bfloat16)
        grad_w_gate = jnp.einsum(
            "nesd,nesf->edf", arrived, gate_grad_low, preferred_element_type=jnp.float32
        )
        grad_w_up = jnp.einsum(
            "nesd,nesf->edf", arrived, up_grad_low, preferred_element_type=jnp.float32
        )
        grad_slots = (
            jnp.einsum("nesf,edf->nesd", gate_grad_low, w_gate, preferred_element_type=jnp.float32)
            + jnp.einsum("nesf,edf->nesd", up_grad_low, w_up, preferred_element_type=jnp.float32)
        ).astype(jnp.bfloat16)
        grad_back = move_slots(grad_slots).reshape(experts * slot_rows, model_width)
        grad_normed_two = jnp.sum(
            grad_back[slot_index].reshape(tok_rows, top_count, model_width).astype(jnp.float32), axis=1
        )
        prob_grad = jnp.broadcast_to(experts * shares / total_tokens, router_probs.shape)
        (grad_logits,) = router_back((grad_gates, prob_grad))
        logits_low = grad_logits.astype(jnp.bfloat16)
        grad_normed_two = grad_normed_two + jnp.einsum(
            "te,de->td", logits_low, w_router_all, preferred_element_type=jnp.float32
        )
        grad_w_router = jnp.einsum(
            "td,te->de", normed_two_low, logits_low, preferred_element_type=jnp.float32
        )
        router_grad = grad_w_router.T
    grad_residual_part, grad_ffn_gain = ffn_back(grad_normed_two)
    grad_residual = grad_out + grad_residual_part
    grad_pieces = plane_gather(grad_residual.astype(BF))
    if dense:
        out_grad = product(
            [attn_rows], grad_pieces, ((0,), (0,)), (head_cols, model_width), BF
        )
    else:
        out_grad = lax.dot_general(
            attn_rows, jnp.concatenate(grad_pieces, axis=0), tn, preferred_element_type=F32
        ).astype(BF)
    if dense:
        out_sent = after(out_sent, grad_pieces)
        out_diag = swap(out_sent[0], 4), swap(out_sent[1], 2)
        query = after(query, out_sent, out_grad)
    out_grad = lax.all_to_all(
        out_grad.reshape(ctx_count, piece_rows, model_width), "ctx", 0, 0, tiled=True
    )
    head_grads, grad_query_gain, grad_key_gain = pl.pallas_call(
        functools.partial(attend_back_kernel, heads, piece_count),
        out_shape=(
            jax.ShapeDtypeStruct((2 * ctx_count, half_rows, width), BF),
            jax.ShapeDtypeStruct((1, head_dim), F32),
            jax.ShapeDtypeStruct((1, head_dim), F32),
        ),
        in_specs=[SMEM_SPEC] * 2 + [VMEM_SPEC] * (11 + piece_count),
        out_specs=[VMEM_SPEC] * 3,
        scratch_shapes=[
            pltpu.VMEM((stacked, seq_len), F32),
            pltpu.VMEM((stacked, seq_len), F32),
            pltpu.VMEM((seq_len, head_dim), F32),
            pltpu.VMEM((seq_len, head_dim), F32),
            pltpu.VMEM((2 * ctx_count, half_rows, head_cols), BF),
        ],
        compiler_params=pltpu.CompilerParams(vmem_limit_bytes=ATTEND_LIMIT),
        cost_estimate=COST,
    )(
        places,
        first,
        *grad_pieces,
        out_weight,
        query,
        key,
        value,
        raw,
        query_gain_row,
        key_gain_row,
        cosine,
        sine,
        seg_row,
        seg_col,
    )
    head_grads = head_grads.reshape(seq_len, width)
    heads_back = lambda rows, kind: lax.dot_general(
        rows, weight, nt, preferred_element_type=F32
    ).astype(kind)
    if dense:
        step = Order(out_grad)

        def weight_parts(places, kind):
            return product(
                hidden_pieces,
                [step.take(head_grads)],
                ((0,), (0,)),
                (shard_width, width),
                kind,
                starts=places,
            )

        def add_send(got, part, kind=BF):
            total = sum_of([step.take(got), part], kind)
            step.give(total)
            return ring(total)

        (first,) = weight_parts(planes[1:2], BF)
        step.give(first)
        total = ring(first)
        out_x, out_y = add_diag(*step.take((out_blocks[1], out_blocks[2])), *step.take(out_diag))
        step.give(out_x, out_y)
        out_got = swap(out_x, 2), swap(out_y, 4)
        more = weight_parts(planes[jnp.asarray([2, 3, 0])], F32)
        step.give(more)
        total = add_send(total, more[0])
        side = seq_len // 2
        give = product(
            [step.take(head_grads[side:])], [weight], ((1,), (1,)), (side, model_width), BF
        )
        step.give(give)
        got = swap(give, 1)
        keep_part = product(
            [step.take(head_grads[:side])], [weight], ((1,), (1,)), (side, model_width), BF
        )
        step.give(keep_part)
        total = add_send(total, more[1])
        out_parts = step.take(out_grad).reshape(wt_count, block_rows, model_width)
        out_parts = [
            lax.dynamic_index_in_dim(out_parts, planes[j], 0, keepdims=False)
            for j in range(wt_count)
        ]
        step.give(out_parts[1])
        out_total = ring(out_parts[1])
        sums = sum_of([out_blocks[0]] + list(step.take(out_got)), F32)
        step.give(sums)
        sums = sums.reshape(wt_count, tok_rows, model_width)
        kept = sum_of([keep_part, step.take(got)], BF)
        kept_sent = kept[3 * tok_rows : -half_rows], kept[-half_rows:]
        step.give(kept_sent)
        kept_diag = swap(kept_sent[0], 4), swap(kept_sent[1], 2)
        mixed_low = step.take(sums[1]).astype(BF)
        step.give(mixed_low)
        mixed_total = ring(mixed_low)
        weight_grad = sum_of([step.take(total), more[2]], BF)
        step.give(weight_grad)
        weight_x, weight_y = swap(weight_grad, 2), swap(weight_grad, 4)
        half = weight_grad.shape[0] // 2
        weight_x, weight_y = step.take((weight_x, weight_y))
        weight_sent = weight_x[:half], weight_y[half:]
        step.give(weight_sent)
        weight_pieces = [
            weight_grad,
            weight_x,
            weight_y,
            swap(weight_sent[0], 4),
            swap(weight_sent[1], 2),
        ]
        weight_pieces = weight_pieces + [swap(piece, 1) for piece in weight_pieces]
        kept_x, kept_y = add_diag(
            kept[tok_rows : 2 * tok_rows], kept[2 * tok_rows : 3 * tok_rows], *step.take(kept_diag)
        )
        step.give(kept_x, kept_y)
        kept_got = swap(kept_x, 2), swap(kept_y, 4)
        out_total = add_send(out_total, out_parts[2])
        mixed_total = add_send(mixed_total, sums[2])
        kept_got = step.take(kept_got)
        grad_normed_one = sum_of([kept[:tok_rows]] + list(kept_got), F32)
    else:
        hidden_rows = jnp.concatenate(hidden_pieces, axis=0)
        weight_grad = lax.dot_general(hidden_rows, head_grads, tn, preferred_element_type=F32)
        weight_grad = lax.psum_scatter(
            weight_grad.astype(BF), "wt", scatter_dimension=0, tiled=True
        )
        weight_grads = jnp.concatenate(plane_gather(weight_grad), axis=0)
        grad_w_query, grad_w_key, grad_w_value = place_weight_grads(
            weight_grads.reshape(ctx_count, -1, width), owners, share, head_dim
        )
        out_grad = lax.psum_scatter(out_grad, "wt", scatter_dimension=0, tiled=True)
        out_grads = jnp.concatenate(plane_gather(out_grad.reshape(-1, model_width)), axis=0)
        grad_w_output = place_rows(
            out_grads.reshape(ctx_count, own_chunks, piece_rows, model_width), owners
        ).reshape(w_output.shape)
        grad_normed_one = plane_scatter(heads_back, head_grads)
    grad_inputs_part, grad_attn_gain = attn_back(grad_normed_one)
    grad_inputs = grad_residual + grad_inputs_part

    part = head_dim // wt_count
    prob_sums = jnp.sum(router_probs, axis=0)
    prob_row = jnp.zeros((shard_width - 2 * part,), F32)
    if dense:
        prob_row = lax.dynamic_update_slice_in_dim(prob_row, prob_sums, plane * experts, 0)
    gains = jnp.concatenate(
        [
            grad_query_gain.reshape(wt_count, part),
            grad_key_gain.reshape(wt_count, part),
            jnp.broadcast_to(prob_row[None], (wt_count, shard_width - 2 * part)),
        ],
        axis=1,
    )
    small = jnp.concatenate([router_grad, grad_ffn_gain[None], grad_attn_gain[None]], axis=0)
    small = small.reshape(experts + 2, wt_count, shard_width).transpose(1, 0, 2)
    small = jnp.concatenate([small, gains[:, None]], axis=1)[planes]
    if dense:
        out_total = add_send(out_total, out_parts[3])
        mixed_total = add_send(mixed_total, sums[3])
        small_low = step.take(small[1])
        small_total = ring(small_low)
        out_total = sum_of([step.take(out_total), out_parts[0]], BF)
        step.give(out_total)
        out_x, out_y = swap(out_total, 2), swap(out_total, 4)
        small_total = add_send(small_total, small[2], F32)
        grad_w_query, grad_w_key, grad_w_value = place_weight_pieces(
            step.take(weight_pieces), owners, share, head_dim
        )
        step.give(grad_w_value)
        out_x, out_y = step.take((out_x, out_y))
        half = out_total.shape[0] // 2
        out_sent = out_x[:half], out_y[half:]
        step.give(out_sent)
        out_pieces = [out_total, out_x, out_y, swap(out_sent[0], 4), swap(out_sent[1], 2)]
        out_pieces = out_pieces + [swap(piece, 1) for piece in out_pieces]
        small_total = add_send(small_total, small[3], F32)
        output = step.take(mixed_total).astype(F32) + sums[0]
        output = (residual + output).astype(BF)
        step.give(output)
        small = step.take(small_total) + small[0]
        step.give(small)
        grad_w_output = place_row_pieces(step.take(out_pieces), owners, own_chunks)
        grad_w_output = grad_w_output.reshape(w_output.shape)
        small = axis_sum(small, "ctx")
    else:
        small = ring_sum([small[j] for j in range(wt_count)], F32)
        small = axis_sum(small, "ctx")
    if dense:
        prob_sums = small[experts + 2, 2 * part : 2 * part + wt_count * experts]
        prob_sums = jnp.sum(prob_sums.reshape(wt_count, experts), axis=0)
    else:
        prob_sums = axis_sum(axis_sum(prob_sums[None], "ctx"), "wt")[0]
    balance = experts * experts * shares * (prob_sums / total_tokens)
    loss_value = jnp.mean(balance)
    return (
        output[None],
        loss_value,
        balance,
        grad_inputs[None],
        small[experts + 1],
        small[experts],
        small[experts + 2, :part],
        small[experts + 2, part : 2 * part],
        grad_w_query,
        grad_w_key,
        grad_w_value,
        grad_w_output,
        small[:experts].T,
        grad_w_gate,
        grad_w_up,
        grad_w_down,
    )


def solution(mesh):
    in_specs = (
        P("wt", "ctx", None),
        P("wt", "ctx", None),
        P("wt", None),
        P("wt", "ctx", None),
        P(),
        P(),
        P(),
        P(),
        P(),
        P("wt", None),
        P("wt", None),
        P("wt", None),
        P("wt", None),
        P("wt", None),
        P(("ctx", "wt"), None, None),
        P(("ctx", "wt"), None, None),
        P(("ctx", "wt"), None, None),
    )
    out_specs = (
        P("wt", "ctx", None),
        P(),
        P(),
        P("wt", "ctx", None),
        P("wt"),
        P("wt"),
        P("wt"),
        P("wt"),
        P("wt", None),
        P("wt", None),
        P("wt", None),
        P("wt", None),
        P("wt", None),
        P(("ctx", "wt"), None, None),
        P(("ctx", "wt"), None, None),
        P(("ctx", "wt"), None, None),
    )
    return jax.shard_map(local, mesh=mesh, in_specs=in_specs, out_specs=out_specs, check_vma=False)
```
